1024 devices in a mesh: lev: 32 (over z), wave: 32 (over x, y, core).
Axes of the slice: x: 4, y: 4, z: 32, core: 2. Of those that a mesh axis runs over, the one named last changes fastest.
Arguments:
- legendre: float32 [320, 64, 641], P('wave'), may hold values from -0.25 to 0.25
- spectral: float32 [320, 64, 2, 641], P('wave', 'lev'), may hold values from -0.12 to 0.12
- pair_low: int32 [320], replicated, may hold values from 0 to 319, each once
- dep_lat: int32 [1280], P('wave'), may hold values from 0 to 62, as said below
- dep_col: int32 [1280], P('wave'), may hold values from 0 to 1279, as said below
- lon_steps: int32 [1280, 128], P('wave'), may hold values from 0 to 24
- tilt_steps: int32 [1280, 128], P('wave'), may hold values from 0 to 15
Outputs:
- grid_field: float32 [64, 128, 1280], P('lev', 'wave')
- departed: float32 [64, 128, 1280], P('lev', 'wave')
The draws below stay inside these ranges and needn't reach their ends.
Inputs may be any that keep to these rules, and one draw needn't show every extreme that they name: dep_lat lies between the arrival block's own latitude index in its hemisphere minus 2 and that index plus 1, clipped to the band. dep_col is the arrival block's first column plus -3 to 3, modulo 1280.
All inputs are finite; a program needn't handle non-finite values.
Results may differ from the reference program's by a relative error of at most 0.0003.
Values sent between devices are 32-bit elements; how exact they have to be, the bound alone decides.
A program may use at most 32 MiB of HBM per device.

```python
import math
import jax
import jax.numpy as jnp
from jax import lax

M = 640
NLON = 1280
WAVENUMBER_PAIRS = 320
PAIR_SLOTS = 641
PAIRS_DEV = 2
BLK = 128
NORTH_LATITUDES = 64
ROWS = 4
NROWS = 128
LEVEL_FIELDS = 64
BLOCKS_ALL = 1280
N_WAVE = 32


def draw_dep_lat(key, part):
    block_ids = jnp.arange(BLOCKS_ALL, dtype=jnp.int32)
    arrival_rows = block_ids * BLK // NLON
    own_lat = arrival_rows // ROWS * PAIRS_DEV + arrival_rows % PAIRS_DEV
    lat_step = jax.random.randint(jax.random.fold_in(key, 21), (BLOCKS_ALL,), -2, 2)
    return jnp.clip(own_lat + lat_step, 0, NORTH_LATITUDES - 2).astype(jnp.int32)


def draw_dep_col(key, part):
    block_ids = jnp.arange(BLOCKS_ALL, dtype=jnp.int32)
    first_col = block_ids * BLK % NLON
    col_step = jax.random.randint(jax.random.fold_in(key, 31), (BLOCKS_ALL,), -3, 4)
    return ((first_col + col_step) % NLON).astype(jnp.int32)


def touch_ends(entries, stream_key, smallest, largest):
    dims = entries.shape
    index_at = [jax.random.randint(jax.random.fold_in(stream_key, axis), (), 0, dims[axis]) for axis in range(len(dims))]
    entries = entries.at[tuple(index_at)].set(smallest)
    longest = dims.index(max(dims))
    index_at[longest] = (index_at[longest] + 1) % dims[longest]
    return entries.at[tuple(index_at)].set(largest)


def levels(key, dims, cuts, least, top_value):
    def one(dim, parts):
        heights = jax.random.uniform(jax.random.fold_in(jax.random.fold_in(key, 6), dim), (parts,), jnp.float32, least / len(cuts), top_value / len(cuts))
        return jnp.repeat(jnp.exp(heights), dims[dim] // parts).reshape((-1,) + (1,) * (len(dims) - dim - 1))

    loudness = one(*cuts[0])
    for cut in cuts[1:]:
        loudness = loudness * one(*cut)
    return loudness


def normal_values(own_key, dims, deviation, bound, split=(), kind=jnp.bfloat16):
    array = deviation * jax.random.normal(own_key, dims, jnp.float32)
    if split:
        array = array * levels(own_key, dims, split, -0.22, 0.18)
    return jnp.clip(array, -bound, bound).astype(kind)


def setup_inputs(seed: int = 0) -> dict:
    key_of = jax.random.split(jax.random.key(seed), 8)
    return {
        "legendre": normal_values(key_of[0], (WAVENUMBER_PAIRS, NORTH_LATITUDES, PAIR_SLOTS), PAIR_SLOTS ** -0.5, 0.25, ((0, 32),), jnp.float32),
        "spectral": normal_values(key_of[1], (WAVENUMBER_PAIRS, LEVEL_FIELDS, 2, PAIR_SLOTS), 0.02, 0.12, ((0, 32), (1, 32)), jnp.float32),
        "pair_low": jax.random.permutation(key_of[2], WAVENUMBER_PAIRS).astype(jnp.int32),
        "dep_lat": draw_dep_lat(jax.random.fold_in(key_of[7], 71), 0),
        "dep_col": draw_dep_col(jax.random.fold_in(key_of[7], 71), 0),
        "lon_steps": touch_ends(jax.random.randint(key_of[5], (BLOCKS_ALL, BLK), 0, 25), jax.random.fold_in(key_of[5], 1), 0, 24).astype(jnp.int32),
        "tilt_steps": touch_ends(jax.random.randint(key_of[6], (BLOCKS_ALL, BLK), 0, 16), jax.random.fold_in(key_of[6], 1), 0, 15).astype(jnp.int32),
    }


highest = lax.Precision.HIGHEST


def slot_masks(lower_wave, wavenumber_count, slot_count):
    slot_pos = jnp.arange(slot_count, dtype=jnp.int32)[None, :]
    first_len = wavenumber_count - lower_wave[:, None]
    second = slot_pos >= first_len
    offset = jnp.where(second, slot_pos - first_len, slot_pos)
    parity = offset % 2
    member = second.astype(jnp.int32)
    pieces = []
    for member_id in range(2):
        for parity_split in range(2):
            pieces.append(((member == member_id) & (parity == parity_split)).astype(jnp.float32))
    stacked = jnp.stack(pieces, axis=1)
    return stacked.reshape(lower_wave.shape[0], 2, 2, slot_count)


def fourier_rows(matrix, lower_wave, wavenumber_count):
    lon_count = 2 * wavenumber_count
    wave_table = jnp.stack([lower_wave, wavenumber_count - 1 - lower_wave], axis=0)
    gaussian_weights = jnp.where(wave_table == 0, 1.0, 2.0).astype(jnp.float32)
    lon_block = 512 if lon_count % 512 == 0 else 128

    def one_block(first_lon):
        lon_ids = first_lon + jnp.arange(lon_block, dtype=jnp.int32)
        phases = (wave_table[:, :, None] * lon_ids[None, None, :]) % lon_count
        angles = phases.astype(jnp.float32) * (2.0 * math.pi / lon_count)
        dft_table = jnp.stack([gaussian_weights[:, :, None] * jnp.cos(angles), -gaussian_weights[:, :, None] * jnp.sin(angles)], axis=1)
        dft_table = dft_table.reshape(4 * lower_wave.shape[0], lon_block)
        return jnp.dot(matrix, dft_table, precision=highest, preferred_element_type=jnp.float32)

    block_starts = jnp.arange(lon_count // lon_block, dtype=jnp.int32) * lon_block
    blocks = lax.map(one_block, block_starts)
    return jnp.moveaxis(blocks, 0, 1).reshape(matrix.shape[0], lon_count)


def mix_corners(flat_field, row_lo, row_hi, col_lo, col_hi, lon_frac, lat_frac, lon_count):
    def lookup(row_sel, col_sel):
        return jnp.take(flat_field, row_sel * lon_count + col_sel, axis=-1)

    lower_row = (1.0 - lon_frac) * lookup(row_lo, col_lo) + lon_frac * lookup(row_lo, col_hi)
    upper_row = (1.0 - lon_frac) * lookup(row_hi, col_lo) + lon_frac * lookup(row_hi, col_hi)
    return (1.0 - lat_frac) * lower_row + lat_frac * upper_row


def reference(legendre, spectral, pair_low, dep_lat, dep_col, lon_steps, tilt_steps):
    slot_count = M + 1
    slot_mask = slot_masks(pair_low, M, slot_count)

    def per_pair(pair_items):
        coeffs, table_rows, mask_rows = pair_items
        level_count = coeffs.shape[0]
        masked = coeffs[:, :, None, None, :] * mask_rows[None, None, :, :, :]
        masked = masked.reshape(level_count * 8, slot_count)
        halves = jnp.dot(masked, table_rows.T, precision=highest, preferred_element_type=jnp.float32)
        halves = halves.reshape(level_count, 2, 2, 2, table_rows.shape[0])
        northern = halves[:, :, :, 0] + halves[:, :, :, 1]
        southern = halves[:, :, :, 0] - halves[:, :, :, 1]
        return jnp.stack([northern, southern], axis=3)

    results = lax.map(per_pair, (spectral, legendre, slot_mask))
    arranged = results.transpose(1, 4, 5, 3, 2, 0)
    arranged = arranged.reshape(LEVEL_FIELDS, 2, N_WAVE, PAIRS_DEV, 2, 2, WAVENUMBER_PAIRS)
    arranged = arranged.transpose(0, 2, 1, 3, 4, 5, 6).reshape(LEVEL_FIELDS * NROWS, 4 * WAVENUMBER_PAIRS)
    grid_field = fourier_rows(arranged, pair_low, M).reshape(LEVEL_FIELDS, NROWS, NLON)

    block_ids = jnp.arange(BLOCKS_ALL, dtype=jnp.int32)
    arrival_rows = (block_ids * BLK) // NLON
    hemisphere = (arrival_rows % ROWS) // PAIRS_DEV

    def row_of(lat_ids):
        return (lat_ids // PAIRS_DEV) * ROWS + hemisphere * PAIRS_DEV + lat_ids % PAIRS_DEV

    row_lo = row_of(dep_lat)[:, None]
    row_hi = row_of(dep_lat + 1)[:, None]
    quarters = 4 * (dep_col[:, None] + jnp.arange(BLK, dtype=jnp.int32)[None, :]) + lon_steps - 12
    col_lo = (quarters // 4) % NLON
    col_hi = (col_lo + 1) % NLON
    lon_frac = (quarters % 4).astype(jnp.float32) * 0.25
    lat_frac = (tilt_steps % 4).astype(jnp.float32) * 0.25

    def one_level(level_field):
        flat_field = level_field.reshape(NROWS * NLON)
        return mix_corners(flat_field, row_lo, row_hi, col_lo, col_hi, lon_frac, lat_frac, NLON)

    horizontal = lax.map(one_level, grid_field)
    upper_level = jnp.concatenate([horizontal[1:], horizontal[-1:]], axis=0)
    vertical = (tilt_steps // 4).astype(jnp.float32) * 0.25
    departed = (1.0 - vertical) * horizontal + vertical * upper_level
    return grid_field, departed.reshape(LEVEL_FIELDS, NROWS, NLON)
```

```python
import functools
import math

import jax
import jax.numpy as jnp
import numpy as np
from jax import lax
from jax.experimental import pallas as pl
from jax.experimental.pallas import tpu as pltpu
from jax.sharding import PartitionSpec as P

MESH = pl.DeviceIdType.MESH
NT = (((1,), (1,)), ((), ()))
f32 = jnp.float32
bf16 = jnp.bfloat16


def split(x):
    hi = x.astype(bf16)
    lo = (x - hi.astype(f32)).astype(bf16)
    return hi, lo


def legendre_into(send_ref, low_of, leg_ref, spec_ref, wait_pair, y_ref, z_ref, turn):
    pairs, lats, slots = leg_ref.shape
    top = slots - 1
    k = lax.broadcasted_iota(jnp.int32, (8, slots), 1)
    row = lax.broadcasted_iota(jnp.int32, (8, slots), 0)
    hemi, member, part = row // 4, (row // 2) % 2, row % 2
    y_ref[...] = jnp.zeros_like(y_ref)
    send_ref[0] = jnp.zeros(send_ref.shape[1:], f32)
    send_ref[lats // 2 + 1] = jnp.zeros(send_ref.shape[1:], f32)
    for s in range(pairs):
        wait_pair(s)
        first = top - low_of(s)
        keep = (k >= first) == (member == 1)
        odd = (k + member * first) % 2
        mask = jnp.where(keep, 1 - 2 * (hemi * odd), 0).astype(f32)
        rows = []
        for lev in range(2):
            re = jnp.broadcast_to(spec_ref[s, lev, 0:1, :], (8, slots))
            im = jnp.broadcast_to(spec_ref[s, lev, 1:2, :], (8, slots))
            rows.append(jnp.where(part == 0, re, im) * mask)
        hi, lo = split(jnp.concatenate(rows, axis=0))
        leg_hi, leg_lo = split(leg_ref[s])
        both = lax.dot_general(jnp.concatenate([hi, lo], axis=0), leg_hi, NT, preferred_element_type=f32)
        small = lax.dot_general(hi, leg_lo, NT, preferred_element_type=f32)
        y_ref[pl.ds(s, 16, stride=16), :] = both[:16] + (both[16:] + small)
    lane = lax.broadcasted_iota(jnp.int32, (lats // 2, 128), 1)
    for lev in range(2):
        z_ref[...] = y_ref[pl.ds(128 * lev, 128), :].T
        even = z_ref[pl.ds(0, lats // 2, stride=2), :]
        odd = z_ref[pl.ds(1, lats // 2, stride=2), :]
        for h in range(2):
            if h == 0:
                val = jnp.where(lane < 64, even, pltpu.roll(odd, 64, 1))
            else:
                val = jnp.where(lane < 64, pltpu.roll(even, 64, 1), odd)
            val = pltpu.roll(val, 16 * turn, 1)
            for j in range(lats // 2):
                send_ref[1 + j, lev, h : h + 1, :] = val[j : j + 1, :]


def exchange_kernel(
    waves, levs, low_ref, leg_hbm, spec_hbm, recv_ref,
    leg_ref, spec_ref, y_ref, z_ref, send_ref,
    leg_sem, spec_sem, self_sem, send_sem, recv_sem, up_send_sem, up_recv_sem,
):
    me = lax.axis_index("wave")
    lev = lax.axis_index("lev")
    above = lax.rem(lev + 1, levs)
    below = lax.rem(lev + levs - 1, levs)
    pairs = leg_ref.shape[0]
    spec_copy = pltpu.make_async_copy(spec_hbm, spec_ref, spec_sem)
    spec_copy.start()
    leg_copies = [
        pltpu.make_async_copy(leg_hbm.at[s], leg_ref.at[s], leg_sem.at[s]) for s in range(pairs)
    ]
    for copy in leg_copies:
        copy.start()

    barrier = pltpu.get_barrier_semaphore()

    def greet(d, _):
        pl.semaphore_signal(barrier, inc=1, device_id={"lev": lev, "wave": lax.rem(me + d, waves)}, device_id_type=MESH)
        return 0

    def greet_above(w, _):
        pl.semaphore_signal(barrier, inc=1, device_id={"lev": above, "wave": w}, device_id_type=MESH)
        return 0

    lax.fori_loop(1, waves, greet, 0)
    lax.fori_loop(0, waves, greet_above, 0)

    def wait_pair(s):
        if s == 0:
            spec_copy.wait()
        leg_copies[s].wait()

    legendre_into(
        send_ref, lambda s: low_ref[me * pairs + s], leg_ref, spec_ref, wait_pair, y_ref, z_ref,
        lax.rem(me, 8),
    )
    pl.semaphore_wait(barrier, 2 * waves - 1)

    def across(peer, sender):
        return pltpu.make_async_remote_copy(
            src_ref=send_ref.at[pl.ds(peer, 3)],
            dst_ref=recv_ref.at[sender, :, pl.ds(0, 2)],
            send_sem=send_sem.at[peer],
            recv_sem=recv_sem.at[sender],
            device_id={"lev": lev, "wave": peer},
            device_id_type=MESH,
        )

    def down(peer, sender):
        return pltpu.make_async_remote_copy(
            src_ref=send_ref.at[pl.ds(peer, 3), 0],
            dst_ref=recv_ref.at[sender, :, 2],
            send_sem=up_send_sem.at[peer],
            recv_sem=up_recv_sem.at[sender],
            device_id={"lev": below, "wave": peer},
            device_id_type=MESH,
        )

    def start(d, _):
        peer = lax.rem(me + d, waves)
        down(peer, me).start()

        @pl.when(d > 0)
        def _():
            across(peer, me).start()

        return 0

    lax.fori_loop(0, waves, start, 0)
    own = pltpu.make_async_copy(send_ref.at[pl.ds(me, 3)], recv_ref.at[me, :, pl.ds(0, 2)], self_sem)
    own.start()
    own.wait()

    def finish(d, _):
        peer = lax.rem(me + d, waves)
        down(peer, peer).wait_recv()
        down(peer, me).wait_send()

        @pl.when(d > 0)
        def _():
            across(peer, peer).wait_recv()
            across(peer, me).wait_send()

        return 0

    lax.fori_loop(0, waves, finish, 0)


def exchange(pair_low, legendre, spectral, waves, levs):
    pairs, lats, slots = legendre.shape
    any_space = pl.BlockSpec(memory_space=pl.ANY)
    return pl.pallas_call(
        functools.partial(exchange_kernel, waves, levs),
        out_shape=jax.ShapeDtypeStruct((waves, 3, 4, 2, 128), f32),
        in_specs=[pl.BlockSpec(memory_space=pltpu.SMEM), any_space, any_space],
        out_specs=pl.BlockSpec(memory_space=pltpu.VMEM),
        scratch_shapes=[
            pltpu.VMEM((pairs, lats, slots), f32),
            pltpu.VMEM(spectral.shape, f32),
            pltpu.VMEM((256, lats), f32),
            pltpu.VMEM((lats, 128), f32),
            pltpu.VMEM((lats // 2 + 2, 2, 2, 128), f32),
            pltpu.SemaphoreType.DMA((pairs,)),
            pltpu.SemaphoreType.DMA,
            pltpu.SemaphoreType.DMA,
            pltpu.SemaphoreType.DMA((waves,)),
            pltpu.SemaphoreType.DMA((waves,)),
            pltpu.SemaphoreType.DMA((waves,)),
            pltpu.SemaphoreType.DMA((waves,)),
        ],
        compiler_params=pltpu.CompilerParams(collective_id=0, has_side_effects=True),
    )(pair_low, legendre, spectral)


def spread_low(low_ref):
    lane = lax.broadcasted_iota(jnp.int32, (8, 128), 1)
    parts = [jnp.broadcast_to(low_ref[pl.ds(128 * v, 128)].reshape(1, 128), (8, 128)) for v in range(3)]
    out = []
    for v in range(4):
        source = 80 * v + 10 * (lane // 16) + lane % 16
        first = 80 * v // 128
        last = (80 * v + 79) // 128
        got = jnp.take_along_axis(parts[first], source % 128, axis=1)
        if last != first:
            other = jnp.take_along_axis(parts[last], source % 128, axis=1)
            got = jnp.where(source // 128 == first, got, other)
        out.append(jnp.where(lane % 16 < 10, got, -1))
    return out


def order_into(order_ref, low_ref, top):
    low = spread_low(low_ref)
    columns = order_ref.shape[1]
    for e in range(2):
        for n0 in range(0, columns, 16):
            g, q, mu0 = n0 // 128, n0 % 128 // 32, n0 % 32
            p = 4 * g + q
            row = lax.broadcasted_iota(jnp.int32, (8, 128), 0)
            halves = []
            for half in range(2):
                m = p + 10 * (32 * e + mu0 + 8 * half + row)
                want = m if e == 0 else top - 1 - m
                weight = jnp.where(m == 0, 1.0, 2.0) if (e == 0 and p == 0) else jnp.full((8, 128), 2.0, f32)
                halves.append((want, weight))
            for v in range(4):
                if p >= 10:
                    block = jnp.zeros((16, 128), f32)
                else:
                    block = jnp.concatenate(
                        [jnp.where(low[v] == want, weight, 0.0) for want, weight in halves], axis=0
                    )
                order_ref[e, pl.ds(n0, 16), pl.ds(128 * v, 128)] = block.astype(bf16)


def grid_kernel(
    low_ref, lat_ref, col_ref, recv_ref, lon_ref, tilt_ref, table_hi_ref, table_lo_ref, twiddle_ref,
    grid_ref, departed_ref, order_ref, x_ref, field_ref, edge_ref, levs,
):
    wave = lax.axis_index("wave")
    last = lax.axis_index("lev") == levs - 1
    top = 640
    order_into(order_ref, low_ref, top)

    lane = lax.broadcasted_iota(jnp.int32, (8, 128), 1)
    slot = lane // 16
    for grp in range(4):
        for t in range(3):
            arr = [recv_ref[8 * grp + j, t] for j in range(8)]
            for bit in range(3):
                step = 1 << bit
                on = (slot & step) != 0
                arr = [jnp.where(on, arr[(j + step) % 8], arr[j]) for j in range(8)]
            for e in range(2):
                for r in range(2):
                    pieces = []
                    for l in range(2):
                        c = 4 * l + 2 * e + r
                        pieces.append(pltpu.roll(arr[-c % 8], (128 - 16 * c) % 128, 1))
                    hi, lo = split(jnp.concatenate(pieces, axis=0))
                    cols = pl.ds(128 * grp, 128)
                    x_ref[e, pl.ds(48 * r + 16 * t, 16), cols] = hi
                    x_ref[e, pl.ds(96 + 48 * r + 16 * t, 16), cols] = lo

    sums = []
    for e in range(2):
        both = lax.dot_general(x_ref[e], order_ref[e], NT, preferred_element_type=f32)
        sums.append(both[:96] + both[96:])

    slot48 = lax.broadcasted_iota(jnp.int32, (48, 128), 1) // 32
    by_q = [[] for _ in range(4)]
    for g in range(3):
        arr = []
        for i in range(4):
            block = sums[i // 2][48 * (i % 2) : 48 * (i % 2) + 48, 128 * g : 128 * g + 128]
            arr.append(pltpu.roll(block, 32 * i, 1) if i else block)
        for bit in range(2):
            step = 1 << bit
            on = (slot48 & step) != 0
            arr = [jnp.where(on, arr[(j + step) % 4], arr[j]) for j in range(4)]
        for q in range(4):
            if 4 * g + q < 10:
                by_q[q].append(arr[-q % 4])
    re, im = [None] * 10, [None] * 10
    for q in range(4):
        n = 48 * len(by_q[q])
        hi, lo = split(jnp.concatenate(by_q[q], axis=0))
        rows = pl.ds(32 * (-q % 4), 128)
        both = jnp.dot(jnp.concatenate([hi, lo], axis=0), table_hi_ref[rows, :], preferred_element_type=f32)
        small = jnp.dot(hi, table_lo_ref[rows, :], preferred_element_type=f32)
        total = both[:n] + (both[n:] + small)
        for g in range(len(by_q[q])):
            p = 4 * g + q
            a, b = total[48 * g : 48 * g + 48, :128], total[48 * g : 48 * g + 48, 128:]
            if p == 0:
                re[p], im[p] = a, b
            else:
                c = twiddle_ref[2 * p : 2 * p + 1, :]
                s = twiddle_ref[2 * p + 1 : 2 * p + 2, :]
                re[p] = a * c - b * s
                im[p] = a * s + b * c

    def put(x, value):
        field_ref[x] = value

    even = [re[p] + re[10 - p] for p in (1, 2, 3, 4)]
    diff = [im[p] - im[10 - p] for p in (1, 2, 3, 4)]
    for x in range(3):
        co = [math.cos(math.pi * p * x / 5) for p in (1, 2, 3, 4)]
        si = [math.sin(math.pi * p * x / 5) for p in (1, 2, 3, 4)]
        if x == 0:
            a_even = re[0] + (even[1] + even[3])
            a_odd = re[5] + (even[0] + even[2])
            put(0, a_even + a_odd)
            put(5, a_even - a_odd)
            continue
        a_even = re[0] + (co[1] * even[1] + co[3] * even[3])
        a_odd = (co[0] * even[0] + co[2] * even[2]) + (re[5] if x % 2 == 0 else -re[5])
        b_even = si[1] * diff[1] + si[3] * diff[3]
        b_odd = si[0] * diff[0] + si[2] * diff[2]
        a, b = a_even + a_odd, b_even + b_odd
        put(x, a - b)
        put(10 - x, a + b)
        a, b = a_even - a_odd, b_odd - b_even
        put(5 - x, a - b)
        put(5 + x, a + b)

    lane48 = lax.broadcasted_iota(jnp.int32, (48, 128), 1)
    for x in range(10):
        edge_ref[x] = jnp.where(lane48 < 64, field_ref[(x + 1) % 10], field_ref[(x + 9) % 10])
        for l in range(2):
            for row in range(4):
                lev, h = row // 2, row % 2
                grid_ref[lev, pl.ds(2 * h + l, 1), pl.ds(128 * x, 128)] = field_ref[x, pl.ds(8 * (2 + l) + row, 1), :]

    hemi = lax.broadcasted_iota(jnp.int32, (8, 128), 0) % 2 == 1
    keep_own = jnp.logical_and(last, lax.broadcasted_iota(jnp.int32, (8, 128), 0) >= 2)
    for l in range(2):
        for x in range(10):
            north, south = 10 * l + x, 20 + 10 * l + x

            def pick(ref):
                return jnp.where(
                    hemi,
                    jnp.broadcast_to(ref[south : south + 1, :], (8, 128)),
                    jnp.broadcast_to(ref[north : north + 1, :], (8, 128)),
                )

            lon, tilt = pick(lon_ref), pick(tilt_ref)

            def shift_of(block):
                return lax.rem(col_ref[block] - 128 * x + 1280 + 640, 1280) - 640

            base = jnp.where(hemi, shift_of(south), shift_of(north))
            index = lane + base + (lon >> 2) - 3
            nxt = index + 1
            frac = (lon & 3).astype(f32) * 0.25
            g = (tilt & 3).astype(f32) * 0.25
            v = (tilt >> 2).astype(f32) * 0.25
            rows = []
            for off in range(2):
                starts = [
                    pl.multiple_of(8 * (lat_ref[block] - 2 * wave + 2 + off), 8) for block in (north, south)
                ]
                main = jnp.where(hemi, field_ref[x, pl.ds(starts[1], 8), :], field_ref[x, pl.ds(starts[0], 8), :])
                edge = jnp.where(hemi, edge_ref[x, pl.ds(starts[1], 8), :], edge_ref[x, pl.ds(starts[0], 8), :])

                def look(at):
                    inside = (at >> 7) == 0
                    return jnp.where(
                        inside,
                        jnp.take_along_axis(main, at & 127, axis=1),
                        jnp.take_along_axis(edge, at & 127, axis=1),
                    )

                rows.append((1.0 - frac) * look(index) + frac * look(nxt))
            horizontal = (1.0 - g) * rows[0] + g * rows[1]
            upper = jnp.where(keep_own, horizontal, pltpu.roll(horizontal, 6, 0))
            departed = (1.0 - v) * horizontal + v * upper
            for row in range(4):
                lev, h = row // 2, row % 2
                departed_ref[lev, pl.ds(2 * h + l, 1), pl.ds(128 * x, 128)] = departed[row : row + 1, :]


def dft_tables():
    slot = np.arange(224) // 32 % 4
    member, part = slot // 2, slot % 2
    m2 = 32 * member + np.arange(224) % 32
    x = np.arange(128)
    theta = 2 * np.pi * ((m2[:, None] * x[None, :]) % 128) / 128
    c, s = np.cos(theta), np.sin(theta)
    part = part[:, None]
    table = np.concatenate([np.where(part == 0, c, -s), np.where(part == 0, s, c)], axis=1)
    hi = table.astype(jnp.bfloat16)
    lo = (table - hi.astype(np.float64)).astype(jnp.bfloat16)
    angle = 2 * np.pi * np.arange(10)[:, None] * x[None, :] / 1280
    twiddle = np.stack([np.cos(angle), np.sin(angle)], axis=1).reshape(20, 128).astype(np.float32)
    return hi, lo, twiddle


def to_grid(pair_low, dep_lat, dep_col, received, lon_steps, tilt_steps, levs):
    hi, lo, twiddle = dft_tables()
    vmem = pl.BlockSpec(memory_space=pltpu.VMEM)
    smem = pl.BlockSpec(memory_space=pltpu.SMEM)

    def kernel(*refs):
        grid_kernel(*refs, levs)

    low = jnp.pad(pair_low, (0, 64), constant_values=-1)
    return pl.pallas_call(
        kernel,
        out_shape=[jax.ShapeDtypeStruct((2, 4, 1280), f32)] * 2,
        in_specs=[vmem, smem, smem] + [vmem] * 6,
        out_specs=[vmem, vmem],
        scratch_shapes=[
            pltpu.VMEM((2, 384, 512), bf16),
            pltpu.VMEM((2, 192, 512), bf16),
            pltpu.VMEM((10, 48, 128), f32),
            pltpu.VMEM((10, 48, 128), f32),
        ],
        name="grid",
    )(low, dep_lat, dep_col, received, lon_steps, tilt_steps, jnp.asarray(hi), jnp.asarray(lo), jnp.asarray(twiddle))


def per_device(legendre, spectral, pair_low, dep_lat, dep_col, lon_steps, tilt_steps):
    waves, levs = lax.axis_size("wave"), lax.axis_size("lev")
    received = exchange(pair_low, legendre, spectral, waves, levs).reshape(waves, 3, 8, 128)
    return tuple(to_grid(pair_low, dep_lat, dep_col, received, lon_steps, tilt_steps, levs))


def solution(mesh):
    return jax.shard_map(
        per_device,
        mesh=mesh,
        in_specs=(
            P("wave", None, None),
            P("wave", "lev", None, None),
            P(),
            P("wave"),
            P("wave"),
            P("wave", None),
            P("wave", None),
        ),
        out_specs=(P("lev", "wave", None), P("lev", "wave", None)),
        check_vma=False,
    )
```

```python
import functools
import math

import jax
import jax.numpy as jnp
import numpy as np
from jax import lax
from jax.experimental import pallas as pl
from jax.experimental.pallas import tpu as pltpu
from jax.sharding import PartitionSpec as P

MESH = pl.DeviceIdType.MESH
LIMIT = 16 * 1024 * 1024
NT = (((1,), (1,)), ((), ()))
f32 = jnp.float32
bf16 = jnp.bfloat16


def split(x):
    hi = x.astype(bf16)
    lo = (x - hi.astype(f32)).astype(bf16)
    return hi, lo


def legendre_into(send_ref, low_of, leg_ref, spec_ref, wait_pair, y_ref, z_ref, turn):
    pairs, lats, slots = leg_ref.shape
    top = slots - 1
    k = lax.broadcasted_iota(jnp.int32, (8, slots), 1)
    row = lax.broadcasted_iota(jnp.int32, (8, slots), 0)
    hemi, member, part = row // 4, (row // 2) % 2, row % 2
    y_ref[...] = jnp.zeros_like(y_ref)
    send_ref[0] = jnp.zeros(send_ref.shape[1:], f32)
    send_ref[lats // 2 + 1] = jnp.zeros(send_ref.shape[1:], f32)
    for s in range(pairs):
        wait_pair(s)
        first = top - low_of(s)
        keep = (k >= first) == (member == 1)
        odd = (k + member * first) % 2
        mask = jnp.where(keep, 1 - 2 * (hemi * odd), 0).astype(f32)
        rows = []
        for lev in range(2):
            re = jnp.broadcast_to(spec_ref[s, lev, 0:1, :], (8, slots))
            im = jnp.broadcast_to(spec_ref[s, lev, 1:2, :], (8, slots))
            rows.append(jnp.where(part == 0, re, im) * mask)
        hi, lo = split(jnp.concatenate(rows, axis=0))
        leg_hi, leg_lo = split(leg_ref[s])
        both = lax.dot_general(jnp.concatenate([hi, lo], axis=0), leg_hi, NT, preferred_element_type=f32)
        small = lax.dot_general(hi, leg_lo, NT, preferred_element_type=f32)
        y_ref[pl.ds(s, 16, stride=16), :] = both[:16] + (both[16:] + small)
    lane = lax.broadcasted_iota(jnp.int32, (lats // 2, 128), 1)
    for lev in range(2):
        z_ref[...] = y_ref[pl.ds(128 * lev, 128), :].T
        even = z_ref[pl.ds(0, lats // 2, stride=2), :]
        odd = z_ref[pl.ds(1, lats // 2, stride=2), :]
        for h in range(2):
            if h == 0:
                val = jnp.where(lane < 64, even, pltpu.roll(odd, 64, 1))
            else:
                val = jnp.where(lane < 64, pltpu.roll(even, 64, 1), odd)
            val = pltpu.roll(val, 16 * turn, 1)
            for j in range(lats // 2):
                send_ref[1 + j, lev, h : h + 1, :] = val[j : j + 1, :]


def exchange_kernel(
    waves, levs, low_hbm, leg_hbm, spec_hbm, recv_ref, order_ref,
    low_smem, low_vmem, leg_ref, spec_ref, y_ref, z_ref, send_ref,
    low_sem, leg_sem, spec_sem, send_sem, recv_sem, down_send_sem, down_recv_sem,
):
    me = lax.axis_index("wave")
    lev = lax.axis_index("lev")
    pairs, _, slots = leg_ref.shape
    low_copy = pltpu.make_async_copy(low_hbm, low_smem, low_sem.at[0])
    low_copy.start()
    spec_copy = pltpu.make_async_copy(spec_hbm, spec_ref, spec_sem)
    spec_copy.start()
    leg_copies = [
        pltpu.make_async_copy(leg_hbm.at[s], leg_ref.at[s], leg_sem.at[s]) for s in range(pairs)
    ]
    for copy in leg_copies:
        copy.start()
    low_again = pltpu.make_async_copy(low_hbm, low_vmem, low_sem.at[1])
    low_again.start()

    barrier = pltpu.get_barrier_semaphore()

    def greet(d, _):
        pl.semaphore_signal(barrier, inc=1, device_id={"lev": lev, "wave": lax.rem(me + d, waves)}, device_id_type=MESH)
        return 0

    def greet_above(w, _):
        pl.semaphore_signal(barrier, inc=1, device_id={"lev": lev + 1, "wave": w}, device_id_type=MESH)
        return 0

    lax.fori_loop(1, waves, greet, 0)

    @pl.when(lev < levs - 1)
    def _():
        lax.fori_loop(0, waves, greet_above, 0)

    low_copy.wait()

    def wait_pair(s):
        if s == 0:
            spec_copy.wait()
        leg_copies[s].wait()

    legendre_into(
        send_ref, lambda s: low_smem[me * pairs + s], leg_ref, spec_ref, wait_pair, y_ref, z_ref,
        lax.rem(me, 8),
    )
    pl.semaphore_wait(barrier, waves - 1 + jnp.where(lev > 0, waves, 0))

    def across(d, _):
        peer = lax.rem(me + d, waves)
        pltpu.make_async_remote_copy(
            src_ref=send_ref.at[pl.ds(peer, 3)],
            dst_ref=recv_ref.at[me, :, pl.ds(0, 2)],
            send_sem=send_sem,
            recv_sem=recv_sem,
            device_id={"lev": lev, "wave": peer},
            device_id_type=MESH,
        ).start()
        return 0

    def down(d, _):
        peer = lax.rem(me + d, waves)
        pltpu.make_async_remote_copy(
            src_ref=send_ref.at[pl.ds(peer, 3), 0],
            dst_ref=recv_ref.at[me, :, 2],
            send_sem=down_send_sem,
            recv_sem=down_recv_sem,
            device_id={"lev": lev - 1, "wave": peer},
            device_id_type=MESH,
        ).start()
        return 0

    lax.fori_loop(1, waves, across, 0)

    @pl.when(lev > 0)
    def _():
        lax.fori_loop(0, waves, down, 0)

    own = pltpu.make_async_copy(send_ref.at[pl.ds(me, 3)], recv_ref.at[me, :, pl.ds(0, 2)], recv_sem)
    own.start()
    low_again.wait()
    order_into(order_ref, low_vmem, slots - 1)

    all_across = recv_ref.at[:, :, pl.ds(0, 2)]
    sent_across = recv_ref.at[pl.ds(0, waves - 1), :, pl.ds(0, 2)]
    all_down = recv_ref.at[:, :, 2]
    pltpu.make_async_copy(all_across, all_across, recv_sem).wait()

    @pl.when(lev < levs - 1)
    def _():
        pltpu.make_async_copy(all_down, all_down, down_recv_sem).wait()

    pltpu.make_async_copy(sent_across, sent_across, send_sem).wait()

    @pl.when(lev > 0)
    def _():
        pltpu.make_async_copy(all_down, all_down, down_send_sem).wait()


def exchange(pair_low, legendre, spectral, waves, levs):
    pairs, lats, slots = legendre.shape
    any_space = pl.BlockSpec(memory_space=pltpu.HBM)
    vmem = pl.BlockSpec(memory_space=pltpu.VMEM)
    return pl.pallas_call(
        functools.partial(exchange_kernel, waves, levs),
        out_shape=[
            jax.ShapeDtypeStruct((waves, 3, 4, 2, 128), f32),
            jax.ShapeDtypeStruct((2, 384, 512), bf16),
        ],
        in_specs=[any_space] * 3,
        out_specs=[vmem, vmem],
        scratch_shapes=[
            pltpu.SMEM(pair_low.shape, jnp.int32),
            pltpu.VMEM(pair_low.shape, jnp.int32),
            pltpu.VMEM((pairs, lats, slots), f32),
            pltpu.VMEM(spectral.shape, f32),
            pltpu.VMEM((256, lats), f32),
            pltpu.VMEM((lats, 128), f32),
            pltpu.VMEM((lats // 2 + 2, 2, 2, 128), f32),
            pltpu.SemaphoreType.DMA((2,)),
            pltpu.SemaphoreType.DMA((pairs,)),
            pltpu.SemaphoreType.DMA,
            pltpu.SemaphoreType.DMA,
            pltpu.SemaphoreType.DMA,
            pltpu.SemaphoreType.DMA,
            pltpu.SemaphoreType.DMA,
        ],
        compiler_params=pltpu.CompilerParams(
            collective_id=0, has_side_effects=True, vmem_limit_bytes=LIMIT
        ),
    )(*[pltpu.with_memory_space_constraint(a, pltpu.HBM) for a in (pair_low, legendre, spectral)])


def spread_low(low_ref):
    lane = lax.broadcasted_iota(jnp.int32, (8, 128), 1)
    row = low_ref[...].reshape(1, low_ref.shape[0])
    ends = [(0, 128), (128, 256), (192, 320)]
    parts = [jnp.broadcast_to(row[:, a:b], (8, 128)) for a, b in ends]
    out = []
    for v in range(4):
        source = 80 * v + 10 * (lane // 16) + lane % 16
        first = 80 * v // 128
        last = (80 * v + 79) // 128
        shift = [0, 0, 64]
        got = jnp.take_along_axis(parts[first], (source + shift[first]) % 128, axis=1)
        if last != first:
            other = jnp.take_along_axis(parts[last], (source + shift[last]) % 128, axis=1)
            got = jnp.where(source // 128 == first, got, other)
        out.append(jnp.where(lane % 16 < 10, got, -1))
    return out


def order_into(order_ref, low_ref, top):
    low = spread_low(low_ref)
    columns = order_ref.shape[1]
    for e in range(2):
        for n0 in range(0, columns, 16):
            g, q, mu0 = n0 // 128, n0 % 128 // 32, n0 % 32
            p = 4 * g + q
            row = lax.broadcasted_iota(jnp.int32, (8, 128), 0)
            halves = []
            for half in range(2):
                m = p + 10 * (32 * e + mu0 + 8 * half + row)
                want = m if e == 0 else top - 1 - m
                weight = jnp.where(m == 0, 1.0, 2.0) if (e == 0 and p == 0) else jnp.full((8, 128), 2.0, f32)
                halves.append((want, weight))
            for v in range(4):
                if p >= 10:
                    block = jnp.zeros((16, 128), f32)
                else:
                    block = jnp.concatenate(
                        [jnp.where(low[v] == want, weight, 0.0) for want, weight in halves], axis=0
                    )
                order_ref[e, pl.ds(n0, 16), pl.ds(128 * v, 128)] = block.astype(bf16)


def grid_kernel(
    lat_ref, col_ref, recv_ref, order_ref, lon_ref, tilt_ref, table_hi_ref, table_lo_ref, twiddle_ref,
    grid_ref, departed_ref, x_ref, field_ref, edge_ref, lat_smem, col_smem, lat_sem, col_sem, levs,
):
    lat_copy = pltpu.make_async_copy(lat_ref, lat_smem, lat_sem)
    lat_copy.start()
    col_copy = pltpu.make_async_copy(col_ref, col_smem, col_sem)
    col_copy.start()
    wave = lax.axis_index("wave")
    last = lax.axis_index("lev") == levs - 1

    lane = lax.broadcasted_iota(jnp.int32, (8, 128), 1)
    slot = lane // 16
    for grp in range(4):
        for t in range(3):
            arr = [recv_ref[8 * grp + j, t] for j in range(8)]
            for bit in range(3):
                step = 1 << bit
                on = (slot & step) != 0
                arr = [jnp.where(on, arr[(j + step) % 8], arr[j]) for j in range(8)]
            for e in range(2):
                for r in range(2):
                    pieces = []
                    for l in range(2):
                        c = 4 * l + 2 * e + r
                        pieces.append(pltpu.roll(arr[-c % 8], (128 - 16 * c) % 128, 1))
                    hi, lo = split(jnp.concatenate(pieces, axis=0))
                    cols = pl.ds(128 * grp, 128)
                    x_ref[e, pl.ds(48 * r + 16 * t, 16), cols] = hi
                    x_ref[e, pl.ds(96 + 48 * r + 16 * t, 16), cols] = lo

    sums = []
    for e in range(2):
        both = lax.dot_general(x_ref[e], order_ref[e], NT, preferred_element_type=f32)
        sums.append(both[:96] + both[96:])

    slot48 = lax.broadcasted_iota(jnp.int32, (48, 128), 1) // 32
    by_q = [[] for _ in range(4)]
    for g in range(3):
        arr = []
        for i in range(4):
            block = sums[i // 2][48 * (i % 2) : 48 * (i % 2) + 48, 128 * g : 128 * g + 128]
            arr.append(pltpu.roll(block, 32 * i, 1) if i else block)
        for bit in range(2):
            step = 1 << bit
            on = (slot48 & step) != 0
            arr = [jnp.where(on, arr[(j + step) % 4], arr[j]) for j in range(4)]
        for q in range(4):
            if 4 * g + q < 10:
                by_q[q].append(arr[-q % 4])
    re, im = [None] * 10, [None] * 10
    for q in range(4):
        n = 48 * len(by_q[q])
        hi, lo = split(jnp.concatenate(by_q[q], axis=0))
        rows = pl.ds(32 * (-q % 4), 128)
        both = jnp.dot(jnp.concatenate([hi, lo], axis=0), table_hi_ref[rows, :], preferred_element_type=f32)
        small = jnp.dot(hi, table_lo_ref[rows, :], preferred_element_type=f32)
        total = both[:n] + (both[n:] + small)
        for g in range(len(by_q[q])):
            p = 4 * g + q
            a, b = total[48 * g : 48 * g + 48, :128], total[48 * g : 48 * g + 48, 128:]
            if p == 0:
                re[p], im[p] = a, b
            else:
                c = twiddle_ref[2 * p : 2 * p + 1, :]
                s = twiddle_ref[2 * p + 1 : 2 * p + 2, :]
                re[p] = a * c - b * s
                im[p] = a * s + b * c

    def put(x, value):
        field_ref[x] = value

    even = [re[p] + re[10 - p] for p in (1, 2, 3, 4)]
    diff = [im[p] - im[10 - p] for p in (1, 2, 3, 4)]
    for x in range(3):
        co = [math.cos(math.pi * p * x / 5) for p in (1, 2, 3, 4)]
        si = [math.sin(math.pi * p * x / 5) for p in (1, 2, 3, 4)]
        if x == 0:
            a_even = re[0] + (even[1] + even[3])
            a_odd = re[5] + (even[0] + even[2])
            put(0, a_even + a_odd)
            put(5, a_even - a_odd)
            continue
        a_even = re[0] + (co[1] * even[1] + co[3] * even[3])
        a_odd = (co[0] * even[0] + co[2] * even[2]) + (re[5] if x % 2 == 0 else -re[5])
        b_even = si[1] * diff[1] + si[3] * diff[3]
        b_odd = si[0] * diff[0] + si[2] * diff[2]
        a, b = a_even + a_odd, b_even + b_odd
        put(x, a - b)
        put(10 - x, a + b)
        a, b = a_even - a_odd, b_odd - b_even
        put(5 - x, a - b)
        put(5 + x, a + b)

    lane48 = lax.broadcasted_iota(jnp.int32, (48, 128), 1)
    for x in range(10):
        edge_ref[x] = jnp.where(lane48 < 64, field_ref[(x + 1) % 10], field_ref[(x + 9) % 10])
        for l in range(2):
            for row in range(4):
                lev, h = row // 2, row % 2
                grid_ref[lev, pl.ds(2 * h + l, 1), pl.ds(128 * x, 128)] = field_ref[x, pl.ds(8 * (2 + l) + row, 1), :]

    lat_copy.wait()
    col_copy.wait()
    hemi = lax.broadcasted_iota(jnp.int32, (8, 128), 0) % 2 == 1
    keep_own = jnp.logical_and(last, lax.broadcasted_iota(jnp.int32, (8, 128), 0) >= 2)
    for l in range(2):
        for x in range(10):
            north, south = 10 * l + x, 20 + 10 * l + x

            def pick(ref):
                return jnp.where(
                    hemi,
                    jnp.broadcast_to(ref[south : south + 1, :], (8, 128)),
                    jnp.broadcast_to(ref[north : north + 1, :], (8, 128)),
                )

            lon, tilt = pick(lon_ref), pick(tilt_ref)

            def shift_of(block):
                return lax.rem(col_smem[block] - 128 * x + 1280 + 640, 1280) - 640

            base = jnp.where(hemi, shift_of(south), shift_of(north))
            index = lane + base + (lon >> 2) - 3
            nxt = index + 1
            frac = (lon & 3).astype(f32) * 0.25
            g = (tilt & 3).astype(f32) * 0.25
            v = (tilt >> 2).astype(f32) * 0.25
            rows = []
            for off in range(2):
                starts = [
                    pl.multiple_of(8 * (lat_smem[block] - 2 * wave + 2 + off), 8) for block in (north, south)
                ]
                main = jnp.where(hemi, field_ref[x, pl.ds(starts[1], 8), :], field_ref[x, pl.ds(starts[0], 8), :])
                edge = jnp.where(hemi, edge_ref[x, pl.ds(starts[1], 8), :], edge_ref[x, pl.ds(starts[0], 8), :])

                def look(at):
                    inside = (at >> 7) == 0
                    return jnp.where(
                        inside,
                        jnp.take_along_axis(main, at & 127, axis=1),
                        jnp.take_along_axis(edge, at & 127, axis=1),
                    )

                rows.append((1.0 - frac) * look(index) + frac * look(nxt))
            horizontal = (1.0 - g) * rows[0] + g * rows[1]
            upper = jnp.where(keep_own, horizontal, pltpu.roll(horizontal, 6, 0))
            departed = (1.0 - v) * horizontal + v * upper
            for row in range(4):
                lev, h = row // 2, row % 2
                departed_ref[lev, pl.ds(2 * h + l, 1), pl.ds(128 * x, 128)] = departed[row : row + 1, :]


def dft_tables():
    slot = np.arange(224) // 32 % 4
    member, part = slot // 2, slot % 2
    m2 = 32 * member + np.arange(224) % 32
    x = np.arange(128)
    theta = 2 * np.pi * ((m2[:, None] * x[None, :]) % 128) / 128
    c, s = np.cos(theta), np.sin(theta)
    part = part[:, None]
    table = np.concatenate([np.where(part == 0, c, -s), np.where(part == 0, s, c)], axis=1)
    hi = table.astype(jnp.bfloat16)
    lo = (table - hi.astype(np.float64)).astype(jnp.bfloat16)
    angle = 2 * np.pi * np.arange(10)[:, None] * x[None, :] / 1280
    twiddle = np.stack([np.cos(angle), np.sin(angle)], axis=1).reshape(20, 128).astype(np.float32)
    return hi, lo, twiddle


def to_grid(dep_lat, dep_col, received, order, lon_steps, tilt_steps, levs):
    hi, lo, twiddle = dft_tables()
    vmem = pl.BlockSpec(memory_space=pltpu.VMEM)
    outside = pl.BlockSpec(memory_space=pl.ANY)

    def kernel(*refs):
        grid_kernel(*refs, levs)

    return pl.pallas_call(
        kernel,
        out_shape=[jax.ShapeDtypeStruct((2, 4, 1280), f32)] * 2,
        in_specs=[outside, outside] + [vmem] * 7,
        out_specs=[vmem, vmem],
        scratch_shapes=[
            pltpu.VMEM((2, 192, 512), bf16),
            pltpu.VMEM((10, 48, 128), f32),
            pltpu.VMEM((10, 48, 128), f32),
            pltpu.SMEM(dep_lat.shape, jnp.int32),
            pltpu.SMEM(dep_col.shape, jnp.int32),
            pltpu.SemaphoreType.DMA,
            pltpu.SemaphoreType.DMA,
        ],
        compiler_params=pltpu.CompilerParams(vmem_limit_bytes=LIMIT),
        name="grid",
    )(dep_lat, dep_col, received, order, lon_steps, tilt_steps, jnp.asarray(hi), jnp.asarray(lo), jnp.asarray(twiddle))


def per_device(legendre, spectral, pair_low, dep_lat, dep_col, lon_steps, tilt_steps):
    waves, levs = lax.axis_size("wave"), lax.axis_size("lev")
    received, order = exchange(pair_low, legendre, spectral, waves, levs)
    received = received.reshape(waves, 3, 8, 128)
    return tuple(to_grid(dep_lat, dep_col, received, order, lon_steps, tilt_steps, levs))


def solution(mesh):
    return jax.shard_map(
        per_device,
        mesh=mesh,
        in_specs=(
            P("wave", None, None),
            P("wave", "lev", None, None),
            P(),
            P("wave"),
            P("wave"),
            P("wave", None),
            P("wave", None),
        ),
        out_specs=(P("lev", "wave", None), P("lev", "wave", None)),
        check_vma=False,
    )
```

```python
import functools
import math

import jax
import jax.numpy as jnp
import numpy as np
from jax import lax
from jax.experimental import pallas as pl
from jax.experimental.pallas import tpu as pltpu
from jax.sharding import PartitionSpec as P

MESH = pl.DeviceIdType.MESH
LIMIT = 16 * 1024 * 1024
NT = (((1,), (1,)), ((), ()))
f32 = jnp.float32
bf16 = jnp.bfloat16


def split(x):
    hi = x.astype(bf16)
    lo = (x - hi.astype(f32)).astype(bf16)
    return hi, lo


def legendre_into(send_ref, low_of, leg_ref, spec_ref, wait_pair, y_ref, z_ref, turn):
    pairs, lats, slots = leg_ref.shape
    top = slots - 1
    k = lax.broadcasted_iota(jnp.int32, (8, slots), 1)
    row = lax.broadcasted_iota(jnp.int32, (8, slots), 0)
    hemi, member, part = row // 4, (row // 2) % 2, row % 2
    y_ref[...] = jnp.zeros_like(y_ref)
    send_ref[0] = jnp.zeros(send_ref.shape[1:], f32)
    send_ref[lats // 2 + 1] = jnp.zeros(send_ref.shape[1:], f32)
    for s in range(pairs):
        wait_pair(s)
        first = top - low_of(s)
        keep = (k >= first) == (member == 1)
        odd = (k + member * first) % 2
        mask = jnp.where(keep, 1 - 2 * (hemi * odd), 0).astype(f32)
        rows = []
        for lev in range(2):
            re = jnp.broadcast_to(spec_ref[s, lev, 0:1, :], (8, slots))
            im = jnp.broadcast_to(spec_ref[s, lev, 1:2, :], (8, slots))
            rows.append(jnp.where(part == 0, re, im) * mask)
        hi, lo = split(jnp.concatenate(rows, axis=0))
        leg_hi, leg_lo = split(leg_ref[s])
        both = lax.dot_general(jnp.concatenate([hi, lo], axis=0), leg_hi, NT, preferred_element_type=f32)
        small = lax.dot_general(hi, leg_lo, NT, preferred_element_type=f32)
        y_ref[pl.ds(s, 16, stride=16), :] = both[:16] + (both[16:] + small)
    lane = lax.broadcasted_iota(jnp.int32, (lats // 2, 128), 1)
    for lev in range(2):
        z_ref[...] = y_ref[pl.ds(128 * lev, 128), :].T
        even = z_ref[pl.ds(0, lats // 2, stride=2), :]
        odd = z_ref[pl.ds(1, lats // 2, stride=2), :]
        for h in range(2):
            if h == 0:
                val = jnp.where(lane < 64, even, pltpu.roll(odd, 64, 1))
            else:
                val = jnp.where(lane < 64, pltpu.roll(even, 64, 1), odd)
            val = pltpu.roll(val, 16 * turn, 1)
            for j in range(lats // 2):
                send_ref[1 + j, lev, h : h + 1, :] = val[j : j + 1, :]


def exchange_kernel(
    waves, levs, low_hbm, leg_hbm, spec_hbm, recv_ref, order_ref,
    low_smem, low_vmem, leg_ref, spec_ref, y_ref, z_ref, send_ref,
    low_sem, leg_sem, spec_sem, send_sem, recv_sem, down_send_sem, down_recv_sem, ready, ready_down,
):
    me = lax.axis_index("wave")
    lev = lax.axis_index("lev")
    pairs, _, slots = leg_ref.shape
    low_copy = pltpu.make_async_copy(low_hbm, low_smem, low_sem.at[0])
    low_copy.start()
    spec_copy = pltpu.make_async_copy(spec_hbm, spec_ref, spec_sem)
    spec_copy.start()
    leg_copies = [
        pltpu.make_async_copy(leg_hbm.at[s], leg_ref.at[s], leg_sem.at[s]) for s in range(pairs)
    ]
    for copy in leg_copies:
        copy.start()
    low_again = pltpu.make_async_copy(low_hbm, low_vmem, low_sem.at[1])
    low_again.start()

    barrier = pltpu.get_barrier_semaphore()
    late = me == 0
    lower, upper = lev > 0, lev < levs - 1
    peers, all_waves = waves - 1, waves

    def signal(sem, to_lev, to_wave):
        pl.semaphore_signal(sem, inc=1, device_id={"lev": to_lev, "wave": to_wave}, device_id_type=MESH)

    def each(first, body):
        def step(d, _):
            body(d)
            return 0

        lax.fori_loop(first, waves, step, 0)

    @pl.when(jnp.logical_not(late))
    def _():
        each(1, lambda d: signal(barrier, lev, lax.rem(me + d, waves)))

        @pl.when(upper)
        def _():
            each(0, lambda w: signal(barrier, lev + 1, w))

    @pl.when(lower)
    def _():
        signal(barrier, lev - 1, 0)

    @pl.when(late)
    def _():
        pl.semaphore_wait(barrier, peers + jnp.where(lower, peers, 0) + jnp.where(upper, all_waves, 0))
        each(1, lambda d: signal(ready, lev, d))

        @pl.when(upper)
        def _():
            each(0, lambda w: signal(ready_down, lev + 1, w))

    low_copy.wait()

    def wait_pair(s):
        if s == 0:
            spec_copy.wait()
        leg_copies[s].wait()

    legendre_into(
        send_ref, lambda s: low_smem[me * pairs + s], leg_ref, spec_ref, wait_pair, y_ref, z_ref,
        lax.rem(me, 8),
    )

    @pl.when(jnp.logical_not(late))
    def _():
        pl.semaphore_wait(barrier, peers - 1 + jnp.where(lower, peers, 0))

    def across(peer):
        pltpu.make_async_remote_copy(
            src_ref=send_ref.at[pl.ds(peer, 3)],
            dst_ref=recv_ref.at[me, :, pl.ds(0, 2)],
            send_sem=send_sem,
            recv_sem=recv_sem,
            device_id={"lev": lev, "wave": peer},
            device_id_type=MESH,
        ).start()

    def down(peer):
        pltpu.make_async_remote_copy(
            src_ref=send_ref.at[pl.ds(peer, 3), 0],
            dst_ref=recv_ref.at[me, :, 2],
            send_sem=down_send_sem,
            recv_sem=down_recv_sem,
            device_id={"lev": lev - 1, "wave": peer},
            device_id_type=MESH,
        ).start()

    def spread(d):
        peer = lax.rem(me + d, waves)

        @pl.when(peer != 0)
        def _():
            across(peer)

    each(1, spread)

    @pl.when(lower)
    def _():
        each(1, down)

    own = pltpu.make_async_copy(send_ref.at[pl.ds(me, 3)], recv_ref.at[me, :, pl.ds(0, 2)], recv_sem)
    own.start()
    low_again.wait()
    order_into(order_ref, low_vmem, slots - 1)

    @pl.when(jnp.logical_not(late))
    def _():
        pl.semaphore_wait(ready, 1)
        across(0)

    @pl.when(lower)
    def _():
        pl.semaphore_wait(ready_down, 1)
        down(0)

    all_across = recv_ref.at[:, :, pl.ds(0, 2)]
    sent_across = recv_ref.at[pl.ds(0, waves - 1), :, pl.ds(0, 2)]
    all_down = recv_ref.at[:, :, 2]
    pltpu.make_async_copy(all_across, all_across, recv_sem).wait()

    @pl.when(upper)
    def _():
        pltpu.make_async_copy(all_down, all_down, down_recv_sem).wait()

    pltpu.make_async_copy(sent_across, sent_across, send_sem).wait()

    @pl.when(lower)
    def _():
        pltpu.make_async_copy(all_down, all_down, down_send_sem).wait()


def exchange(pair_low, legendre, spectral, waves, levs):
    pairs, lats, slots = legendre.shape
    any_space = pl.BlockSpec(memory_space=pltpu.HBM)
    vmem = pl.BlockSpec(memory_space=pltpu.VMEM)
    return pl.pallas_call(
        functools.partial(exchange_kernel, waves, levs),
        out_shape=[
            jax.ShapeDtypeStruct((waves, 3, 4, 2, 128), f32),
            jax.ShapeDtypeStruct((2, 384, 512), bf16),
        ],
        in_specs=[any_space] * 3,
        out_specs=[vmem, vmem],
        scratch_shapes=[
            pltpu.SMEM(pair_low.shape, jnp.int32),
            pltpu.VMEM(pair_low.shape, jnp.int32),
            pltpu.VMEM((pairs, lats, slots), f32),
            pltpu.VMEM(spectral.shape, f32),
            pltpu.VMEM((256, lats), f32),
            pltpu.VMEM((lats, 128), f32),
            pltpu.VMEM((lats // 2 + 2, 2, 2, 128), f32),
            pltpu.SemaphoreType.DMA((2,)),
            pltpu.SemaphoreType.DMA((pairs,)),
            pltpu.SemaphoreType.DMA,
            pltpu.SemaphoreType.DMA,
            pltpu.SemaphoreType.DMA,
            pltpu.SemaphoreType.DMA,
            pltpu.SemaphoreType.DMA,
            pltpu.SemaphoreType.REGULAR,
            pltpu.SemaphoreType.REGULAR,
        ],
        compiler_params=pltpu.CompilerParams(
            collective_id=0, has_side_effects=True, vmem_limit_bytes=LIMIT
        ),
    )(*[pltpu.with_memory_space_constraint(a, pltpu.HBM) for a in (pair_low, legendre, spectral)])


def spread_low(low_ref):
    lane = lax.broadcasted_iota(jnp.int32, (8, 128), 1)
    row = low_ref[...].reshape(1, low_ref.shape[0])
    ends = [(0, 128), (128, 256), (192, 320)]
    parts = [jnp.broadcast_to(row[:, a:b], (8, 128)) for a, b in ends]
    out = []
    for v in range(4):
        source = 80 * v + 10 * (lane // 16) + lane % 16
        first = 80 * v // 128
        last = (80 * v + 79) // 128
        shift = [0, 0, 64]
        got = jnp.take_along_axis(parts[first], (source + shift[first]) % 128, axis=1)
        if last != first:
            other = jnp.take_along_axis(parts[last], (source + shift[last]) % 128, axis=1)
            got = jnp.where(source // 128 == first, got, other)
        out.append(jnp.where(lane % 16 < 10, got, -1))
    return out


def order_into(order_ref, low_ref, top):
    low = spread_low(low_ref)
    columns = order_ref.shape[1]
    for e in range(2):
        for n0 in range(0, columns, 16):
            g, q, mu0 = n0 // 128, n0 % 128 // 32, n0 % 32
            p = 4 * g + q
            row = lax.broadcasted_iota(jnp.int32, (8, 128), 0)
            halves = []
            for half in range(2):
                m = p + 10 * (32 * e + mu0 + 8 * half + row)
                want = m if e == 0 else top - 1 - m
                weight = jnp.where(m == 0, 1.0, 2.0) if (e == 0 and p == 0) else jnp.full((8, 128), 2.0, f32)
                halves.append((want, weight))
            for v in range(4):
                if p >= 10:
                    block = jnp.zeros((16, 128), f32)
                else:
                    block = jnp.concatenate(
                        [jnp.where(low[v] == want, weight, 0.0) for want, weight in halves], axis=0
                    )
                order_ref[e, pl.ds(n0, 16), pl.ds(128 * v, 128)] = block.astype(bf16)


def grid_kernel(
    lat_ref, col_ref, recv_ref, order_ref, lon_ref, tilt_ref, table_hi_ref, table_lo_ref, twiddle_ref,
    grid_ref, departed_ref, x_ref, field_ref, edge_ref, lat_smem, col_smem, lat_sem, col_sem, levs,
):
    lat_copy = pltpu.make_async_copy(lat_ref, lat_smem, lat_sem)
    lat_copy.start()
    col_copy = pltpu.make_async_copy(col_ref, col_smem, col_sem)
    col_copy.start()
    wave = lax.axis_index("wave")
    last = lax.axis_index("lev") == levs - 1

    lane = lax.broadcasted_iota(jnp.int32, (8, 128), 1)
    slot = lane // 16
    for grp in range(4):
        for t in range(3):
            arr = [recv_ref[8 * grp + j, t] for j in range(8)]
            for bit in range(3):
                step = 1 << bit
                on = (slot & step) != 0
                arr = [jnp.where(on, arr[(j + step) % 8], arr[j]) for j in range(8)]
            for e in range(2):
                for r in range(2):
                    pieces = []
                    for l in range(2):
                        c = 4 * l + 2 * e + r
                        pieces.append(pltpu.roll(arr[-c % 8], (128 - 16 * c) % 128, 1))
                    hi, lo = split(jnp.concatenate(pieces, axis=0))
                    cols = pl.ds(128 * grp, 128)
                    x_ref[e, pl.ds(48 * r + 16 * t, 16), cols] = hi
                    x_ref[e, pl.ds(96 + 48 * r + 16 * t, 16), cols] = lo

    sums = []
    for e in range(2):
        both = lax.dot_general(x_ref[e], order_ref[e], NT, preferred_element_type=f32)
        sums.append(both[:96] + both[96:])

    slot48 = lax.broadcasted_iota(jnp.int32, (48, 128), 1) // 32
    by_q = [[] for _ in range(4)]
    for g in range(3):
        arr = []
        for i in range(4):
            block = sums[i // 2][48 * (i % 2) : 48 * (i % 2) + 48, 128 * g : 128 * g + 128]
            arr.append(pltpu.roll(block, 32 * i, 1) if i else block)
        for bit in range(2):
            step = 1 << bit
            on = (slot48 & step) != 0
            arr = [jnp.where(on, arr[(j + step) % 4], arr[j]) for j in range(4)]
        for q in range(4):
            if 4 * g + q < 10:
                by_q[q].append(arr[-q % 4])
    re, im = [None] * 10, [None] * 10
    for q in range(4):
        n = 48 * len(by_q[q])
        hi, lo = split(jnp.concatenate(by_q[q], axis=0))
        rows = pl.ds(32 * (-q % 4), 128)
        both = jnp.dot(jnp.concatenate([hi, lo], axis=0), table_hi_ref[rows, :], preferred_element_type=f32)
        small = jnp.dot(hi, table_lo_ref[rows, :], preferred_element_type=f32)
        total = both[:n] + (both[n:] + small)
        for g in range(len(by_q[q])):
            p = 4 * g + q
            a, b = total[48 * g : 48 * g + 48, :128], total[48 * g : 48 * g + 48, 128:]
            if p == 0:
                re[p], im[p] = a, b
            else:
                c = twiddle_ref[2 * p : 2 * p + 1, :]
                s = twiddle_ref[2 * p + 1 : 2 * p + 2, :]
                re[p] = a * c - b * s
                im[p] = a * s + b * c

    def put(x, value):
        field_ref[x] = value

    even = [re[p] + re[10 - p] for p in (1, 2, 3, 4)]
    diff = [im[p] - im[10 - p] for p in (1, 2, 3, 4)]
    for x in range(3):
        co = [math.cos(math.pi * p * x / 5) for p in (1, 2, 3, 4)]
        si = [math.sin(math.pi * p * x / 5) for p in (1, 2, 3, 4)]
        if x == 0:
            a_even = re[0] + (even[1] + even[3])
            a_odd = re[5] + (even[0] + even[2])
            put(0, a_even + a_odd)
            put(5, a_even - a_odd)
            continue
        a_even = re[0] + (co[1] * even[1] + co[3] * even[3])
        a_odd = (co[0] * even[0] + co[2] * even[2]) + (re[5] if x % 2 == 0 else -re[5])
        b_even = si[1] * diff[1] + si[3] * diff[3]
        b_odd = si[0] * diff[0] + si[2] * diff[2]
        a, b = a_even + a_odd, b_even + b_odd
        put(x, a - b)
        put(10 - x, a + b)
        a, b = a_even - a_odd, b_odd - b_even
        put(5 - x, a - b)
        put(5 + x, a + b)

    lane48 = lax.broadcasted_iota(jnp.int32, (48, 128), 1)
    for x in range(10):
        edge_ref[x] = jnp.where(lane48 < 64, field_ref[(x + 1) % 10], field_ref[(x + 9) % 10])
        for l in range(2):
            for row in range(4):
                lev, h = row // 2, row % 2
                grid_ref[lev, pl.ds(2 * h + l, 1), pl.ds(128 * x, 128)] = field_ref[x, pl.ds(8 * (2 + l) + row, 1), :]

    lat_copy.wait()
    col_copy.wait()
    hemi = lax.broadcasted_iota(jnp.int32, (8, 128), 0) % 2 == 1
    keep_own = jnp.logical_and(last, lax.broadcasted_iota(jnp.int32, (8, 128), 0) >= 2)
    for l in range(2):
        for x in range(10):
            north, south = 10 * l + x, 20 + 10 * l + x

            def pick(ref):
                return jnp.where(
                    hemi,
                    jnp.broadcast_to(ref[south : south + 1, :], (8, 128)),
                    jnp.broadcast_to(ref[north : north + 1, :], (8, 128)),
                )

            lon, tilt = pick(lon_ref), pick(tilt_ref)

            def shift_of(block):
                return lax.rem(col_smem[block] - 128 * x + 1280 + 640, 1280) - 640

            base = jnp.where(hemi, shift_of(south), shift_of(north))
            index = lane + base + (lon >> 2) - 3
            nxt = index + 1
            frac = (lon & 3).astype(f32) * 0.25
            g = (tilt & 3).astype(f32) * 0.25
            v = (tilt >> 2).astype(f32) * 0.25
            rows = []
            for off in range(2):
                starts = [
                    pl.multiple_of(8 * (lat_smem[block] - 2 * wave + 2 + off), 8) for block in (north, south)
                ]
                main = jnp.where(hemi, field_ref[x, pl.ds(starts[1], 8), :], field_ref[x, pl.ds(starts[0], 8), :])
                edge = jnp.where(hemi, edge_ref[x, pl.ds(starts[1], 8), :], edge_ref[x, pl.ds(starts[0], 8), :])

                def look(at):
                    inside = (at >> 7) == 0
                    return jnp.where(
                        inside,
                        jnp.take_along_axis(main, at & 127, axis=1),
                        jnp.take_along_axis(edge, at & 127, axis=1),
                    )

                rows.append((1.0 - frac) * look(index) + frac * look(nxt))
            horizontal = (1.0 - g) * rows[0] + g * rows[1]
            upper = jnp.where(keep_own, horizontal, pltpu.roll(horizontal, 6, 0))
            departed = (1.0 - v) * horizontal + v * upper
            for row in range(4):
                lev, h = row // 2, row % 2
                departed_ref[lev, pl.ds(2 * h + l, 1), pl.ds(128 * x, 128)] = departed[row : row + 1, :]


def dft_tables():
    slot = np.arange(224) // 32 % 4
    member, part = slot // 2, slot % 2
    m2 = 32 * member + np.arange(224) % 32
    x = np.arange(128)
    theta = 2 * np.pi * ((m2[:, None] * x[None, :]) % 128) / 128
    c, s = np.cos(theta), np.sin(theta)
    part = part[:, None]
    table = np.concatenate([np.where(part == 0, c, -s), np.where(part == 0, s, c)], axis=1)
    hi = table.astype(jnp.bfloat16)
    lo = (table - hi.astype(np.float64)).astype(jnp.bfloat16)
    angle = 2 * np.pi * np.arange(10)[:, None] * x[None, :] / 1280
    twiddle = np.stack([np.cos(angle), np.sin(angle)], axis=1).reshape(20, 128).astype(np.float32)
    return hi, lo, twiddle


def to_grid(dep_lat, dep_col, received, order, lon_steps, tilt_steps, levs):
    hi, lo, twiddle = dft_tables()
    vmem = pl.BlockSpec(memory_space=pltpu.VMEM)
    outside = pl.BlockSpec(memory_space=pl.ANY)

    def kernel(*refs):
        grid_kernel(*refs, levs)

    return pl.pallas_call(
        kernel,
        out_shape=[jax.ShapeDtypeStruct((2, 4, 1280), f32)] * 2,
        in_specs=[outside, outside] + [vmem] * 7,
        out_specs=[vmem, vmem],
        scratch_shapes=[
            pltpu.VMEM((2, 192, 512), bf16),
            pltpu.VMEM((10, 48, 128), f32),
            pltpu.VMEM((10, 48, 128), f32),
            pltpu.SMEM(dep_lat.shape, jnp.int32),
            pltpu.SMEM(dep_col.shape, jnp.int32),
            pltpu.SemaphoreType.DMA,
            pltpu.SemaphoreType.DMA,
        ],
        compiler_params=pltpu.CompilerParams(vmem_limit_bytes=LIMIT),
        name="grid",
    )(dep_lat, dep_col, received, order, lon_steps, tilt_steps, jnp.asarray(hi), jnp.asarray(lo), jnp.asarray(twiddle))


def per_device(legendre, spectral, pair_low, dep_lat, dep_col, lon_steps, tilt_steps):
    waves, levs = lax.axis_size("wave"), lax.axis_size("lev")
    received, order = exchange(pair_low, legendre, spectral, waves, levs)
    received = received.reshape(waves, 3, 8, 128)
    return tuple(to_grid(dep_lat, dep_col, received, order, lon_steps, tilt_steps, levs))


def solution(mesh):
    return jax.shard_map(
        per_device,
        mesh=mesh,
        in_specs=(
            P("wave", None, None),
            P("wave", "lev", None, None),
            P(),
            P("wave"),
            P("wave"),
            P("wave", None),
            P("wave", None),
        ),
        out_specs=(P("lev", "wave", None), P("lev", "wave", None)),
        check_vma=False,
    )
```

```python
import functools
import math

import jax
import jax.numpy as jnp
import numpy as np
from jax import lax
from jax.experimental import pallas as pl
from jax.experimental.pallas import tpu as pltpu
from jax.sharding import PartitionSpec as P

MESH = pl.DeviceIdType.MESH
LIMIT = 16 * 1024 * 1024
NT = (((1,), (1,)), ((), ()))
f32 = jnp.float32
bf16 = jnp.bfloat16


def split(x):
    hi = x.astype(bf16)
    lo = (x - hi.astype(f32)).astype(bf16)
    return hi, lo


def legendre_into(send_ref, low_of, leg_ref, spec_ref, wait_pair, y_ref, z_ref, turn):
    pairs, lats, slots = leg_ref.shape
    top = slots - 1
    k = lax.broadcasted_iota(jnp.int32, (8, slots), 1)
    row = lax.broadcasted_iota(jnp.int32, (8, slots), 0)
    hemi, member, part = row // 4, (row // 2) % 2, row % 2
    y_ref[...] = jnp.zeros_like(y_ref)
    send_ref[0] = jnp.zeros(send_ref.shape[1:], f32)
    send_ref[lats // 2 + 1] = jnp.zeros(send_ref.shape[1:], f32)
    for s in range(pairs):
        wait_pair(s)
        first = top - low_of(s)
        keep = (k >= first) == (member == 1)
        odd = (k + member * first) % 2
        mask = jnp.where(keep, 1 - 2 * (hemi * odd), 0).astype(f32)
        rows = []
        for lev in range(2):
            re = jnp.broadcast_to(spec_ref[s, lev, 0:1, :], (8, slots))
            im = jnp.broadcast_to(spec_ref[s, lev, 1:2, :], (8, slots))
            rows.append(jnp.where(part == 0, re, im) * mask)
        hi, lo = split(jnp.concatenate(rows, axis=0))
        leg_hi, leg_lo = split(leg_ref[s])
        both = lax.dot_general(jnp.concatenate([hi, lo], axis=0), leg_hi, NT, preferred_element_type=f32)
        small = lax.dot_general(hi, leg_lo, NT, preferred_element_type=f32)
        y_ref[pl.ds(s, 16, stride=16), :] = both[:16] + (both[16:] + small)
    lane = lax.broadcasted_iota(jnp.int32, (lats // 2, 128), 1)
    for lev in range(2):
        z_ref[...] = y_ref[pl.ds(128 * lev, 128), :].T
        even = z_ref[pl.ds(0, lats // 2, stride=2), :]
        odd = z_ref[pl.ds(1, lats // 2, stride=2), :]
        for h in range(2):
            if h == 0:
                val = jnp.where(lane < 64, even, pltpu.roll(odd, 64, 1))
            else:
                val = jnp.where(lane < 64, pltpu.roll(even, 64, 1), odd)
            val = pltpu.roll(val, 16 * turn, 1)
            for j in range(lats // 2):
                send_ref[1 + j, lev, h : h + 1, :] = val[j : j + 1, :]


def exchange_kernel(
    waves, levs, low_hbm, leg_hbm, spec_hbm, recv_ref, order_ref,
    low_smem, low_vmem, leg_ref, spec_ref, y_ref, z_ref, send_ref,
    low_sem, leg_sem, spec_sem, send_sem, recv_sem, down_send_sem, down_recv_sem,
    proxy_ref, proxy_sem, proxy_down_sem, relay_sem, relay_down_sem, ready,
):
    me = lax.axis_index("wave")
    lev = lax.axis_index("lev")
    pairs, _, slots = leg_ref.shape
    low_copy = pltpu.make_async_copy(low_hbm, low_smem, low_sem.at[0])
    low_copy.start()
    spec_copy = pltpu.make_async_copy(spec_hbm, spec_ref, spec_sem)
    spec_copy.start()
    leg_copies = [
        pltpu.make_async_copy(leg_hbm.at[s], leg_ref.at[s], leg_sem.at[s]) for s in range(pairs)
    ]
    for copy in leg_copies:
        copy.start()
    low_again = pltpu.make_async_copy(low_hbm, low_vmem, low_sem.at[1])
    low_again.start()

    barrier = pltpu.get_barrier_semaphore()
    late = me == 0
    lower, upper = lev > 0, lev < levs - 1
    peers = waves - 1

    def signal(sem, to_lev, to_wave):
        pl.semaphore_signal(sem, inc=1, device_id={"lev": to_lev, "wave": to_wave}, device_id_type=MESH)

    def each(first, body):
        def step(d, _):
            body(d)
            return 0

        lax.fori_loop(first, waves, step, 0)

    @pl.when(jnp.logical_not(late))
    def _():
        each(1, lambda d: signal(barrier, lev, lax.rem(me + d, waves)))

        @pl.when(upper)
        def _():
            each(0, lambda w: signal(barrier, lev + 1, w))

    @pl.when(late)
    def _():
        pl.semaphore_wait(barrier, peers + jnp.where(lower, peers, 0))
        signal(ready, lev, 1)

    low_copy.wait()

    def wait_pair(s):
        if s == 0:
            spec_copy.wait()
            for copy in leg_copies:
                copy.wait()

    legendre_into(
        send_ref, lambda s: low_smem[me * pairs + s], leg_ref, spec_ref, wait_pair, y_ref, z_ref,
        lax.rem(me, 8),
    )

    @pl.when(jnp.logical_not(late))
    def _():
        pl.semaphore_wait(barrier, peers - 1 + jnp.where(lower, peers, 0))

    def across(peer, slots_of, to_wave, sem):
        pltpu.make_async_remote_copy(
            src_ref=send_ref.at[pl.ds(peer, 3)],
            dst_ref=slots_of.at[me, :, pl.ds(0, 2)],
            send_sem=send_sem,
            recv_sem=sem,
            device_id={"lev": lev, "wave": to_wave},
            device_id_type=MESH,
        ).start()

    def down(peer, slots_of, to_wave, sem):
        pltpu.make_async_remote_copy(
            src_ref=send_ref.at[pl.ds(peer, 3), 0],
            dst_ref=slots_of.at[me, :, 2],
            send_sem=down_send_sem,
            recv_sem=sem,
            device_id={"lev": lev - 1, "wave": to_wave},
            device_id_type=MESH,
        ).start()

    def spread(d):
        peer = lax.rem(me + waves // 2 + d, waves)

        @pl.when(jnp.logical_and(peer != 0, peer != me))
        def _():
            across(peer, recv_ref, peer, recv_sem)

    each(0, spread)

    @pl.when(me > 1)
    def _():
        across(0, proxy_ref, 1, proxy_sem)

    @pl.when(lower)
    def _():
        each(1, lambda w: down(w, recv_ref, w, down_recv_sem))
        down(0, proxy_ref, 1, proxy_down_sem)

    pltpu.make_async_copy(send_ref.at[pl.ds(me, 3)], recv_ref.at[me, :, pl.ds(0, 2)], recv_sem).start()
    low_again.wait()
    order_into(order_ref, low_vmem, slots - 1)

    def wait_for(part, sem):
        pltpu.make_async_copy(part, part, sem).wait()

    def relay(part_of, sem, to_sem):
        return pltpu.make_async_remote_copy(
            src_ref=part_of(proxy_ref),
            dst_ref=part_of(recv_ref),
            send_sem=sem,
            recv_sem=to_sem,
            device_id={"lev": lev, "wave": 0},
            device_id_type=MESH,
        )

    def others(ref):
        return ref.at[pl.ds(1, waves - 1), :, pl.ds(0, 2)]

    def downs(ref):
        return ref.at[:, :, 2]

    @pl.when(me == 1)
    def _():
        pltpu.make_async_copy(send_ref.at[pl.ds(0, 3)], proxy_ref.at[me, :, pl.ds(0, 2)], proxy_sem).start()
        wait_for(others(proxy_ref), proxy_sem)

        @pl.when(upper)
        def _():
            wait_for(downs(proxy_ref), proxy_down_sem)

        pl.semaphore_wait(ready, 1)
        relay(others, relay_sem, recv_sem).start()

        @pl.when(upper)
        def _():
            relay(downs, relay_down_sem, down_recv_sem).start()

    wait_for(recv_ref.at[:, :, pl.ds(0, 2)], recv_sem)

    @pl.when(upper)
    def _():
        wait_for(downs(recv_ref), down_recv_sem)

    @pl.when(me == 1)
    def _():
        wait_for(others(proxy_ref), relay_sem)
        wait_for(recv_ref.at[pl.ds(0, waves - 2), :, pl.ds(0, 2)], send_sem)

        @pl.when(upper)
        def _():
            wait_for(downs(proxy_ref), relay_down_sem)

    @pl.when(me != 1)
    def _():
        wait_for(others(recv_ref), send_sem)

    @pl.when(lower)
    def _():
        wait_for(downs(recv_ref), down_send_sem)


def exchange(pair_low, legendre, spectral, waves, levs):
    pairs, lats, slots = legendre.shape
    any_space = pl.BlockSpec(memory_space=pltpu.HBM)
    vmem = pl.BlockSpec(memory_space=pltpu.VMEM)
    return pl.pallas_call(
        functools.partial(exchange_kernel, waves, levs),
        out_shape=[
            jax.ShapeDtypeStruct((waves, 3, 4, 2, 128), f32),
            jax.ShapeDtypeStruct((2, 384, 512), bf16),
        ],
        in_specs=[any_space] * 3,
        out_specs=[vmem, vmem],
        scratch_shapes=[
            pltpu.SMEM(pair_low.shape, jnp.int32),
            pltpu.VMEM(pair_low.shape, jnp.int32),
            pltpu.VMEM((pairs, lats, slots), f32),
            pltpu.VMEM(spectral.shape, f32),
            pltpu.VMEM((256, lats), f32),
            pltpu.VMEM((lats, 128), f32),
            pltpu.VMEM((lats // 2 + 2, 2, 2, 128), f32),
            pltpu.SemaphoreType.DMA((2,)),
            pltpu.SemaphoreType.DMA((pairs,)),
            pltpu.SemaphoreType.DMA,
            pltpu.SemaphoreType.DMA,
            pltpu.SemaphoreType.DMA,
            pltpu.SemaphoreType.DMA,
            pltpu.SemaphoreType.DMA,
            pltpu.VMEM((waves, 3, 4, 2, 128), f32),
            pltpu.SemaphoreType.DMA,
            pltpu.SemaphoreType.DMA,
            pltpu.SemaphoreType.DMA,
            pltpu.SemaphoreType.DMA,
            pltpu.SemaphoreType.REGULAR,
        ],
        compiler_params=pltpu.CompilerParams(
            collective_id=0, has_side_effects=True, vmem_limit_bytes=LIMIT
        ),
    )(*[pltpu.with_memory_space_constraint(a, pltpu.HBM) for a in (pair_low, legendre, spectral)])


def spread_low(low_ref):
    lane = lax.broadcasted_iota(jnp.int32, (8, 128), 1)
    row = low_ref[...].reshape(1, low_ref.shape[0])
    ends = [(0, 128), (128, 256), (192, 320)]
    parts = [jnp.broadcast_to(row[:, a:b], (8, 128)) for a, b in ends]
    out = []
    for v in range(4):
        source = 80 * v + 10 * (lane // 16) + lane % 16
        first = 80 * v // 128
        last = (80 * v + 79) // 128
        shift = [0, 0, 64]
        got = jnp.take_along_axis(parts[first], (source + shift[first]) % 128, axis=1)
        if last != first:
            other = jnp.take_along_axis(parts[last], (source + shift[last]) % 128, axis=1)
            got = jnp.where(source // 128 == first, got, other)
        out.append(jnp.where(lane % 16 < 10, got, -1))
    return out


def order_into(order_ref, low_ref, top):
    low = spread_low(low_ref)
    columns = order_ref.shape[1]
    for e in range(2):
        for n0 in range(0, columns, 16):
            g, q, mu0 = n0 // 128, n0 % 128 // 32, n0 % 32
            p = 4 * g + q
            row = lax.broadcasted_iota(jnp.int32, (8, 128), 0)
            halves = []
            for half in range(2):
                m = p + 10 * (32 * e + mu0 + 8 * half + row)
                want = m if e == 0 else top - 1 - m
                weight = jnp.where(m == 0, 1.0, 2.0) if (e == 0 and p == 0) else jnp.full((8, 128), 2.0, f32)
                halves.append((want, weight))
            for v in range(4):
                if p >= 10:
                    block = jnp.zeros((16, 128), f32)
                else:
                    block = jnp.concatenate(
                        [jnp.where(low[v] == want, weight, 0.0) for want, weight in halves], axis=0
                    )
                order_ref[e, pl.ds(n0, 16), pl.ds(128 * v, 128)] = block.astype(bf16)


def grid_kernel(
    lat_ref, col_ref, recv_ref, order_ref, lon_ref, tilt_ref, table_hi_ref, table_lo_ref, twiddle_ref,
    grid_ref, departed_ref, x_ref, field_ref, edge_ref, lat_smem, col_smem, lat_sem, col_sem, levs,
):
    lat_copy = pltpu.make_async_copy(lat_ref, lat_smem, lat_sem)
    lat_copy.start()
    col_copy = pltpu.make_async_copy(col_ref, col_smem, col_sem)
    col_copy.start()
    wave = lax.axis_index("wave")
    last = lax.axis_index("lev") == levs - 1

    lane = lax.broadcasted_iota(jnp.int32, (8, 128), 1)
    slot = lane // 16
    for grp in range(4):
        for t in range(3):
            arr = [recv_ref[8 * grp + j, t] for j in range(8)]
            for bit in range(3):
                step = 1 << bit
                on = (slot & step) != 0
                arr = [jnp.where(on, arr[(j + step) % 8], arr[j]) for j in range(8)]
            for e in range(2):
                for r in range(2):
                    pieces = []
                    for l in range(2):
                        c = 4 * l + 2 * e + r
                        pieces.append(pltpu.roll(arr[-c % 8], (128 - 16 * c) % 128, 1))
                    hi, lo = split(jnp.concatenate(pieces, axis=0))
                    cols = pl.ds(128 * grp, 128)
                    x_ref[e, pl.ds(48 * r + 16 * t, 16), cols] = hi
                    x_ref[e, pl.ds(96 + 48 * r + 16 * t, 16), cols] = lo

    sums = []
    for e in range(2):
        both = lax.dot_general(x_ref[e], order_ref[e], NT, preferred_element_type=f32)
        sums.append(both[:96] + both[96:])

    slot48 = lax.broadcasted_iota(jnp.int32, (48, 128), 1) // 32
    by_q = [[] for _ in range(4)]
    for g in range(3):
        arr = []
        for i in range(4):
            block = sums[i // 2][48 * (i % 2) : 48 * (i % 2) + 48, 128 * g : 128 * g + 128]
            arr.append(pltpu.roll(block, 32 * i, 1) if i else block)
        for bit in range(2):
            step = 1 << bit
            on = (slot48 & step) != 0
            arr = [jnp.where(on, arr[(j + step) % 4], arr[j]) for j in range(4)]
        for q in range(4):
            if 4 * g + q < 10:
                by_q[q].append(arr[-q % 4])
    re, im = [None] * 10, [None] * 10
    for q in range(4):
        n = 48 * len(by_q[q])
        hi, lo = split(jnp.concatenate(by_q[q], axis=0))
        rows = pl.ds(32 * (-q % 4), 128)
        both = jnp.dot(jnp.concatenate([hi, lo], axis=0), table_hi_ref[rows, :], preferred_element_type=f32)
        small = jnp.dot(hi, table_lo_ref[rows, :], preferred_element_type=f32)
        total = both[:n] + (both[n:] + small)
        for g in range(len(by_q[q])):
            p = 4 * g + q
            a, b = total[48 * g : 48 * g + 48, :128], total[48 * g : 48 * g + 48, 128:]
            if p == 0:
                re[p], im[p] = a, b
            else:
                c = twiddle_ref[2 * p : 2 * p + 1, :]
                s = twiddle_ref[2 * p + 1 : 2 * p + 2, :]
                re[p] = a * c - b * s
                im[p] = a * s + b * c

    def put(x, value):
        field_ref[x] = value

    even = [re[p] + re[10 - p] for p in (1, 2, 3, 4)]
    diff = [im[p] - im[10 - p] for p in (1, 2, 3, 4)]
    for x in range(3):
        co = [math.cos(math.pi * p * x / 5) for p in (1, 2, 3, 4)]
        si = [math.sin(math.pi * p * x / 5) for p in (1, 2, 3, 4)]
        if x == 0:
            a_even = re[0] + (even[1] + even[3])
            a_odd = re[5] + (even[0] + even[2])
            put(0, a_even + a_odd)
            put(5, a_even - a_odd)
            continue
        a_even = re[0] + (co[1] * even[1] + co[3] * even[3])
        a_odd = (co[0] * even[0] + co[2] * even[2]) + (re[5] if x % 2 == 0 else -re[5])
        b_even = si[1] * diff[1] + si[3] * diff[3]
        b_odd = si[0] * diff[0] + si[2] * diff[2]
        a, b = a_even + a_odd, b_even + b_odd
        put(x, a - b)
        put(10 - x, a + b)
        a, b = a_even - a_odd, b_odd - b_even
        put(5 - x, a - b)
        put(5 + x, a + b)

    lane48 = lax.broadcasted_iota(jnp.int32, (48, 128), 1)
    for x in range(10):
        edge_ref[x] = jnp.where(lane48 < 64, field_ref[(x + 1) % 10], field_ref[(x + 9) % 10])
        for l in range(2):
            for row in range(4):
                lev, h = row // 2, row % 2
                grid_ref[lev, pl.ds(2 * h + l, 1), pl.ds(128 * x, 128)] = field_ref[x, pl.ds(8 * (2 + l) + row, 1), :]

    lat_copy.wait()
    col_copy.wait()
    hemi = lax.broadcasted_iota(jnp.int32, (8, 128), 0) % 2 == 1
    keep_own = jnp.logical_and(last, lax.broadcasted_iota(jnp.int32, (8, 128), 0) >= 2)
    for l in range(2):
        for x in range(10):
            north, south = 10 * l + x, 20 + 10 * l + x

            def pick(ref):
                return jnp.where(
                    hemi,
                    jnp.broadcast_to(ref[south : south + 1, :], (8, 128)),
                    jnp.broadcast_to(ref[north : north + 1, :], (8, 128)),
                )

            lon, tilt = pick(lon_ref), pick(tilt_ref)

            def shift_of(block):
                return lax.rem(col_smem[block] - 128 * x + 1280 + 640, 1280) - 640

            base = jnp.where(hemi, shift_of(south), shift_of(north))
            index = lane + base + (lon >> 2) - 3
            nxt = index + 1
            frac = (lon & 3).astype(f32) * 0.25
            g = (tilt & 3).astype(f32) * 0.25
            v = (tilt >> 2).astype(f32) * 0.25
            rows = []
            for off in range(2):
                starts = [
                    pl.multiple_of(8 * (lat_smem[block] - 2 * wave + 2 + off), 8) for block in (north, south)
                ]
                main = jnp.where(hemi, field_ref[x, pl.ds(starts[1], 8), :], field_ref[x, pl.ds(starts[0], 8), :])
                edge = jnp.where(hemi, edge_ref[x, pl.ds(starts[1], 8), :], edge_ref[x, pl.ds(starts[0], 8), :])

                def look(at):
                    inside = (at >> 7) == 0
                    return jnp.where(
                        inside,
                        jnp.take_along_axis(main, at & 127, axis=1),
                        jnp.take_along_axis(edge, at & 127, axis=1),
                    )

                rows.append((1.0 - frac) * look(index) + frac * look(nxt))
            horizontal = (1.0 - g) * rows[0] + g * rows[1]
            upper = jnp.where(keep_own, horizontal, pltpu.roll(horizontal, 6, 0))
            departed = (1.0 - v) * horizontal + v * upper
            for row in range(4):
                lev, h = row // 2, row % 2
                departed_ref[lev, pl.ds(2 * h + l, 1), pl.ds(128 * x, 128)] = departed[row : row + 1, :]


def dft_tables():
    slot = np.arange(224) // 32 % 4
    member, part = slot // 2, slot % 2
    m2 = 32 * member + np.arange(224) % 32
    x = np.arange(128)
    theta = 2 * np.pi * ((m2[:, None] * x[None, :]) % 128) / 128
    c, s = np.cos(theta), np.sin(theta)
    part = part[:, None]
    table = np.concatenate([np.where(part == 0, c, -s), np.where(part == 0, s, c)], axis=1)
    hi = table.astype(jnp.bfloat16)
    lo = (table - hi.astype(np.float64)).astype(jnp.bfloat16)
    angle = 2 * np.pi * np.arange(10)[:, None] * x[None, :] / 1280
    twiddle = np.stack([np.cos(angle), np.sin(angle)], axis=1).reshape(20, 128).astype(np.float32)
    return hi, lo, twiddle


def to_grid(dep_lat, dep_col, received, order, lon_steps, tilt_steps, levs):
    hi, lo, twiddle = dft_tables()
    vmem = pl.BlockSpec(memory_space=pltpu.VMEM)
    outside = pl.BlockSpec(memory_space=pl.ANY)

    def kernel(*refs):
        grid_kernel(*refs, levs)

    return pl.pallas_call(
        kernel,
        out_shape=[jax.ShapeDtypeStruct((2, 4, 1280), f32)] * 2,
        in_specs=[outside, outside] + [vmem] * 7,
        out_specs=[vmem, vmem],
        scratch_shapes=[
            pltpu.VMEM((2, 192, 512), bf16),
            pltpu.VMEM((10, 48, 128), f32),
            pltpu.VMEM((10, 48, 128), f32),
            pltpu.SMEM(dep_lat.shape, jnp.int32),
            pltpu.SMEM(dep_col.shape, jnp.int32),
            pltpu.SemaphoreType.DMA,
            pltpu.SemaphoreType.DMA,
        ],
        compiler_params=pltpu.CompilerParams(vmem_limit_bytes=LIMIT),
        name="grid",
    )(dep_lat, dep_col, received, order, lon_steps, tilt_steps, jnp.asarray(hi), jnp.asarray(lo), jnp.asarray(twiddle))


def per_device(legendre, spectral, pair_low, dep_lat, dep_col, lon_steps, tilt_steps):
    waves, levs = lax.axis_size("wave"), lax.axis_size("lev")
    received, order = exchange(pair_low, legendre, spectral, waves, levs)
    received = received.reshape(waves, 3, 8, 128)
    return tuple(to_grid(dep_lat, dep_col, received, order, lon_steps, tilt_steps, levs))


def solution(mesh):
    return jax.shard_map(
        per_device,
        mesh=mesh,
        in_specs=(
            P("wave", None, None),
            P("wave", "lev", None, None),
            P(),
            P("wave"),
            P("wave"),
            P("wave", None),
            P("wave", None),
        ),
        out_specs=(P("lev", "wave", None), P("lev", "wave", None)),
        check_vma=False,
    )
```

```python
import functools
import math

import jax
import jax.numpy as jnp
import numpy as np
from jax import lax
from jax.experimental import pallas as pl
from jax.experimental.pallas import tpu as pltpu
from jax.sharding import PartitionSpec as P

MESH = pl.DeviceIdType.MESH
LIMIT = 16 * 1024 * 1024
NT = (((1,), (1,)), ((), ()))
f32 = jnp.float32
bf16 = jnp.bfloat16


def split(x):
    hi = x.astype(bf16)
    lo = (x - hi.astype(f32)).astype(bf16)
    return hi, lo


def legendre_into(send_ref, low_of, leg_ref, spec_ref, wait_pair, y_ref, z_ref, turn):
    pairs, lats, slots = leg_ref.shape
    top = slots - 1
    k = lax.broadcasted_iota(jnp.int32, (8, slots), 1)
    row = lax.broadcasted_iota(jnp.int32, (8, slots), 0)
    southern, second, real = row >= 4, (row & 2) != 0, (row & 1) == 0
    signed_k = jnp.where(second, k, -k)

    def signs(parity):
        return jnp.where(jnp.logical_and(southern, parity != 0), -1.0, 1.0)

    sign_even = signs(k & 1)
    sign_odd = jnp.where(second, signs((k + 1) & 1), sign_even)
    y_ref[...] = jnp.zeros_like(y_ref)
    send_ref[0] = jnp.zeros(send_ref.shape[1:], f32)
    send_ref[lats // 2 + 1] = jnp.zeros(send_ref.shape[1:], f32)
    for s in range(pairs):
        wait_pair(s)
        first = top - low_of(s)
        keep = signed_k >= jnp.where(second, first, 1 - first)
        mask = jnp.where(keep, jnp.where((first & 1) == 0, sign_even, sign_odd), 0.0)
        rows = []
        for lev in range(2):
            re = jnp.broadcast_to(spec_ref[s, lev, 0:1, :], (8, slots))
            im = jnp.broadcast_to(spec_ref[s, lev, 1:2, :], (8, slots))
            rows.append(jnp.where(real, re, im) * mask)
        hi, lo = split(jnp.concatenate(rows, axis=0))
        leg_hi, leg_lo = split(leg_ref[s])
        both = lax.dot_general(jnp.concatenate([hi, lo], axis=0), leg_hi, NT, preferred_element_type=f32)
        small = lax.dot_general(hi, leg_lo, NT, preferred_element_type=f32)
        y_ref[pl.ds(s, 16, stride=16), :] = both[:16] + (both[16:] + small)
    lane = lax.broadcasted_iota(jnp.int32, (lats // 2, 128), 1)
    for lev in range(2):
        z_ref[...] = y_ref[pl.ds(128 * lev, 128), :].T
        even = z_ref[pl.ds(0, lats // 2, stride=2), :]
        odd = z_ref[pl.ds(1, lats // 2, stride=2), :]
        for h in range(2):
            if h == 0:
                val = jnp.where(lane < 64, even, pltpu.roll(odd, 64, 1))
            else:
                val = jnp.where(lane < 64, pltpu.roll(even, 64, 1), odd)
            val = pltpu.roll(val, 16 * turn, 1)
            for j in range(lats // 2):
                send_ref[1 + j, lev, h : h + 1, :] = val[j : j + 1, :]


def exchange_kernel(
    waves, levs, low_hbm, leg_hbm, spec_hbm, col_hbm, lon_hbm, tilt_hbm,
    recv_ref, order_ref, index_ref, mix_ref,
    low_smem, low_vmem, leg_ref, spec_ref, y_ref, z_ref, send_ref,
    low_sem, leg_sem, spec_sem, send_sem, recv_sem, down_send_sem, down_recv_sem,
    proxy_ref, proxy_sem, proxy_down_sem, relay_sem, relay_down_sem, ready,
    col_smem, lon_vmem, tilt_vmem, plan_sem,
):
    me = lax.axis_index("wave")
    lev = lax.axis_index("lev")
    pairs, _, slots = leg_ref.shape
    low_copy = pltpu.make_async_copy(low_hbm, low_smem, low_sem.at[0])
    low_copy.start()
    spec_copy = pltpu.make_async_copy(spec_hbm, spec_ref, spec_sem)
    spec_copy.start()
    leg_copies = [
        pltpu.make_async_copy(leg_hbm.at[s], leg_ref.at[s], leg_sem.at[s]) for s in range(pairs)
    ]
    for copy in leg_copies:
        copy.start()
    low_again = pltpu.make_async_copy(low_hbm, low_vmem, low_sem.at[1])
    low_again.start()
    plan_copies = [
        pltpu.make_async_copy(src, dst, plan_sem.at[i])
        for i, (src, dst) in enumerate([(col_hbm, col_smem), (lon_hbm, lon_vmem), (tilt_hbm, tilt_vmem)])
    ]
    for copy in plan_copies:
        copy.start()

    barrier = pltpu.get_barrier_semaphore()
    late = me == 0
    lower, upper = lev > 0, lev < levs - 1
    peers = waves - 1

    def signal(sem, to_lev, to_wave):
        pl.semaphore_signal(sem, inc=1, device_id={"lev": to_lev, "wave": to_wave}, device_id_type=MESH)

    def each(first, body):
        def step(d, _):
            body(d)
            return 0

        lax.fori_loop(first, waves, step, 0)

    @pl.when(jnp.logical_not(late))
    def _():
        each(1, lambda d: signal(barrier, lev, lax.rem(me + d, waves)))

        @pl.when(upper)
        def _():
            each(0, lambda w: signal(barrier, lev + 1, w))

    @pl.when(late)
    def _():
        pl.semaphore_wait(barrier, peers + jnp.where(lower, peers, 0))
        signal(ready, lev, 1)

    low_copy.wait()

    def wait_pair(s):
        if s == 0:
            spec_copy.wait()
            for copy in leg_copies:
                copy.wait()

    legendre_into(
        send_ref, lambda s: low_smem[me * pairs + s], leg_ref, spec_ref, wait_pair, y_ref, z_ref,
        lax.rem(me, 8),
    )

    @pl.when(jnp.logical_not(late))
    def _():
        pl.semaphore_wait(barrier, peers - 1 + jnp.where(lower, peers, 0))

    def across(peer, slots_of, to_wave, sem):
        pltpu.make_async_remote_copy(
            src_ref=send_ref.at[pl.ds(peer, 3)],
            dst_ref=slots_of.at[me, :, pl.ds(0, 2)],
            send_sem=send_sem,
            recv_sem=sem,
            device_id={"lev": lev, "wave": to_wave},
            device_id_type=MESH,
        ).start()

    def down(peer, slots_of, to_wave, sem):
        pltpu.make_async_remote_copy(
            src_ref=send_ref.at[pl.ds(peer, 3), 0],
            dst_ref=slots_of.at[me, :, 2],
            send_sem=down_send_sem,
            recv_sem=sem,
            device_id={"lev": lev - 1, "wave": to_wave},
            device_id_type=MESH,
        ).start()

    def spread(d):
        peer = lax.rem(me + waves // 2 + d, waves)

        @pl.when(jnp.logical_and(peer != 0, peer != me))
        def _():
            across(peer, recv_ref, peer, recv_sem)

    each(0, spread)

    @pl.when(me > 1)
    def _():
        across(0, proxy_ref, 1, proxy_sem)

    @pl.when(lower)
    def _():
        each(1, lambda w: down(w, recv_ref, w, down_recv_sem))
        down(0, proxy_ref, 1, proxy_down_sem)

    pltpu.make_async_copy(send_ref.at[pl.ds(me, 3)], recv_ref.at[me, :, pl.ds(0, 2)], recv_sem).start()
    low_again.wait()
    order_into(order_ref, low_vmem, slots - 1)
    for copy in plan_copies:
        copy.wait()
    plan_into(index_ref, mix_ref, col_smem, lon_vmem, tilt_vmem)

    def wait_for(part, sem):
        pltpu.make_async_copy(part, part, sem).wait()

    def relay(part_of, sem, to_sem):
        return pltpu.make_async_remote_copy(
            src_ref=part_of(proxy_ref),
            dst_ref=part_of(recv_ref),
            send_sem=sem,
            recv_sem=to_sem,
            device_id={"lev": lev, "wave": 0},
            device_id_type=MESH,
        )

    def others(ref):
        return ref.at[pl.ds(1, waves - 1), :, pl.ds(0, 2)]

    def downs(ref):
        return ref.at[:, :, 2]

    @pl.when(me == 1)
    def _():
        pltpu.make_async_copy(send_ref.at[pl.ds(0, 3)], proxy_ref.at[me, :, pl.ds(0, 2)], proxy_sem).start()
        wait_for(others(proxy_ref), proxy_sem)

        @pl.when(upper)
        def _():
            wait_for(downs(proxy_ref), proxy_down_sem)

        pl.semaphore_wait(ready, 1)
        relay(others, relay_sem, recv_sem).start()

        @pl.when(upper)
        def _():
            relay(downs, relay_down_sem, down_recv_sem).start()

    wait_for(recv_ref.at[:, :, pl.ds(0, 2)], recv_sem)

    @pl.when(upper)
    def _():
        wait_for(downs(recv_ref), down_recv_sem)

    @pl.when(me == 1)
    def _():
        wait_for(others(proxy_ref), relay_sem)
        wait_for(recv_ref.at[pl.ds(0, waves - 2), :, pl.ds(0, 2)], send_sem)

        @pl.when(upper)
        def _():
            wait_for(downs(proxy_ref), relay_down_sem)

    @pl.when(me != 1)
    def _():
        wait_for(others(recv_ref), send_sem)

    @pl.when(lower)
    def _():
        wait_for(downs(recv_ref), down_send_sem)


def exchange(pair_low, legendre, spectral, dep_col, lon_steps, tilt_steps, waves, levs):
    pairs, lats, slots = legendre.shape
    any_space = pl.BlockSpec(memory_space=pltpu.HBM)
    operands = (pair_low, legendre, spectral, dep_col, lon_steps, tilt_steps)
    vmem = pl.BlockSpec(memory_space=pltpu.VMEM)
    return pl.pallas_call(
        functools.partial(exchange_kernel, waves, levs),
        out_shape=[
            jax.ShapeDtypeStruct((waves, 3, 4, 2, 128), f32),
            jax.ShapeDtypeStruct((2, 384, 512), bf16),
            jax.ShapeDtypeStruct((20, 8, 128), jnp.int32),
            jax.ShapeDtypeStruct((20, 5, 8, 128), f32),
        ],
        in_specs=[any_space] * 6,
        out_specs=[vmem] * 4,
        scratch_shapes=[
            pltpu.SMEM(pair_low.shape, jnp.int32),
            pltpu.VMEM(pair_low.shape, jnp.int32),
            pltpu.VMEM((pairs, lats, slots), f32),
            pltpu.VMEM(spectral.shape, f32),
            pltpu.VMEM((256, lats), f32),
            pltpu.VMEM((lats, 128), f32),
            pltpu.VMEM((lats // 2 + 2, 2, 2, 128), f32),
            pltpu.SemaphoreType.DMA((2,)),
            pltpu.SemaphoreType.DMA((pairs,)),
            pltpu.SemaphoreType.DMA,
            pltpu.SemaphoreType.DMA,
            pltpu.SemaphoreType.DMA,
            pltpu.SemaphoreType.DMA,
            pltpu.SemaphoreType.DMA,
            pltpu.VMEM((waves, 3, 4, 2, 128), f32),
            pltpu.SemaphoreType.DMA,
            pltpu.SemaphoreType.DMA,
            pltpu.SemaphoreType.DMA,
            pltpu.SemaphoreType.DMA,
            pltpu.SemaphoreType.REGULAR,
            pltpu.SMEM(dep_col.shape, jnp.int32),
            pltpu.VMEM(lon_steps.shape, jnp.int32),
            pltpu.VMEM(tilt_steps.shape, jnp.int32),
            pltpu.SemaphoreType.DMA((3,)),
        ],
        compiler_params=pltpu.CompilerParams(
            collective_id=0, has_side_effects=True, vmem_limit_bytes=LIMIT
        ),
    )(*[pltpu.with_memory_space_constraint(a, pltpu.HBM) for a in operands])


def spread_low(low_ref):
    lane = lax.broadcasted_iota(jnp.int32, (8, 128), 1)
    row = low_ref[...].reshape(1, low_ref.shape[0])
    ends = [(0, 128), (128, 256), (192, 320)]
    parts = [jnp.broadcast_to(row[:, a:b], (8, 128)) for a, b in ends]
    out = []
    for v in range(4):
        source = 80 * v + 10 * (lane // 16) + lane % 16
        first = 80 * v // 128
        last = (80 * v + 79) // 128
        shift = [0, 0, 64]
        got = jnp.take_along_axis(parts[first], (source + shift[first]) % 128, axis=1)
        if last != first:
            other = jnp.take_along_axis(parts[last], (source + shift[last]) % 128, axis=1)
            got = jnp.where(source // 128 == first, got, other)
        out.append(jnp.where(lane % 16 < 10, got, -1))
    return out


def order_into(order_ref, low_ref, top):
    low = spread_low(low_ref)
    columns = order_ref.shape[1]
    for e in range(2):
        for n0 in range(0, columns, 16):
            g, q, mu0 = n0 // 128, n0 % 128 // 32, n0 % 32
            p = 4 * g + q
            row = lax.broadcasted_iota(jnp.int32, (8, 128), 0)
            halves = []
            for half in range(2):
                m = p + 10 * (32 * e + mu0 + 8 * half + row)
                want = m if e == 0 else top - 1 - m
                weight = jnp.where(m == 0, 1.0, 2.0) if (e == 0 and p == 0) else jnp.full((8, 128), 2.0, f32)
                halves.append((want, weight))
            for v in range(4):
                if p >= 10:
                    block = jnp.zeros((16, 128), f32)
                else:
                    block = jnp.concatenate(
                        [jnp.where(low[v] == want, weight, 0.0) for want, weight in halves], axis=0
                    )
                order_ref[e, pl.ds(n0, 16), pl.ds(128 * v, 128)] = block.astype(bf16)


def plan_into(index_ref, mix_ref, col_ref, lon_ref, tilt_ref):
    lane = lax.broadcasted_iota(jnp.int32, (8, 128), 1)
    hemi = lax.broadcasted_iota(jnp.int32, (8, 128), 0) % 2 == 1
    for l in range(2):
        for x in range(10):
            north, south = 10 * l + x, 20 + 10 * l + x

            def pick(ref):
                return jnp.where(
                    hemi,
                    jnp.broadcast_to(ref[south : south + 1, :], (8, 128)),
                    jnp.broadcast_to(ref[north : north + 1, :], (8, 128)),
                )

            lon, tilt = pick(lon_ref), pick(tilt_ref)

            def shift_of(block):
                return lax.rem(col_ref[block] - 128 * x + 1280 + 640, 1280) - 643

            n = 10 * l + x
            index_ref[n] = lane + jnp.where(hemi, shift_of(south), shift_of(north)) + (lon >> 2)
            f = (lon & 3).astype(f32) * 0.25
            g = (tilt & 3).astype(f32) * 0.25
            mix_ref[n, 0] = (1.0 - g) * (1.0 - f)
            mix_ref[n, 1] = (1.0 - g) * f
            mix_ref[n, 2] = g * (1.0 - f)
            mix_ref[n, 3] = g * f
            mix_ref[n, 4] = (tilt >> 2).astype(f32) * 0.25


def grid_kernel(
    lat_ref, recv_ref, order_ref, index_ref, mix_ref, table_hi_ref, table_lo_ref, twiddle_ref,
    grid_ref, departed_ref, x_ref, field_ref, edge_ref, lat_smem, lat_sem, levs,
):
    lat_copy = pltpu.make_async_copy(lat_ref, lat_smem, lat_sem)
    lat_copy.start()
    wave = lax.axis_index("wave")
    last = lax.axis_index("lev") == levs - 1

    lane = lax.broadcasted_iota(jnp.int32, (8, 128), 1)
    slot = lane // 16
    for grp in range(4):
        for t in range(3):
            arr = [recv_ref[8 * grp + j, t] for j in range(8)]
            for bit in range(3):
                step = 1 << bit
                on = (slot & step) != 0
                arr = [jnp.where(on, arr[(j + step) % 8], arr[j]) for j in range(8)]
            for e in range(2):
                for r in range(2):
                    pieces = []
                    for l in range(2):
                        c = 4 * l + 2 * e + r
                        pieces.append(pltpu.roll(arr[-c % 8], (128 - 16 * c) % 128, 1))
                    hi, lo = split(jnp.concatenate(pieces, axis=0))
                    cols = pl.ds(128 * grp, 128)
                    x_ref[e, pl.ds(48 * r + 16 * t, 16), cols] = hi
                    x_ref[e, pl.ds(96 + 48 * r + 16 * t, 16), cols] = lo

    sums = []
    for e in range(2):
        both = lax.dot_general(x_ref[e], order_ref[e], NT, preferred_element_type=f32)
        sums.append(both[:96] + both[96:])

    slot48 = lax.broadcasted_iota(jnp.int32, (48, 128), 1) // 32
    by_q = [[] for _ in range(4)]
    for g in range(3):
        arr = []
        for i in range(4):
            block = sums[i // 2][48 * (i % 2) : 48 * (i % 2) + 48, 128 * g : 128 * g + 128]
            arr.append(pltpu.roll(block, 32 * i, 1) if i else block)
        for bit in range(2):
            step = 1 << bit
            on = (slot48 & step) != 0
            arr = [jnp.where(on, arr[(j + step) % 4], arr[j]) for j in range(4)]
        for q in range(4):
            if 4 * g + q < 10:
                by_q[q].append(arr[-q % 4])
    re, im = [None] * 10, [None] * 10
    for q in range(4):
        n = 48 * len(by_q[q])
        hi, lo = split(jnp.concatenate(by_q[q], axis=0))
        rows = pl.ds(32 * (-q % 4), 128)
        both = jnp.dot(jnp.concatenate([hi, lo], axis=0), table_hi_ref[rows, :], preferred_element_type=f32)
        small = jnp.dot(hi, table_lo_ref[rows, :], preferred_element_type=f32)
        total = both[:n] + (both[n:] + small)
        for g in range(len(by_q[q])):
            p = 4 * g + q
            a, b = total[48 * g : 48 * g + 48, :128], total[48 * g : 48 * g + 48, 128:]
            if p == 0:
                re[p], im[p] = a, b
            else:
                c = twiddle_ref[2 * p : 2 * p + 1, :]
                s = twiddle_ref[2 * p + 1 : 2 * p + 2, :]
                re[p] = a * c - b * s
                im[p] = a * s + b * c

    def put(x, value):
        field_ref[x] = value

    even = [re[p] + re[10 - p] for p in (1, 2, 3, 4)]
    diff = [im[p] - im[10 - p] for p in (1, 2, 3, 4)]
    for x in range(3):
        co = [math.cos(math.pi * p * x / 5) for p in (1, 2, 3, 4)]
        si = [math.sin(math.pi * p * x / 5) for p in (1, 2, 3, 4)]
        if x == 0:
            a_even = re[0] + (even[1] + even[3])
            a_odd = re[5] + (even[0] + even[2])
            put(0, a_even + a_odd)
            put(5, a_even - a_odd)
            continue
        a_even = re[0] + (co[1] * even[1] + co[3] * even[3])
        a_odd = (co[0] * even[0] + co[2] * even[2]) + (re[5] if x % 2 == 0 else -re[5])
        b_even = si[1] * diff[1] + si[3] * diff[3]
        b_odd = si[0] * diff[0] + si[2] * diff[2]
        a, b = a_even + a_odd, b_even + b_odd
        put(x, a - b)
        put(10 - x, a + b)
        a, b = a_even - a_odd, b_odd - b_even
        put(5 - x, a - b)
        put(5 + x, a + b)

    lane48 = lax.broadcasted_iota(jnp.int32, (48, 128), 1)
    for x in range(10):
        edge_ref[x] = jnp.where(lane48 < 64, field_ref[(x + 1) % 10], field_ref[(x + 9) % 10])
        for l in range(2):
            for row in range(4):
                lev, h = row // 2, row % 2
                grid_ref[lev, pl.ds(2 * h + l, 1), pl.ds(128 * x, 128)] = field_ref[x, pl.ds(8 * (2 + l) + row, 1), :]

    lat_copy.wait()
    hemi = lax.broadcasted_iota(jnp.int32, (8, 128), 0) % 2 == 1
    keep_own = jnp.logical_and(last, lax.broadcasted_iota(jnp.int32, (8, 128), 0) >= 2)
    for l in range(2):
        for x in range(10):
            north, south = 10 * l + x, 20 + 10 * l + x

            n = 10 * l + x
            index = index_ref[n]
            nxt = index + 1
            starts = [8 * (lat_smem[block] + (2 - 2 * wave)) for block in (north, south)]
            rows = []
            for off in range(2):
                at = [pl.multiple_of(start + 8 * off, 8) for start in starts]
                main = jnp.where(hemi, field_ref[x, pl.ds(at[1], 8), :], field_ref[x, pl.ds(at[0], 8), :])
                edge = jnp.where(hemi, edge_ref[x, pl.ds(at[1], 8), :], edge_ref[x, pl.ds(at[0], 8), :])

                def look(column):
                    wrapped = column & 127
                    return jnp.where(
                        wrapped == column,
                        jnp.take_along_axis(main, wrapped, axis=1),
                        jnp.take_along_axis(edge, wrapped, axis=1),
                    )

                rows.append(mix_ref[n, 2 * off] * look(index) + mix_ref[n, 2 * off + 1] * look(nxt))
            horizontal = rows[0] + rows[1]
            v = mix_ref[n, 4]
            upper = jnp.where(keep_own, horizontal, pltpu.roll(horizontal, 6, 0))
            departed = (1.0 - v) * horizontal + v * upper
            for row in range(4):
                lev, h = row // 2, row % 2
                departed_ref[lev, pl.ds(2 * h + l, 1), pl.ds(128 * x, 128)] = departed[row : row + 1, :]


def dft_tables():
    slot = np.arange(224) // 32 % 4
    member, part = slot // 2, slot % 2
    m2 = 32 * member + np.arange(224) % 32
    x = np.arange(128)
    theta = 2 * np.pi * ((m2[:, None] * x[None, :]) % 128) / 128
    c, s = np.cos(theta), np.sin(theta)
    part = part[:, None]
    table = np.concatenate([np.where(part == 0, c, -s), np.where(part == 0, s, c)], axis=1)
    hi = table.astype(jnp.bfloat16)
    lo = (table - hi.astype(np.float64)).astype(jnp.bfloat16)
    angle = 2 * np.pi * np.arange(10)[:, None] * x[None, :] / 1280
    twiddle = np.stack([np.cos(angle), np.sin(angle)], axis=1).reshape(20, 128).astype(np.float32)
    return hi, lo, twiddle


def to_grid(dep_lat, received, order, index, mix, levs):
    hi, lo, twiddle = dft_tables()
    vmem = pl.BlockSpec(memory_space=pltpu.VMEM)
    outside = pl.BlockSpec(memory_space=pl.ANY)

    def kernel(*refs):
        grid_kernel(*refs, levs)

    return pl.pallas_call(
        kernel,
        out_shape=[jax.ShapeDtypeStruct((2, 4, 1280), f32)] * 2,
        in_specs=[outside] + [vmem] * 7,
        out_specs=[vmem, vmem],
        scratch_shapes=[
            pltpu.VMEM((2, 192, 512), bf16),
            pltpu.VMEM((10, 48, 128), f32),
            pltpu.VMEM((10, 48, 128), f32),
            pltpu.SMEM(dep_lat.shape, jnp.int32),
            pltpu.SemaphoreType.DMA,
        ],
        compiler_params=pltpu.CompilerParams(vmem_limit_bytes=LIMIT),
        name="grid",
    )(dep_lat, received, order, index, mix, jnp.asarray(hi), jnp.asarray(lo), jnp.asarray(twiddle))


def per_device(legendre, spectral, pair_low, dep_lat, dep_col, lon_steps, tilt_steps):
    waves, levs = lax.axis_size("wave"), lax.axis_size("lev")
    received, order, index, mix = exchange(
        pair_low, legendre, spectral, dep_col, lon_steps, tilt_steps, waves, levs
    )
    received = received.reshape(waves, 3, 8, 128)
    return tuple(to_grid(dep_lat, received, order, index, mix, levs))


def solution(mesh):
    return jax.shard_map(
        per_device,
        mesh=mesh,
        in_specs=(
            P("wave", None, None),
            P("wave", "lev", None, None),
            P(),
            P("wave"),
            P("wave"),
            P("wave", None),
            P("wave", None),
        ),
        out_specs=(P("lev", "wave", None), P("lev", "wave", None)),
        check_vma=False,
    )
```

```python
import functools
import math

import jax
import jax.numpy as jnp
import numpy as np
from jax import lax
from jax.experimental import pallas as pl
from jax.experimental.pallas import tpu as pltpu
from jax.sharding import PartitionSpec as P

MESH = pl.DeviceIdType.MESH
LIMIT = 16 * 1024 * 1024
NT = (((1,), (1,)), ((), ()))
f32 = jnp.float32
bf16 = jnp.bfloat16


def split(x):
    hi = x.astype(bf16)
    lo = (x - hi.astype(f32)).astype(bf16)
    return hi, lo


def legendre_into(send_ref, low_of, leg_ref, spec_ref, wait_pair, y_ref, z_ref, turn):
    pairs, lats, slots = leg_ref.shape
    top = slots - 1
    k = lax.broadcasted_iota(jnp.int32, (8, slots), 1)
    row = lax.broadcasted_iota(jnp.int32, (8, slots), 0)
    southern, second, real = row >= 4, (row & 2) != 0, (row & 1) == 0
    signed_k = jnp.where(second, k, -k)

    def signs(parity):
        return jnp.where(jnp.logical_and(southern, parity != 0), -1.0, 1.0)

    sign_even = signs(k & 1)
    sign_odd = jnp.where(second, signs((k + 1) & 1), sign_even)
    y_ref[...] = jnp.zeros_like(y_ref)
    send_ref[0] = jnp.zeros(send_ref.shape[1:], f32)
    send_ref[lats // 2 + 1] = jnp.zeros(send_ref.shape[1:], f32)
    for s in range(pairs):
        wait_pair(s)
        first = top - low_of(s)
        keep = signed_k >= jnp.where(second, first, 1 - first)
        mask = jnp.where(keep, jnp.where((first & 1) == 0, sign_even, sign_odd), 0.0)
        rows = []
        for lev in range(2):
            re = jnp.broadcast_to(spec_ref[s, lev, 0:1, :], (8, slots))
            im = jnp.broadcast_to(spec_ref[s, lev, 1:2, :], (8, slots))
            rows.append(jnp.where(real, re, im) * mask)
        hi, lo = split(jnp.concatenate(rows, axis=0))
        leg_hi, leg_lo = split(leg_ref[s])
        both = lax.dot_general(jnp.concatenate([hi, lo], axis=0), leg_hi, NT, preferred_element_type=f32)
        small = lax.dot_general(hi, leg_lo, NT, preferred_element_type=f32)
        y_ref[pl.ds(s, 16, stride=16), :] = both[:16] + (both[16:] + small)
    lane = lax.broadcasted_iota(jnp.int32, (lats // 2, 128), 1)
    for lev in range(2):
        z_ref[...] = y_ref[pl.ds(128 * lev, 128), :].T
        even = z_ref[pl.ds(0, lats // 2, stride=2), :]
        odd = z_ref[pl.ds(1, lats // 2, stride=2), :]
        for h in range(2):
            if h == 0:
                val = jnp.where(lane < 64, even, pltpu.roll(odd, 64, 1))
            else:
                val = jnp.where(lane < 64, pltpu.roll(even, 64, 1), odd)
            val = pltpu.roll(val, 16 * turn, 1)
            for j in range(lats // 2):
                send_ref[1 + j, lev, h : h + 1, :] = val[j : j + 1, :]


def exchange_kernel(
    waves, levs, low_hbm, leg_hbm, spec_hbm, col_hbm, lon_hbm, tilt_hbm,
    recv_ref, order_ref, index_ref, mix_ref,
    low_smem, low_vmem, leg_ref, spec_ref, y_ref, z_ref, send_ref,
    low_sem, leg_sem, spec_sem, send_sem, recv_sem, down_send_sem, down_recv_sem,
    proxy_ref, proxy_sem, proxy_down_sem, relay_sem, relay_down_sem, ready,
    col_smem, lon_vmem, tilt_vmem, plan_sem,
):
    me = lax.axis_index("wave")
    lev = lax.axis_index("lev")
    pairs, _, slots = leg_ref.shape
    low_copy = pltpu.make_async_copy(low_hbm, low_smem, low_sem.at[0])
    low_copy.start()
    spec_copy = pltpu.make_async_copy(spec_hbm, spec_ref, spec_sem)
    spec_copy.start()
    for s in range(0, pairs, 2):
        pltpu.make_async_copy(leg_hbm.at[pl.ds(s, 2)], leg_ref.at[pl.ds(s, 2)], leg_sem).start()
    low_again = pltpu.make_async_copy(low_hbm, low_vmem, low_sem.at[1])
    low_again.start()
    plan_copies = [
        pltpu.make_async_copy(src, dst, plan_sem.at[i])
        for i, (src, dst) in enumerate([(col_hbm, col_smem), (lon_hbm, lon_vmem), (tilt_hbm, tilt_vmem)])
    ]
    for copy in plan_copies:
        copy.start()

    barrier = pltpu.get_barrier_semaphore()
    late = me == 0
    lower, upper = lev > 0, lev < levs - 1
    peers = waves - 1

    def signal(sem, to_lev, to_wave):
        pl.semaphore_signal(sem, inc=1, device_id={"lev": to_lev, "wave": to_wave}, device_id_type=MESH)

    def each(first, body):
        def step(d, _):
            body(d)
            return 0

        lax.fori_loop(first, waves, step, 0)

    @pl.when(jnp.logical_not(late))
    def _():
        each(1, lambda d: signal(barrier, lev, lax.rem(me + d, waves)))

        @pl.when(upper)
        def _():
            each(0, lambda w: signal(barrier, lev + 1, w))

    @pl.when(late)
    def _():
        pl.semaphore_wait(barrier, peers + jnp.where(lower, peers, 0))
        signal(ready, lev, 1)

    low_copy.wait()

    def wait_pair(s):
        if s == 0:
            spec_copy.wait()
            pltpu.make_async_copy(leg_hbm, leg_ref, leg_sem).wait()

    legendre_into(
        send_ref, lambda s: low_smem[me * pairs + s], leg_ref, spec_ref, wait_pair, y_ref, z_ref,
        lax.rem(me, 8),
    )

    @pl.when(jnp.logical_not(late))
    def _():
        pl.semaphore_wait(barrier, peers - 1 + jnp.where(lower, peers, 0))

    def across(peer, slots_of, to_wave, sem):
        pltpu.make_async_remote_copy(
            src_ref=send_ref.at[pl.ds(peer, 3)],
            dst_ref=slots_of.at[me, :, pl.ds(0, 2)],
            send_sem=send_sem,
            recv_sem=sem,
            device_id={"lev": lev, "wave": to_wave},
            device_id_type=MESH,
        ).start()

    def down(peer, slots_of, to_wave, sem):
        pltpu.make_async_remote_copy(
            src_ref=send_ref.at[pl.ds(peer, 3), 0],
            dst_ref=slots_of.at[me, :, 2],
            send_sem=down_send_sem,
            recv_sem=sem,
            device_id={"lev": lev - 1, "wave": to_wave},
            device_id_type=MESH,
        ).start()

    def turn(quarter):
        return jnp.where(quarter == 0, 0, jnp.where(quarter == 1, 3, quarter - 1))

    def spread(d):
        peer = lax.rem(me + 8 * turn(d // 8) + d % 8, waves)

        @pl.when(peer != 0)
        def _():
            across(peer, recv_ref, peer, recv_sem)

    @pl.when(late)
    def _():
        for peer in [*range(1, 8), *range(24, 32), *range(8, 24)]:
            across(peer, recv_ref, peer, recv_sem)

    @pl.when(jnp.logical_not(late))
    def _():
        each(1, spread)

    @pl.when(me > 1)
    def _():
        across(0, proxy_ref, 1, proxy_sem)

    @pl.when(lower)
    def _():
        each(1, lambda w: down(w, recv_ref, w, down_recv_sem))
        down(0, proxy_ref, 1, proxy_down_sem)

    pltpu.make_async_copy(send_ref.at[pl.ds(me, 3)], recv_ref.at[me, :, pl.ds(0, 2)], recv_sem).start()
    low_again.wait()
    order_into(order_ref, low_vmem, slots - 1)
    for copy in plan_copies:
        copy.wait()
    plan_into(index_ref, mix_ref, col_smem, lon_vmem, tilt_vmem)

    def wait_for(part, sem):
        pltpu.make_async_copy(part, part, sem).wait()

    def relay(part_of, sem, to_sem):
        return pltpu.make_async_remote_copy(
            src_ref=part_of(proxy_ref),
            dst_ref=part_of(recv_ref),
            send_sem=sem,
            recv_sem=to_sem,
            device_id={"lev": lev, "wave": 0},
            device_id_type=MESH,
        )

    def others(ref):
        return ref.at[pl.ds(1, waves - 1), :, pl.ds(0, 2)]

    def downs(ref):
        return ref.at[:, :, 2]

    @pl.when(me == 1)
    def _():
        pltpu.make_async_copy(send_ref.at[pl.ds(0, 3)], proxy_ref.at[me, :, pl.ds(0, 2)], proxy_sem).start()
        wait_for(others(proxy_ref), proxy_sem)

        @pl.when(upper)
        def _():
            wait_for(downs(proxy_ref), proxy_down_sem)

        pl.semaphore_wait(ready, 1)
        relay(others, relay_sem, recv_sem).start()

        @pl.when(upper)
        def _():
            relay(downs, relay_down_sem, down_recv_sem).start()

    wait_for(recv_ref.at[:, :, pl.ds(0, 2)], recv_sem)

    @pl.when(upper)
    def _():
        wait_for(downs(recv_ref), down_recv_sem)

    @pl.when(me == 1)
    def _():
        wait_for(others(proxy_ref), relay_sem)
        wait_for(recv_ref.at[pl.ds(0, waves - 2), :, pl.ds(0, 2)], send_sem)

        @pl.when(upper)
        def _():
            wait_for(downs(proxy_ref), relay_down_sem)

    @pl.when(me != 1)
    def _():
        wait_for(others(recv_ref), send_sem)

    @pl.when(lower)
    def _():
        wait_for(downs(recv_ref), down_send_sem)


def exchange(pair_low, legendre, spectral, dep_col, lon_steps, tilt_steps, waves, levs):
    pairs, lats, slots = legendre.shape
    any_space = pl.BlockSpec(memory_space=pltpu.HBM)
    operands = (pair_low, legendre, spectral, dep_col, lon_steps, tilt_steps)
    vmem = pl.BlockSpec(memory_space=pltpu.VMEM)
    return pl.pallas_call(
        functools.partial(exchange_kernel, waves, levs),
        out_shape=[
            jax.ShapeDtypeStruct((waves, 3, 4, 2, 128), f32),
            jax.ShapeDtypeStruct((2, 384, 512), bf16),
            jax.ShapeDtypeStruct((20, 8, 128), jnp.int32),
            jax.ShapeDtypeStruct((20, 5, 8, 128), f32),
        ],
        in_specs=[any_space] * 6,
        out_specs=[vmem] * 4,
        scratch_shapes=[
            pltpu.SMEM(pair_low.shape, jnp.int32),
            pltpu.VMEM(pair_low.shape, jnp.int32),
            pltpu.VMEM((pairs, lats, slots), f32),
            pltpu.VMEM(spectral.shape, f32),
            pltpu.VMEM((256, lats), f32),
            pltpu.VMEM((lats, 128), f32),
            pltpu.VMEM((lats // 2 + 2, 2, 2, 128), f32),
            pltpu.SemaphoreType.DMA((2,)),
            pltpu.SemaphoreType.DMA,
            pltpu.SemaphoreType.DMA,
            pltpu.SemaphoreType.DMA,
            pltpu.SemaphoreType.DMA,
            pltpu.SemaphoreType.DMA,
            pltpu.SemaphoreType.DMA,
            pltpu.VMEM((waves, 3, 4, 2, 128), f32),
            pltpu.SemaphoreType.DMA,
            pltpu.SemaphoreType.DMA,
            pltpu.SemaphoreType.DMA,
            pltpu.SemaphoreType.DMA,
            pltpu.SemaphoreType.REGULAR,
            pltpu.SMEM(dep_col.shape, jnp.int32),
            pltpu.VMEM(lon_steps.shape, jnp.int32),
            pltpu.VMEM(tilt_steps.shape, jnp.int32),
            pltpu.SemaphoreType.DMA((3,)),
        ],
        compiler_params=pltpu.CompilerParams(
            collective_id=0, has_side_effects=True, vmem_limit_bytes=LIMIT
        ),
    )(*[pltpu.with_memory_space_constraint(a, pltpu.HBM) for a in operands])


def spread_low(low_ref):
    lane = lax.broadcasted_iota(jnp.int32, (8, 128), 1)
    row = low_ref[...].reshape(1, low_ref.shape[0])
    ends = [(0, 128), (128, 256), (192, 320)]
    parts = [jnp.broadcast_to(row[:, a:b], (8, 128)) for a, b in ends]
    out = []
    for v in range(4):
        source = 80 * v + 10 * (lane // 16) + lane % 16
        first = 80 * v // 128
        last = (80 * v + 79) // 128
        shift = [0, 0, 64]
        got = jnp.take_along_axis(parts[first], (source + shift[first]) % 128, axis=1)
        if last != first:
            other = jnp.take_along_axis(parts[last], (source + shift[last]) % 128, axis=1)
            got = jnp.where(source // 128 == first, got, other)
        out.append(jnp.where(lane % 16 < 10, got, -1))
    return out


def order_into(order_ref, low_ref, top):
    low = spread_low(low_ref)
    columns = order_ref.shape[1]
    for e in range(2):
        for n0 in range(0, columns, 16):
            g, q, mu0 = n0 // 128, n0 % 128 // 32, n0 % 32
            p = 4 * g + q
            row = lax.broadcasted_iota(jnp.int32, (8, 128), 0)
            halves = []
            for half in range(2):
                m = p + 10 * (32 * e + mu0 + 8 * half + row)
                want = m if e == 0 else top - 1 - m
                weight = jnp.where(m == 0, 1.0, 2.0) if (e == 0 and p == 0) else jnp.full((8, 128), 2.0, f32)
                halves.append((want, weight))
            for v in range(4):
                if p >= 10:
                    block = jnp.zeros((16, 128), f32)
                else:
                    block = jnp.concatenate(
                        [jnp.where(low[v] == want, weight, 0.0) for want, weight in halves], axis=0
                    )
                order_ref[e, pl.ds(n0, 16), pl.ds(128 * v, 128)] = block.astype(bf16)


def plan_into(index_ref, mix_ref, col_ref, lon_ref, tilt_ref):
    lane = lax.broadcasted_iota(jnp.int32, (8, 128), 1)
    hemi = lax.broadcasted_iota(jnp.int32, (8, 128), 0) % 2 == 1
    for l in range(2):
        for x in range(10):
            north, south = 10 * l + x, 20 + 10 * l + x

            def pick(ref):
                return jnp.where(
                    hemi,
                    jnp.broadcast_to(ref[south : south + 1, :], (8, 128)),
                    jnp.broadcast_to(ref[north : north + 1, :], (8, 128)),
                )

            lon, tilt = pick(lon_ref), pick(tilt_ref)

            def shift_of(block):
                return lax.rem(col_ref[block] - 128 * x + 1280 + 640, 1280) - 643

            n = 10 * l + x
            index_ref[n] = lane + jnp.where(hemi, shift_of(south), shift_of(north)) + (lon >> 2)
            f = (lon & 3).astype(f32) * 0.25
            g = (tilt & 3).astype(f32) * 0.25
            mix_ref[n, 0] = (1.0 - g) * (1.0 - f)
            mix_ref[n, 1] = (1.0 - g) * f
            mix_ref[n, 2] = g * (1.0 - f)
            mix_ref[n, 3] = g * f
            mix_ref[n, 4] = (tilt >> 2).astype(f32) * 0.25


def grid_kernel(
    lat_ref, recv_ref, order_ref, index_ref, mix_ref, table_hi_ref, table_lo_ref, twiddle_ref,
    grid_ref, departed_ref, x_ref, field_ref, edge_ref, lat_smem, lat_sem, levs,
):
    lat_copy = pltpu.make_async_copy(lat_ref, lat_smem, lat_sem)
    lat_copy.start()
    wave = lax.axis_index("wave")
    last = lax.axis_index("lev") == levs - 1

    lane = lax.broadcasted_iota(jnp.int32, (8, 128), 1)
    slot = lane // 16
    for grp in range(4):
        for t in range(3):
            arr = [recv_ref[8 * grp + j, t] for j in range(8)]
            for bit in range(3):
                step = 1 << bit
                on = (slot & step) != 0
                arr = [jnp.where(on, arr[(j + step) % 8], arr[j]) for j in range(8)]
            for e in range(2):
                for r in range(2):
                    pieces = []
                    for l in range(2):
                        c = 4 * l + 2 * e + r
                        pieces.append(pltpu.roll(arr[-c % 8], (128 - 16 * c) % 128, 1))
                    hi, lo = split(jnp.concatenate(pieces, axis=0))
                    cols = pl.ds(128 * grp, 128)
                    x_ref[e, pl.ds(48 * r + 16 * t, 16), cols] = hi
                    x_ref[e, pl.ds(96 + 48 * r + 16 * t, 16), cols] = lo

    sums = []
    for e in range(2):
        both = lax.dot_general(x_ref[e], order_ref[e], NT, preferred_element_type=f32)
        sums.append(both[:96] + both[96:])

    slot48 = lax.broadcasted_iota(jnp.int32, (48, 128), 1) // 32
    by_q = [[] for _ in range(4)]
    for g in range(3):
        arr = []
        for i in range(4):
            block = sums[i // 2][48 * (i % 2) : 48 * (i % 2) + 48, 128 * g : 128 * g + 128]
            arr.append(pltpu.roll(block, 32 * i, 1) if i else block)
        for bit in range(2):
            step = 1 << bit
            on = (slot48 & step) != 0
            arr = [jnp.where(on, arr[(j + step) % 4], arr[j]) for j in range(4)]
        for q in range(4):
            if 4 * g + q < 10:
                by_q[q].append(arr[-q % 4])
    re, im = [None] * 10, [None] * 10
    for q in range(4):
        n = 48 * len(by_q[q])
        hi, lo = split(jnp.concatenate(by_q[q], axis=0))
        rows = pl.ds(32 * (-q % 4), 128)
        both = jnp.dot(jnp.concatenate([hi, lo], axis=0), table_hi_ref[rows, :], preferred_element_type=f32)
        small = jnp.dot(hi, table_lo_ref[rows, :], preferred_element_type=f32)
        total = both[:n] + (both[n:] + small)
        for g in range(len(by_q[q])):
            p = 4 * g + q
            a, b = total[48 * g : 48 * g + 48, :128], total[48 * g : 48 * g + 48, 128:]
            if p == 0:
                re[p], im[p] = a, b
            else:
                c = twiddle_ref[2 * p : 2 * p + 1, :]
                s = twiddle_ref[2 * p + 1 : 2 * p + 2, :]
                re[p] = a * c - b * s
                im[p] = a * s + b * c

    def put(x, value):
        field_ref[x] = value

    even = [re[p] + re[10 - p] for p in (1, 2, 3, 4)]
    diff = [im[p] - im[10 - p] for p in (1, 2, 3, 4)]
    for x in range(3):
        co = [math.cos(math.pi * p * x / 5) for p in (1, 2, 3, 4)]
        si = [math.sin(math.pi * p * x / 5) for p in (1, 2, 3, 4)]
        if x == 0:
            a_even = re[0] + (even[1] + even[3])
            a_odd = re[5] + (even[0] + even[2])
            put(0, a_even + a_odd)
            put(5, a_even - a_odd)
            continue
        a_even = re[0] + (co[1] * even[1] + co[3] * even[3])
        a_odd = (co[0] * even[0] + co[2] * even[2]) + (re[5] if x % 2 == 0 else -re[5])
        b_even = si[1] * diff[1] + si[3] * diff[3]
        b_odd = si[0] * diff[0] + si[2] * diff[2]
        a, b = a_even + a_odd, b_even + b_odd
        put(x, a - b)
        put(10 - x, a + b)
        a, b = a_even - a_odd, b_odd - b_even
        put(5 - x, a - b)
        put(5 + x, a + b)

    lane48 = lax.broadcasted_iota(jnp.int32, (48, 128), 1)
    for x in range(10):
        edge_ref[x] = jnp.where(lane48 < 64, field_ref[(x + 1) % 10], field_ref[(x + 9) % 10])
        for l in range(2):
            for row in range(4):
                lev, h = row // 2, row % 2
                grid_ref[lev, pl.ds(2 * h + l, 1), pl.ds(128 * x, 128)] = field_ref[x, pl.ds(8 * (2 + l) + row, 1), :]

    lat_copy.wait()
    hemi = lax.broadcasted_iota(jnp.int32, (8, 128), 0) % 2 == 1
    keep_own = jnp.logical_and(last, lax.broadcasted_iota(jnp.int32, (8, 128), 0) >= 2)
    for l in range(2):
        for x in range(10):
            north, south = 10 * l + x, 20 + 10 * l + x

            n = 10 * l + x
            index = index_ref[n]
            nxt = index + 1
            starts = [8 * (lat_smem[block] + (2 - 2 * wave)) for block in (north, south)]
            rows = []
            for off in range(2):
                at = [pl.multiple_of(start + 8 * off, 8) for start in starts]
                main = jnp.where(hemi, field_ref[x, pl.ds(at[1], 8), :], field_ref[x, pl.ds(at[0], 8), :])
                edge = jnp.where(hemi, edge_ref[x, pl.ds(at[1], 8), :], edge_ref[x, pl.ds(at[0], 8), :])

                def look(column):
                    wrapped = column & 127
                    return jnp.where(
                        wrapped == column,
                        jnp.take_along_axis(main, wrapped, axis=1),
                        jnp.take_along_axis(edge, wrapped, axis=1),
                    )

                rows.append(mix_ref[n, 2 * off] * look(index) + mix_ref[n, 2 * off + 1] * look(nxt))
            horizontal = rows[0] + rows[1]
            v = mix_ref[n, 4]
            upper = jnp.where(keep_own, horizontal, pltpu.roll(horizontal, 6, 0))
            departed = (1.0 - v) * horizontal + v * upper
            for row in range(4):
                lev, h = row // 2, row % 2
                departed_ref[lev, pl.ds(2 * h + l, 1), pl.ds(128 * x, 128)] = departed[row : row + 1, :]


def dft_tables():
    slot = np.arange(224) // 32 % 4
    member, part = slot // 2, slot % 2
    m2 = 32 * member + np.arange(224) % 32
    x = np.arange(128)
    theta = 2 * np.pi * ((m2[:, None] * x[None, :]) % 128) / 128
    c, s = np.cos(theta), np.sin(theta)
    part = part[:, None]
    table = np.concatenate([np.where(part == 0, c, -s), np.where(part == 0, s, c)], axis=1)
    hi = table.astype(jnp.bfloat16)
    lo = (table - hi.astype(np.float64)).astype(jnp.bfloat16)
    angle = 2 * np.pi * np.arange(10)[:, None] * x[None, :] / 1280
    twiddle = np.stack([np.cos(angle), np.sin(angle)], axis=1).reshape(20, 128).astype(np.float32)
    return hi, lo, twiddle


def to_grid(dep_lat, received, order, index, mix, levs):
    hi, lo, twiddle = dft_tables()
    vmem = pl.BlockSpec(memory_space=pltpu.VMEM)
    outside = pl.BlockSpec(memory_space=pl.ANY)

    def kernel(*refs):
        grid_kernel(*refs, levs)

    return pl.pallas_call(
        kernel,
        out_shape=[jax.ShapeDtypeStruct((2, 4, 1280), f32)] * 2,
        in_specs=[outside] + [vmem] * 7,
        out_specs=[vmem, vmem],
        scratch_shapes=[
            pltpu.VMEM((2, 192, 512), bf16),
            pltpu.VMEM((10, 48, 128), f32),
            pltpu.VMEM((10, 48, 128), f32),
            pltpu.SMEM(dep_lat.shape, jnp.int32),
            pltpu.SemaphoreType.DMA,
        ],
        compiler_params=pltpu.CompilerParams(vmem_limit_bytes=LIMIT),
        name="grid",
    )(dep_lat, received, order, index, mix, jnp.asarray(hi), jnp.asarray(lo), jnp.asarray(twiddle))


def per_device(legendre, spectral, pair_low, dep_lat, dep_col, lon_steps, tilt_steps):
    waves, levs = lax.axis_size("wave"), lax.axis_size("lev")
    received, order, index, mix = exchange(
        pair_low, legendre, spectral, dep_col, lon_steps, tilt_steps, waves, levs
    )
    received = received.reshape(waves, 3, 8, 128)
    return tuple(to_grid(dep_lat, received, order, index, mix, levs))


def solution(mesh):
    return jax.shard_map(
        per_device,
        mesh=mesh,
        in_specs=(
            P("wave", None, None),
            P("wave", "lev", None, None),
            P(),
            P("wave"),
            P("wave"),
            P("wave", None),
            P("wave", None),
        ),
        out_specs=(P("lev", "wave", None), P("lev", "wave", None)),
        check_vma=False,
    )
```

```python
import functools
import math

import jax
import jax.numpy as jnp
import numpy as np
from jax import lax
from jax.experimental import pallas as pl
from jax.experimental.pallas import tpu as pltpu
from jax.sharding import PartitionSpec as P

MESH = pl.DeviceIdType.MESH
LIMIT = 16 * 1024 * 1024
ORDER = (2, 3, 28, 29, 12, 13, 20, 21, 30, 31, 10, 11, 14, 15, 26, 27, 6, 7, 24, 25, 8, 9, 22, 23, 18, 19, 1, 4, 5, 16, 17)
NT = (((1,), (1,)), ((), ()))
f32 = jnp.float32
bf16 = jnp.bfloat16


def split(x):
    hi = x.astype(bf16)
    lo = (x - hi.astype(f32)).astype(bf16)
    return hi, lo


def legendre_into(send_ref, low_of, leg_ref, spec_ref, wait_pair, y_ref, z_ref, turn):
    pairs, lats, slots = leg_ref.shape
    top = slots - 1
    k = lax.broadcasted_iota(jnp.int32, (8, slots), 1)
    row = lax.broadcasted_iota(jnp.int32, (8, slots), 0)
    southern, second, real = row >= 4, (row & 2) != 0, (row & 1) == 0
    signed_k = jnp.where(second, k, -k)

    def signs(parity):
        return jnp.where(jnp.logical_and(southern, parity != 0), -1.0, 1.0)

    sign_even = signs(k & 1)
    sign_odd = jnp.where(second, signs((k + 1) & 1), sign_even)
    y_ref[...] = jnp.zeros_like(y_ref)
    send_ref[0] = jnp.zeros(send_ref.shape[1:], f32)
    send_ref[lats // 2 + 1] = jnp.zeros(send_ref.shape[1:], f32)
    for s in range(pairs):
        wait_pair(s)
        first = top - low_of(s)
        keep = signed_k >= jnp.where(second, first, 1 - first)
        mask = jnp.where(keep, jnp.where((first & 1) == 0, sign_even, sign_odd), 0.0)
        both, small = None, None
        for a, b in ((0, 256), (256, 512), (512, slots)):
            rows = []
            for lev in range(2):
                re = jnp.broadcast_to(spec_ref[s, lev, 0:1, a:b], (8, b - a))
                im = jnp.broadcast_to(spec_ref[s, lev, 1:2, a:b], (8, b - a))
                rows.append(jnp.where(real[:, a:b], re, im) * mask[:, a:b])
            hi, lo = split(jnp.concatenate(rows, axis=0))
            leg_hi, leg_lo = split(leg_ref[s, :, a:b])
            d1 = lax.dot_general(jnp.concatenate([hi, lo], axis=0), leg_hi, NT, preferred_element_type=f32)
            d2 = lax.dot_general(hi, leg_lo, NT, preferred_element_type=f32)
            both = d1 if both is None else both + d1
            small = d2 if small is None else small + d2
        y_ref[pl.ds(s, 16, stride=16), :] = both[:16] + (both[16:] + small)
    lane = lax.broadcasted_iota(jnp.int32, (lats // 2, 128), 1)
    for lev in range(2):
        z_ref[...] = y_ref[pl.ds(128 * lev, 128), :].T
        even = z_ref[pl.ds(0, lats // 2, stride=2), :]
        odd = z_ref[pl.ds(1, lats // 2, stride=2), :]
        for h in range(2):
            if h == 0:
                val = jnp.where(lane < 64, even, pltpu.roll(odd, 64, 1))
            else:
                val = jnp.where(lane < 64, pltpu.roll(even, 64, 1), odd)
            val = pltpu.roll(val, 16 * turn, 1)
            for j in range(lats // 2):
                send_ref[1 + j, lev, h : h + 1, :] = val[j : j + 1, :]


def exchange_kernel(
    waves, levs, low_hbm, leg_hbm, spec_hbm, col_hbm, lon_hbm, tilt_hbm,
    recv_ref, order_ref, index_ref, mix_ref,
    low_smem, low_vmem, leg_ref, spec_ref, y_ref, z_ref, send_ref,
    low_sem, leg_sem, spec_sem, send_sem, recv_sem, down_send_sem, down_recv_sem,
    proxy_ref, proxy_sem, proxy_down_sem, relay_sem, relay_down_sem, ready,
    col_smem, lon_vmem, tilt_vmem, plan_sem,
):
    me = lax.axis_index("wave")
    lev = lax.axis_index("lev")
    pairs, _, slots = leg_ref.shape
    low_copy = pltpu.make_async_copy(low_hbm, low_smem, low_sem.at[0])
    low_copy.start()
    spec_copy = pltpu.make_async_copy(spec_hbm, spec_ref, spec_sem)
    spec_copy.start()
    for s in range(0, pairs, 2):
        pltpu.make_async_copy(leg_hbm.at[pl.ds(s, 2)], leg_ref.at[pl.ds(s, 2)], leg_sem).start()
    low_again = pltpu.make_async_copy(low_hbm, low_vmem, low_sem.at[1])
    low_again.start()
    plan_copies = [
        pltpu.make_async_copy(src, dst, plan_sem.at[i])
        for i, (src, dst) in enumerate([(col_hbm, col_smem), (lon_hbm, lon_vmem), (tilt_hbm, tilt_vmem)])
    ]
    for copy in plan_copies:
        copy.start()

    barrier = pltpu.get_barrier_semaphore()
    late = me == 0
    lower, upper = lev > 0, lev < levs - 1
    peers = waves - 1

    def signal(sem, to_lev, to_wave):
        pl.semaphore_signal(sem, inc=1, device_id={"lev": to_lev, "wave": to_wave}, device_id_type=MESH)

    def each(first, body):
        def step(d, _):
            body(d)
            return 0

        lax.fori_loop(first, waves, step, 0)

    @pl.when(jnp.logical_not(late))
    def _():
        each(1, lambda d: signal(barrier, lev, lax.rem(me + d, waves)))

        @pl.when(upper)
        def _():
            each(0, lambda w: signal(barrier, lev + 1, w))

    @pl.when(late)
    def _():
        pl.semaphore_wait(barrier, peers + jnp.where(lower, peers, 0))
        signal(ready, lev, 1)

    low_copy.wait()

    def wait_pair(s):
        if s == 0:
            spec_copy.wait()
            pltpu.make_async_copy(leg_hbm, leg_ref, leg_sem).wait()

    legendre_into(
        send_ref, lambda s: low_smem[me * pairs + s], leg_ref, spec_ref, wait_pair, y_ref, z_ref,
        lax.rem(me, 8),
    )

    @pl.when(jnp.logical_not(late))
    def _():
        pl.semaphore_wait(barrier, peers - 1 + jnp.where(lower, peers, 0))

    def across(peer, slots_of, to_wave, sem):
        pltpu.make_async_remote_copy(
            src_ref=send_ref.at[pl.ds(peer, 3)],
            dst_ref=slots_of.at[me, :, pl.ds(0, 2)],
            send_sem=send_sem,
            recv_sem=sem,
            device_id={"lev": lev, "wave": to_wave},
            device_id_type=MESH,
        ).start()

    def down(peer, slots_of, to_wave, sem):
        pltpu.make_async_remote_copy(
            src_ref=send_ref.at[pl.ds(peer, 3), 0],
            dst_ref=slots_of.at[me, :, 2],
            send_sem=down_send_sem,
            recv_sem=sem,
            device_id={"lev": lev - 1, "wave": to_wave},
            device_id_type=MESH,
        ).start()

    def turn(quarter):
        return jnp.where(quarter == 0, 0, jnp.where(quarter == 1, 3, quarter - 1))

    def spread(d):
        peer = lax.rem(me + 8 * turn(d // 8) + d % 8, waves)

        @pl.when(peer != 0)
        def _():
            across(peer, recv_ref, peer, recv_sem)

    @pl.when(late)
    def _():
        for peer in ORDER:
            across(peer, recv_ref, peer, recv_sem)

    @pl.when(jnp.logical_not(late))
    def _():
        each(1, spread)

    @pl.when(me > 1)
    def _():
        across(0, proxy_ref, 1, proxy_sem)

    @pl.when(lower)
    def _():
        each(1, lambda w: down(w, recv_ref, w, down_recv_sem))
        down(0, proxy_ref, 1, proxy_down_sem)

    pltpu.make_async_copy(send_ref.at[pl.ds(me, 3)], recv_ref.at[me, :, pl.ds(0, 2)], recv_sem).start()
    low_again.wait()
    order_into(order_ref, low_vmem, slots - 1)
    for copy in plan_copies:
        copy.wait()
    plan_into(index_ref, mix_ref, col_smem, lon_vmem, tilt_vmem)

    def wait_for(part, sem):
        pltpu.make_async_copy(part, part, sem).wait()

    def relay(part_of, sem, to_sem):
        return pltpu.make_async_remote_copy(
            src_ref=part_of(proxy_ref),
            dst_ref=part_of(recv_ref),
            send_sem=sem,
            recv_sem=to_sem,
            device_id={"lev": lev, "wave": 0},
            device_id_type=MESH,
        )

    def others(ref):
        return ref.at[pl.ds(1, waves - 1), :, pl.ds(0, 2)]

    def downs(ref):
        return ref.at[:, :, 2]

    @pl.when(me == 1)
    def _():
        pltpu.make_async_copy(send_ref.at[pl.ds(0, 3)], proxy_ref.at[me, :, pl.ds(0, 2)], proxy_sem).start()
        wait_for(others(proxy_ref), proxy_sem)

        @pl.when(upper)
        def _():
            wait_for(downs(proxy_ref), proxy_down_sem)

        pl.semaphore_wait(ready, 1)
        relay(others, relay_sem, recv_sem).start()

        @pl.when(upper)
        def _():
            relay(downs, relay_down_sem, down_recv_sem).start()

    wait_for(recv_ref.at[:, :, pl.ds(0, 2)], recv_sem)

    @pl.when(upper)
    def _():
        wait_for(downs(recv_ref), down_recv_sem)

    @pl.when(me == 1)
    def _():
        wait_for(others(proxy_ref), relay_sem)
        wait_for(recv_ref.at[pl.ds(0, waves - 2), :, pl.ds(0, 2)], send_sem)

        @pl.when(upper)
        def _():
            wait_for(downs(proxy_ref), relay_down_sem)

    @pl.when(me != 1)
    def _():
        wait_for(others(recv_ref), send_sem)

    @pl.when(lower)
    def _():
        wait_for(downs(recv_ref), down_send_sem)


def exchange(pair_low, legendre, spectral, dep_col, lon_steps, tilt_steps, waves, levs):
    pairs, lats, slots = legendre.shape
    any_space = pl.BlockSpec(memory_space=pltpu.HBM)
    operands = (pair_low, legendre, spectral, dep_col, lon_steps, tilt_steps)
    vmem = pl.BlockSpec(memory_space=pltpu.VMEM)
    return pl.pallas_call(
        functools.partial(exchange_kernel, waves, levs),
        out_shape=[
            jax.ShapeDtypeStruct((waves, 3, 4, 2, 128), f32),
            jax.ShapeDtypeStruct((2, 384, 512), bf16),
            jax.ShapeDtypeStruct((20, 8, 128), jnp.int32),
            jax.ShapeDtypeStruct((20, 5, 8, 128), f32),
        ],
        in_specs=[any_space] * 6,
        out_specs=[vmem] * 4,
        scratch_shapes=[
            pltpu.SMEM(pair_low.shape, jnp.int32),
            pltpu.VMEM(pair_low.shape, jnp.int32),
            pltpu.VMEM((pairs, lats, slots), f32),
            pltpu.VMEM(spectral.shape, f32),
            pltpu.VMEM((256, lats), f32),
            pltpu.VMEM((lats, 128), f32),
            pltpu.VMEM((lats // 2 + 2, 2, 2, 128), f32),
            pltpu.SemaphoreType.DMA((2,)),
            pltpu.SemaphoreType.DMA,
            pltpu.SemaphoreType.DMA,
            pltpu.SemaphoreType.DMA,
            pltpu.SemaphoreType.DMA,
            pltpu.SemaphoreType.DMA,
            pltpu.SemaphoreType.DMA,
            pltpu.VMEM((waves, 3, 4, 2, 128), f32),
            pltpu.SemaphoreType.DMA,
            pltpu.SemaphoreType.DMA,
            pltpu.SemaphoreType.DMA,
            pltpu.SemaphoreType.DMA,
            pltpu.SemaphoreType.REGULAR,
            pltpu.SMEM(dep_col.shape, jnp.int32),
            pltpu.VMEM(lon_steps.shape, jnp.int32),
            pltpu.VMEM(tilt_steps.shape, jnp.int32),
            pltpu.SemaphoreType.DMA((3,)),
        ],
        compiler_params=pltpu.CompilerParams(
            collective_id=0, has_side_effects=True, vmem_limit_bytes=LIMIT
        ),
    )(*[pltpu.with_memory_space_constraint(a, pltpu.HBM) for a in operands])


def spread_low(low_ref):
    lane = lax.broadcasted_iota(jnp.int32, (8, 128), 1)
    row = low_ref[...].reshape(1, low_ref.shape[0])
    ends = [(0, 128), (128, 256), (192, 320)]
    parts = [jnp.broadcast_to(row[:, a:b], (8, 128)) for a, b in ends]
    out = []
    for v in range(4):
        source = 80 * v + 10 * (lane // 16) + lane % 16
        first = 80 * v // 128
        last = (80 * v + 79) // 128
        shift = [0, 0, 64]
        got = jnp.take_along_axis(parts[first], (source + shift[first]) % 128, axis=1)
        if last != first:
            other = jnp.take_along_axis(parts[last], (source + shift[last]) % 128, axis=1)
            got = jnp.where(source // 128 == first, got, other)
        out.append(jnp.where(lane % 16 < 10, got, -1))
    return out


def order_into(order_ref, low_ref, top):
    low = spread_low(low_ref)
    columns = order_ref.shape[1]
    for e in range(2):
        for n0 in range(0, columns, 16):
            g, q, mu0 = n0 // 128, n0 % 128 // 32, n0 % 32
            p = 4 * g + q
            row = lax.broadcasted_iota(jnp.int32, (8, 128), 0)
            halves = []
            for half in range(2):
                m = p + 10 * (32 * e + mu0 + 8 * half + row)
                want = m if e == 0 else top - 1 - m
                weight = jnp.where(m == 0, 1.0, 2.0) if (e == 0 and p == 0) else jnp.full((8, 128), 2.0, f32)
                halves.append((want, weight))
            for v in range(4):
                if p >= 10:
                    block = jnp.zeros((16, 128), f32)
                else:
                    block = jnp.concatenate(
                        [jnp.where(low[v] == want, weight, 0.0) for want, weight in halves], axis=0
                    )
                order_ref[e, pl.ds(n0, 16), pl.ds(128 * v, 128)] = block.astype(bf16)


def plan_into(index_ref, mix_ref, col_ref, lon_ref, tilt_ref):
    lane = lax.broadcasted_iota(jnp.int32, (8, 128), 1)
    hemi = lax.broadcasted_iota(jnp.int32, (8, 128), 0) % 2 == 1
    for l in range(2):
        for x in range(10):
            north, south = 10 * l + x, 20 + 10 * l + x

            def pick(ref):
                return jnp.where(
                    hemi,
                    jnp.broadcast_to(ref[south : south + 1, :], (8, 128)),
                    jnp.broadcast_to(ref[north : north + 1, :], (8, 128)),
                )

            lon, tilt = pick(lon_ref), pick(tilt_ref)

            def shift_of(block):
                return lax.rem(col_ref[block] - 128 * x + 1280 + 640, 1280) - 643

            n = 10 * l + x
            index_ref[n] = lane + jnp.where(hemi, shift_of(south), shift_of(north)) + (lon >> 2)
            f = (lon & 3).astype(f32) * 0.25
            g = (tilt & 3).astype(f32) * 0.25
            mix_ref[n, 0] = (1.0 - g) * (1.0 - f)
            mix_ref[n, 1] = (1.0 - g) * f
            mix_ref[n, 2] = g * (1.0 - f)
            mix_ref[n, 3] = g * f
            mix_ref[n, 4] = (tilt >> 2).astype(f32) * 0.25


def grid_kernel(
    lat_ref, recv_ref, order_ref, index_ref, mix_ref, table_hi_ref, table_lo_ref, twiddle_ref,
    grid_ref, departed_ref, x_ref, field_ref, edge_ref, lat_smem, lat_sem, levs,
):
    lat_copy = pltpu.make_async_copy(lat_ref, lat_smem, lat_sem)
    lat_copy.start()
    wave = lax.axis_index("wave")
    last = lax.axis_index("lev") == levs - 1

    lane = lax.broadcasted_iota(jnp.int32, (8, 128), 1)
    slot = lane // 16
    for grp in range(4):
        for t in range(3):
            arr = [recv_ref[8 * grp + j, t] for j in range(8)]
            for bit in range(3):
                step = 1 << bit
                on = (slot & step) != 0
                arr = [jnp.where(on, arr[(j + step) % 8], arr[j]) for j in range(8)]
            for e in range(2):
                for r in range(2):
                    pieces = []
                    for l in range(2):
                        c = 4 * l + 2 * e + r
                        pieces.append(pltpu.roll(arr[-c % 8], (128 - 16 * c) % 128, 1))
                    hi, lo = split(jnp.concatenate(pieces, axis=0))
                    cols = pl.ds(128 * grp, 128)
                    x_ref[e, pl.ds(48 * r + 16 * t, 16), cols] = hi
                    x_ref[e, pl.ds(96 + 48 * r + 16 * t, 16), cols] = lo

    sums = []
    for e in range(2):
        both = lax.dot_general(x_ref[e], order_ref[e], NT, preferred_element_type=f32)
        sums.append(both[:96] + both[96:])

    slot48 = lax.broadcasted_iota(jnp.int32, (48, 128), 1) // 32
    by_q = [[] for _ in range(4)]
    for g in range(3):
        arr = []
        for i in range(4):
            block = sums[i // 2][48 * (i % 2) : 48 * (i % 2) + 48, 128 * g : 128 * g + 128]
            arr.append(pltpu.roll(block, 32 * i, 1) if i else block)
        for bit in range(2):
            step = 1 << bit
            on = (slot48 & step) != 0
            arr = [jnp.where(on, arr[(j + step) % 4], arr[j]) for j in range(4)]
        for q in range(4):
            if 4 * g + q < 10:
                by_q[q].append(arr[-q % 4])
    re, im = [None] * 10, [None] * 10
    for q in range(4):
        n = 48 * len(by_q[q])
        hi, lo = split(jnp.concatenate(by_q[q], axis=0))
        rows = pl.ds(32 * (-q % 4), 128)
        both = jnp.dot(jnp.concatenate([hi, lo], axis=0), table_hi_ref[rows, :], preferred_element_type=f32)
        small = jnp.dot(hi, table_lo_ref[rows, :], preferred_element_type=f32)
        total = both[:n] + (both[n:] + small)
        for g in range(len(by_q[q])):
            p = 4 * g + q
            a, b = total[48 * g : 48 * g + 48, :128], total[48 * g : 48 * g + 48, 128:]
            if p == 0:
                re[p], im[p] = a, b
            else:
                c = twiddle_ref[2 * p : 2 * p + 1, :]
                s = twiddle_ref[2 * p + 1 : 2 * p + 2, :]
                re[p] = a * c - b * s
                im[p] = a * s + b * c

    def put(x, value):
        field_ref[x] = value

    even = [re[p] + re[10 - p] for p in (1, 2, 3, 4)]
    diff = [im[p] - im[10 - p] for p in (1, 2, 3, 4)]
    for x in range(3):
        co = [math.cos(math.pi * p * x / 5) for p in (1, 2, 3, 4)]
        si = [math.sin(math.pi * p * x / 5) for p in (1, 2, 3, 4)]
        if x == 0:
            a_even = re[0] + (even[1] + even[3])
            a_odd = re[5] + (even[0] + even[2])
            put(0, a_even + a_odd)
            put(5, a_even - a_odd)
            continue
        a_even = re[0] + (co[1] * even[1] + co[3] * even[3])
        a_odd = (co[0] * even[0] + co[2] * even[2]) + (re[5] if x % 2 == 0 else -re[5])
        b_even = si[1] * diff[1] + si[3] * diff[3]
        b_odd = si[0] * diff[0] + si[2] * diff[2]
        a, b = a_even + a_odd, b_even + b_odd
        put(x, a - b)
        put(10 - x, a + b)
        a, b = a_even - a_odd, b_odd - b_even
        put(5 - x, a - b)
        put(5 + x, a + b)

    lane48 = lax.broadcasted_iota(jnp.int32, (48, 128), 1)
    for x in range(10):
        edge_ref[x] = jnp.where(lane48 < 64, field_ref[(x + 1) % 10], field_ref[(x + 9) % 10])
        for l in range(2):
            for row in range(4):
                lev, h = row // 2, row % 2
                grid_ref[lev, pl.ds(2 * h + l, 1), pl.ds(128 * x, 128)] = field_ref[x, pl.ds(8 * (2 + l) + row, 1), :]

    lat_copy.wait()
    hemi = lax.broadcasted_iota(jnp.int32, (8, 128), 0) % 2 == 1
    keep_own = jnp.logical_and(last, lax.broadcasted_iota(jnp.int32, (8, 128), 0) >= 2)
    for l in range(2):
        for x in range(10):
            north, south = 10 * l + x, 20 + 10 * l + x

            n = 10 * l + x
            index = index_ref[n]
            nxt = index + 1
            starts = [8 * (lat_smem[block] + (2 - 2 * wave)) for block in (north, south)]
            rows = []
            for off in range(2):
                at = [pl.multiple_of(start + 8 * off, 8) for start in starts]
                main = jnp.where(hemi, field_ref[x, pl.ds(at[1], 8), :], field_ref[x, pl.ds(at[0], 8), :])
                edge = jnp.where(hemi, edge_ref[x, pl.ds(at[1], 8), :], edge_ref[x, pl.ds(at[0], 8), :])

                def look(column):
                    wrapped = column & 127
                    return jnp.where(
                        wrapped == column,
                        jnp.take_along_axis(main, wrapped, axis=1),
                        jnp.take_along_axis(edge, wrapped, axis=1),
                    )

                rows.append(mix_ref[n, 2 * off] * look(index) + mix_ref[n, 2 * off + 1] * look(nxt))
            horizontal = rows[0] + rows[1]
            v = mix_ref[n, 4]
            upper = jnp.where(keep_own, horizontal, pltpu.roll(horizontal, 6, 0))
            departed = (1.0 - v) * horizontal + v * upper
            for row in range(4):
                lev, h = row // 2, row % 2
                departed_ref[lev, pl.ds(2 * h + l, 1), pl.ds(128 * x, 128)] = departed[row : row + 1, :]


def dft_tables():
    slot = np.arange(224) // 32 % 4
    member, part = slot // 2, slot % 2
    m2 = 32 * member + np.arange(224) % 32
    x = np.arange(128)
    theta = 2 * np.pi * ((m2[:, None] * x[None, :]) % 128) / 128
    c, s = np.cos(theta), np.sin(theta)
    part = part[:, None]
    table = np.concatenate([np.where(part == 0, c, -s), np.where(part == 0, s, c)], axis=1)
    hi = table.astype(jnp.bfloat16)
    lo = (table - hi.astype(np.float64)).astype(jnp.bfloat16)
    angle = 2 * np.pi * np.arange(10)[:, None] * x[None, :] / 1280
    twiddle = np.stack([np.cos(angle), np.sin(angle)], axis=1).reshape(20, 128).astype(np.float32)
    return hi, lo, twiddle


def to_grid(dep_lat, received, order, index, mix, levs):
    hi, lo, twiddle = dft_tables()
    vmem = pl.BlockSpec(memory_space=pltpu.VMEM)
    outside = pl.BlockSpec(memory_space=pl.ANY)

    def kernel(*refs):
        grid_kernel(*refs, levs)

    return pl.pallas_call(
        kernel,
        out_shape=[jax.ShapeDtypeStruct((2, 4, 1280), f32)] * 2,
        in_specs=[outside] + [vmem] * 7,
        out_specs=[vmem, vmem],
        scratch_shapes=[
            pltpu.VMEM((2, 192, 512), bf16),
            pltpu.VMEM((10, 48, 128), f32),
            pltpu.VMEM((10, 48, 128), f32),
            pltpu.SMEM(dep_lat.shape, jnp.int32),
            pltpu.SemaphoreType.DMA,
        ],
        compiler_params=pltpu.CompilerParams(vmem_limit_bytes=LIMIT),
        name="grid",
    )(dep_lat, received, order, index, mix, jnp.asarray(hi), jnp.asarray(lo), jnp.asarray(twiddle))


def per_device(legendre, spectral, pair_low, dep_lat, dep_col, lon_steps, tilt_steps):
    waves, levs = lax.axis_size("wave"), lax.axis_size("lev")
    received, order, index, mix = exchange(
        pair_low, legendre, spectral, dep_col, lon_steps, tilt_steps, waves, levs
    )
    received = received.reshape(waves, 3, 8, 128)
    return tuple(to_grid(dep_lat, received, order, index, mix, levs))


def solution(mesh):
    return jax.shard_map(
        per_device,
        mesh=mesh,
        in_specs=(
            P("wave", None, None),
            P("wave", "lev", None, None),
            P(),
            P("wave"),
            P("wave"),
            P("wave", None),
            P("wave", None),
        ),
        out_specs=(P("lev", "wave", None), P("lev", "wave", None)),
        check_vma=False,
    )
```

```python
import functools
import math

import jax
import jax.numpy as jnp
import numpy as np
from jax import lax
from jax.experimental import pallas as pl
from jax.experimental.pallas import tpu as pltpu
from jax.sharding import PartitionSpec as P

MESH = pl.DeviceIdType.MESH
LIMIT = 16 * 1024 * 1024
ORDER = (28, 29, 4, 5, 12, 13, 20, 21, 2, 3, 30, 31, 10, 11, 14, 15, 6, 7, 26, 27, 24, 25, 8, 9, 22, 23, 18, 19, 1, 16, 17)
NT = (((1,), (1,)), ((), ()))
f32 = jnp.float32
bf16 = jnp.bfloat16


def split(x):
    hi = x.astype(bf16)
    lo = (x - hi.astype(f32)).astype(bf16)
    return hi, lo


def legendre_into(send_ref, low_of, leg_ref, spec_ref, wait_pair, y_ref, z_ref, turn):
    pairs, lats, slots = leg_ref.shape
    top = slots - 1
    k = lax.broadcasted_iota(jnp.int32, (8, slots), 1)
    row = lax.broadcasted_iota(jnp.int32, (8, slots), 0)
    southern, second, real = row >= 4, (row & 2) != 0, (row & 1) == 0
    signed_k = jnp.where(second, k, -k)

    def signs(parity):
        return jnp.where(jnp.logical_and(southern, parity != 0), -1.0, 1.0)

    sign_even = signs(k & 1)
    sign_odd = jnp.where(second, signs((k + 1) & 1), sign_even)
    y_ref[...] = jnp.zeros_like(y_ref)
    send_ref[0] = jnp.zeros(send_ref.shape[1:], f32)
    send_ref[lats // 2 + 1] = jnp.zeros(send_ref.shape[1:], f32)
    for s in range(pairs):
        wait_pair(s)
        first = top - low_of(s)
        keep = signed_k >= jnp.where(second, first, 1 - first)
        mask = jnp.where(keep, jnp.where((first & 1) == 0, sign_even, sign_odd), 0.0)
        both, small = None, None
        for a, b in ((0, 256), (256, 512), (512, slots)):
            rows = []
            for lev in range(2):
                re = jnp.broadcast_to(spec_ref[s, lev, 0:1, a:b], (8, b - a))
                im = jnp.broadcast_to(spec_ref[s, lev, 1:2, a:b], (8, b - a))
                rows.append(jnp.where(real[:, a:b], re, im) * mask[:, a:b])
            hi, lo = split(jnp.concatenate(rows, axis=0))
            leg_hi, leg_lo = split(leg_ref[s, :, a:b])
            d1 = lax.dot_general(jnp.concatenate([hi, lo], axis=0), leg_hi, NT, preferred_element_type=f32)
            d2 = lax.dot_general(hi, leg_lo, NT, preferred_element_type=f32)
            both = d1 if both is None else both + d1
            small = d2 if small is None else small + d2
        y_ref[pl.ds(s, 16, stride=16), :] = both[:16] + (both[16:] + small)
    lane = lax.broadcasted_iota(jnp.int32, (lats // 2, 128), 1)
    for lev in range(2):
        z_ref[...] = y_ref[pl.ds(128 * lev, 128), :].T
        even = z_ref[pl.ds(0, lats // 2, stride=2), :]
        odd = z_ref[pl.ds(1, lats // 2, stride=2), :]
        for h in range(2):
            if h == 0:
                val = jnp.where(lane < 64, even, pltpu.roll(odd, 64, 1))
            else:
                val = jnp.where(lane < 64, pltpu.roll(even, 64, 1), odd)
            val = pltpu.roll(val, 16 * turn, 1)
            for j in range(lats // 2):
                send_ref[1 + j, lev, h : h + 1, :] = val[j : j + 1, :]


def exchange_kernel(
    waves, levs, low_hbm, leg_hbm, spec_hbm, col_hbm, lon_hbm, tilt_hbm,
    recv_ref, order_ref, index_ref, mix_ref,
    low_smem, low_vmem, leg_ref, spec_ref, y_ref, z_ref, send_ref,
    low_sem, leg_sem, spec_sem, send_sem, recv_sem, down_send_sem, down_recv_sem,
    proxy_ref, proxy_sem, proxy_down_sem, relay_sem, relay_down_sem, ready,
    col_smem, lon_vmem, tilt_vmem, plan_sem,
):
    me = lax.axis_index("wave")
    lev = lax.axis_index("lev")
    pairs, _, slots = leg_ref.shape
    low_copy = pltpu.make_async_copy(low_hbm, low_smem, low_sem.at[0])
    low_copy.start()
    spec_copy = pltpu.make_async_copy(spec_hbm, spec_ref, spec_sem)
    spec_copy.start()
    for s in range(0, pairs, 2):
        pltpu.make_async_copy(leg_hbm.at[pl.ds(s, 2)], leg_ref.at[pl.ds(s, 2)], leg_sem).start()
    low_again = pltpu.make_async_copy(low_hbm, low_vmem, low_sem.at[1])
    low_again.start()
    plan_copies = [
        pltpu.make_async_copy(src, dst, plan_sem.at[i])
        for i, (src, dst) in enumerate([(col_hbm, col_smem), (lon_hbm, lon_vmem), (tilt_hbm, tilt_vmem)])
    ]
    for copy in plan_copies:
        copy.start()

    barrier = pltpu.get_barrier_semaphore()
    late = me == 0
    lower, upper = lev > 0, lev < levs - 1
    peers = waves - 1

    def signal(sem, to_lev, to_wave):
        pl.semaphore_signal(sem, inc=1, device_id={"lev": to_lev, "wave": to_wave}, device_id_type=MESH)

    def each(first, body):
        def step(d, _):
            body(d)
            return 0

        lax.fori_loop(first, waves, step, 0)

    @pl.when(jnp.logical_not(late))
    def _():
        each(1, lambda d: signal(barrier, lev, lax.rem(me + d, waves)))

        @pl.when(upper)
        def _():
            each(0, lambda w: signal(barrier, lev + 1, w))

    @pl.when(late)
    def _():
        pl.semaphore_wait(barrier, peers + jnp.where(lower, peers, 0))
        signal(ready, lev, 1)

    low_copy.wait()

    def wait_pair(s):
        if s == 0:
            spec_copy.wait()
            pltpu.make_async_copy(leg_hbm, leg_ref, leg_sem).wait()

    legendre_into(
        send_ref, lambda s: low_smem[me * pairs + s], leg_ref, spec_ref, wait_pair, y_ref, z_ref,
        lax.rem(me, 8),
    )

    @pl.when(jnp.logical_not(late))
    def _():
        pl.semaphore_wait(barrier, peers - 1 + jnp.where(lower, peers, 0))

    def across(peer, slots_of, to_wave, sem):
        pltpu.make_async_remote_copy(
            src_ref=send_ref.at[pl.ds(peer, 3)],
            dst_ref=slots_of.at[me, :, pl.ds(0, 2)],
            send_sem=send_sem,
            recv_sem=sem,
            device_id={"lev": lev, "wave": to_wave},
            device_id_type=MESH,
        ).start()

    def down(peer, slots_of, to_wave, sem):
        pltpu.make_async_remote_copy(
            src_ref=send_ref.at[pl.ds(peer, 3), 0],
            dst_ref=slots_of.at[me, :, 2],
            send_sem=down_send_sem,
            recv_sem=sem,
            device_id={"lev": lev - 1, "wave": to_wave},
            device_id_type=MESH,
        ).start()

    def turn(quarter):
        return jnp.where(quarter == 0, 0, jnp.where(quarter == 1, 3, quarter - 1))

    def spread(d):
        peer = lax.rem(me + 8 * turn(d // 8) + d % 8, waves)

        @pl.when(peer != 0)
        def _():
            across(peer, recv_ref, peer, recv_sem)

    @pl.when(late)
    def _():
        for peer in ORDER:
            across(peer, recv_ref, peer, recv_sem)

    @pl.when(jnp.logical_not(late))
    def _():
        each(1, spread)

    @pl.when(me > 1)
    def _():
        across(0, proxy_ref, 1, proxy_sem)

    @pl.when(lower)
    def _():
        each(1, lambda w: down(w, recv_ref, w, down_recv_sem))
        down(0, proxy_ref, 1, proxy_down_sem)

    pltpu.make_async_copy(send_ref.at[pl.ds(me, 3)], recv_ref.at[me, :, pl.ds(0, 2)], recv_sem).start()
    low_again.wait()
    order_into(order_ref, low_vmem, slots - 1)
    for copy in plan_copies:
        copy.wait()
    plan_into(index_ref, mix_ref, col_smem, lon_vmem, tilt_vmem)

    def wait_for(part, sem):
        pltpu.make_async_copy(part, part, sem).wait()

    def relay(part_of, sem, to_sem):
        return pltpu.make_async_remote_copy(
            src_ref=part_of(proxy_ref),
            dst_ref=part_of(recv_ref),
            send_sem=sem,
            recv_sem=to_sem,
            device_id={"lev": lev, "wave": 0},
            device_id_type=MESH,
        )

    def others(ref):
        return ref.at[pl.ds(1, waves - 1), :, pl.ds(0, 2)]

    def downs(ref):
        return ref.at[:, :, 2]

    @pl.when(me == 1)
    def _():
        pltpu.make_async_copy(send_ref.at[pl.ds(0, 3)], proxy_ref.at[me, :, pl.ds(0, 2)], proxy_sem).start()
        wait_for(others(proxy_ref), proxy_sem)

        @pl.when(upper)
        def _():
            wait_for(downs(proxy_ref), proxy_down_sem)

        pl.semaphore_wait(ready, 1)
        relay(others, relay_sem, recv_sem).start()

        @pl.when(upper)
        def _():
            relay(downs, relay_down_sem, down_recv_sem).start()

    wait_for(recv_ref.at[:, :, pl.ds(0, 2)], recv_sem)

    @pl.when(upper)
    def _():
        wait_for(downs(recv_ref), down_recv_sem)

    @pl.when(me == 1)
    def _():
        wait_for(others(proxy_ref), relay_sem)
        wait_for(recv_ref.at[pl.ds(0, waves - 2), :, pl.ds(0, 2)], send_sem)

        @pl.when(upper)
        def _():
            wait_for(downs(proxy_ref), relay_down_sem)

    @pl.when(me != 1)
    def _():
        wait_for(others(recv_ref), send_sem)

    @pl.when(lower)
    def _():
        wait_for(downs(recv_ref), down_send_sem)


def exchange(pair_low, legendre, spectral, dep_col, lon_steps, tilt_steps, waves, levs):
    pairs, lats, slots = legendre.shape
    any_space = pl.BlockSpec(memory_space=pltpu.HBM)
    operands = (pair_low, legendre, spectral, dep_col, lon_steps, tilt_steps)
    vmem = pl.BlockSpec(memory_space=pltpu.VMEM)
    return pl.pallas_call(
        functools.partial(exchange_kernel, waves, levs),
        out_shape=[
            jax.ShapeDtypeStruct((waves, 3, 4, 2, 128), f32),
            jax.ShapeDtypeStruct((2, 384, 512), bf16),
            jax.ShapeDtypeStruct((20, 8, 128), jnp.int32),
            jax.ShapeDtypeStruct((20, 5, 8, 128), f32),
        ],
        in_specs=[any_space] * 6,
        out_specs=[vmem] * 4,
        scratch_shapes=[
            pltpu.SMEM(pair_low.shape, jnp.int32),
            pltpu.VMEM(pair_low.shape, jnp.int32),
            pltpu.VMEM((pairs, lats, slots), f32),
            pltpu.VMEM(spectral.shape, f32),
            pltpu.VMEM((256, lats), f32),
            pltpu.VMEM((lats, 128), f32),
            pltpu.VMEM((lats // 2 + 2, 2, 2, 128), f32),
            pltpu.SemaphoreType.DMA((2,)),
            pltpu.SemaphoreType.DMA,
            pltpu.SemaphoreType.DMA,
            pltpu.SemaphoreType.DMA,
            pltpu.SemaphoreType.DMA,
            pltpu.SemaphoreType.DMA,
            pltpu.SemaphoreType.DMA,
            pltpu.VMEM((waves, 3, 4, 2, 128), f32),
            pltpu.SemaphoreType.DMA,
            pltpu.SemaphoreType.DMA,
            pltpu.SemaphoreType.DMA,
            pltpu.SemaphoreType.DMA,
            pltpu.SemaphoreType.REGULAR,
            pltpu.SMEM(dep_col.shape, jnp.int32),
            pltpu.VMEM(lon_steps.shape, jnp.int32),
            pltpu.VMEM(tilt_steps.shape, jnp.int32),
            pltpu.SemaphoreType.DMA((3,)),
        ],
        compiler_params=pltpu.CompilerParams(
            collective_id=0, has_side_effects=True, vmem_limit_bytes=LIMIT
        ),
    )(*[pltpu.with_memory_space_constraint(a, pltpu.HBM) for a in operands])


def spread_low(low_ref):
    lane = lax.broadcasted_iota(jnp.int32, (8, 128), 1)
    row = low_ref[...].reshape(1, low_ref.shape[0])
    ends = [(0, 128), (128, 256), (192, 320)]
    parts = [jnp.broadcast_to(row[:, a:b], (8, 128)) for a, b in ends]
    out = []
    for v in range(4):
        source = 80 * v + 10 * (lane // 16) + lane % 16
        first = 80 * v // 128
        last = (80 * v + 79) // 128
        shift = [0, 0, 64]
        got = jnp.take_along_axis(parts[first], (source + shift[first]) % 128, axis=1)
        if last != first:
            other = jnp.take_along_axis(parts[last], (source + shift[last]) % 128, axis=1)
            got = jnp.where(source // 128 == first, got, other)
        out.append(jnp.where(lane % 16 < 10, got, -1))
    return out


def order_into(order_ref, low_ref, top):
    low = spread_low(low_ref)
    columns = order_ref.shape[1]
    for e in range(2):
        for n0 in range(0, columns, 16):
            g, q, mu0 = n0 // 128, n0 % 128 // 32, n0 % 32
            p = 4 * g + q
            row = lax.broadcasted_iota(jnp.int32, (8, 128), 0)
            halves = []
            for half in range(2):
                m = p + 10 * (32 * e + mu0 + 8 * half + row)
                want = m if e == 0 else top - 1 - m
                weight = jnp.where(m == 0, 1.0, 2.0) if (e == 0 and p == 0) else jnp.full((8, 128), 2.0, f32)
                halves.append((want, weight))
            for v in range(4):
                if p >= 10:
                    block = jnp.zeros((16, 128), f32)
                else:
                    block = jnp.concatenate(
                        [jnp.where(low[v] == want, weight, 0.0) for want, weight in halves], axis=0
                    )
                order_ref[e, pl.ds(n0, 16), pl.ds(128 * v, 128)] = block.astype(bf16)


def plan_into(index_ref, mix_ref, col_ref, lon_ref, tilt_ref):
    lane = lax.broadcasted_iota(jnp.int32, (8, 128), 1)
    hemi = lax.broadcasted_iota(jnp.int32, (8, 128), 0) % 2 == 1
    for l in range(2):
        for x in range(10):
            north, south = 10 * l + x, 20 + 10 * l + x

            def pick(ref):
                return jnp.where(
                    hemi,
                    jnp.broadcast_to(ref[south : south + 1, :], (8, 128)),
                    jnp.broadcast_to(ref[north : north + 1, :], (8, 128)),
                )

            lon, tilt = pick(lon_ref), pick(tilt_ref)

            def shift_of(block):
                return lax.rem(col_ref[block] - 128 * x + 1280 + 640, 1280) - 643

            n = 10 * l + x
            index_ref[n] = lane + jnp.where(hemi, shift_of(south), shift_of(north)) + (lon >> 2)
            f = (lon & 3).astype(f32) * 0.25
            g = (tilt & 3).astype(f32) * 0.25
            mix_ref[n, 0] = (1.0 - g) * (1.0 - f)
            mix_ref[n, 1] = (1.0 - g) * f
            mix_ref[n, 2] = g * (1.0 - f)
            mix_ref[n, 3] = g * f
            mix_ref[n, 4] = (tilt >> 2).astype(f32) * 0.25


def grid_kernel(
    lat_ref, recv_ref, order_ref, index_ref, mix_ref, table_hi_ref, table_lo_ref, twiddle_ref,
    grid_ref, departed_ref, x_ref, field_ref, edge_ref, lat_smem, lat_sem, levs,
):
    lat_copy = pltpu.make_async_copy(lat_ref, lat_smem, lat_sem)
    lat_copy.start()
    wave = lax.axis_index("wave")
    last = lax.axis_index("lev") == levs - 1

    lane = lax.broadcasted_iota(jnp.int32, (8, 128), 1)
    slot = lane // 16
    for grp in range(4):
        for t in range(3):
            arr = [recv_ref[8 * grp + j, t] for j in range(8)]
            for bit in range(3):
                step = 1 << bit
                on = (slot & step) != 0
                arr = [jnp.where(on, arr[(j + step) % 8], arr[j]) for j in range(8)]
            for e in range(2):
                for r in range(2):
                    pieces = []
                    for l in range(2):
                        c = 4 * l + 2 * e + r
                        pieces.append(pltpu.roll(arr[-c % 8], (128 - 16 * c) % 128, 1))
                    hi, lo = split(jnp.concatenate(pieces, axis=0))
                    cols = pl.ds(128 * grp, 128)
                    x_ref[e, pl.ds(48 * r + 16 * t, 16), cols] = hi
                    x_ref[e, pl.ds(96 + 48 * r + 16 * t, 16), cols] = lo

    sums = []
    for e in range(2):
        both = lax.dot_general(x_ref[e], order_ref[e], NT, preferred_element_type=f32)
        sums.append(both[:96] + both[96:])

    slot48 = lax.broadcasted_iota(jnp.int32, (48, 128), 1) // 32
    by_q = [[] for _ in range(4)]
    for g in range(3):
        arr = []
        for i in range(4):
            block = sums[i // 2][48 * (i % 2) : 48 * (i % 2) + 48, 128 * g : 128 * g + 128]
            arr.append(pltpu.roll(block, 32 * i, 1) if i else block)
        for bit in range(2):
            step = 1 << bit
            on = (slot48 & step) != 0
            arr = [jnp.where(on, arr[(j + step) % 4], arr[j]) for j in range(4)]
        for q in range(4):
            if 4 * g + q < 10:
                by_q[q].append(arr[-q % 4])
    re, im = [None] * 10, [None] * 10
    for q in range(4):
        n = 48 * len(by_q[q])
        hi, lo = split(jnp.concatenate(by_q[q], axis=0))
        rows = pl.ds(32 * (-q % 4), 128)
        both = jnp.dot(jnp.concatenate([hi, lo], axis=0), table_hi_ref[rows, :], preferred_element_type=f32)
        small = jnp.dot(hi, table_lo_ref[rows, :], preferred_element_type=f32)
        total = both[:n] + (both[n:] + small)
        for g in range(len(by_q[q])):
            p = 4 * g + q
            a, b = total[48 * g : 48 * g + 48, :128], total[48 * g : 48 * g + 48, 128:]
            if p == 0:
                re[p], im[p] = a, b
            else:
                c = twiddle_ref[2 * p : 2 * p + 1, :]
                s = twiddle_ref[2 * p + 1 : 2 * p + 2, :]
                re[p] = a * c - b * s
                im[p] = a * s + b * c

    def put(x, value):
        field_ref[x] = value

    even = [re[p] + re[10 - p] for p in (1, 2, 3, 4)]
    diff = [im[p] - im[10 - p] for p in (1, 2, 3, 4)]
    for x in range(3):
        co = [math.cos(math.pi * p * x / 5) for p in (1, 2, 3, 4)]
        si = [math.sin(math.pi * p * x / 5) for p in (1, 2, 3, 4)]
        if x == 0:
            a_even = re[0] + (even[1] + even[3])
            a_odd = re[5] + (even[0] + even[2])
            put(0, a_even + a_odd)
            put(5, a_even - a_odd)
            continue
        a_even = re[0] + (co[1] * even[1] + co[3] * even[3])
        a_odd = (co[0] * even[0] + co[2] * even[2]) + (re[5] if x % 2 == 0 else -re[5])
        b_even = si[1] * diff[1] + si[3] * diff[3]
        b_odd = si[0] * diff[0] + si[2] * diff[2]
        a, b = a_even + a_odd, b_even + b_odd
        put(x, a - b)
        put(10 - x, a + b)
        a, b = a_even - a_odd, b_odd - b_even
        put(5 - x, a - b)
        put(5 + x, a + b)

    lane48 = lax.broadcasted_iota(jnp.int32, (48, 128), 1)
    for x in range(10):
        edge_ref[x] = jnp.where(lane48 < 64, field_ref[(x + 1) % 10], field_ref[(x + 9) % 10])
        for l in range(2):
            for row in range(4):
                lev, h = row // 2, row % 2
                grid_ref[lev, pl.ds(2 * h + l, 1), pl.ds(128 * x, 128)] = field_ref[x, pl.ds(8 * (2 + l) + row, 1), :]

    lat_copy.wait()
    hemi = lax.broadcasted_iota(jnp.int32, (8, 128), 0) % 2 == 1
    keep_own = jnp.logical_and(last, lax.broadcasted_iota(jnp.int32, (8, 128), 0) >= 2)
    for l in range(2):
        for x in range(10):
            north, south = 10 * l + x, 20 + 10 * l + x

            n = 10 * l + x
            index = index_ref[n]
            nxt = index + 1
            starts = [8 * (lat_smem[block] + (2 - 2 * wave)) for block in (north, south)]
            rows = []
            for off in range(2):
                at = [pl.multiple_of(start + 8 * off, 8) for start in starts]
                main = jnp.where(hemi, field_ref[x, pl.ds(at[1], 8), :], field_ref[x, pl.ds(at[0], 8), :])
                edge = jnp.where(hemi, edge_ref[x, pl.ds(at[1], 8), :], edge_ref[x, pl.ds(at[0], 8), :])

                def look(column):
                    wrapped = column & 127
                    return jnp.where(
                        wrapped == column,
                        jnp.take_along_axis(main, wrapped, axis=1),
                        jnp.take_along_axis(edge, wrapped, axis=1),
                    )

                rows.append(mix_ref[n, 2 * off] * look(index) + mix_ref[n, 2 * off + 1] * look(nxt))
            horizontal = rows[0] + rows[1]
            v = mix_ref[n, 4]
            upper = jnp.where(keep_own, horizontal, pltpu.roll(horizontal, 6, 0))
            departed = (1.0 - v) * horizontal + v * upper
            for row in range(4):
                lev, h = row // 2, row % 2
                departed_ref[lev, pl.ds(2 * h + l, 1), pl.ds(128 * x, 128)] = departed[row : row + 1, :]


def dft_tables():
    slot = np.arange(224) // 32 % 4
    member, part = slot // 2, slot % 2
    m2 = 32 * member + np.arange(224) % 32
    x = np.arange(128)
    theta = 2 * np.pi * ((m2[:, None] * x[None, :]) % 128) / 128
    c, s = np.cos(theta), np.sin(theta)
    part = part[:, None]
    table = np.concatenate([np.where(part == 0, c, -s), np.where(part == 0, s, c)], axis=1)
    hi = table.astype(jnp.bfloat16)
    lo = (table - hi.astype(np.float64)).astype(jnp.bfloat16)
    angle = 2 * np.pi * np.arange(10)[:, None] * x[None, :] / 1280
    twiddle = np.stack([np.cos(angle), np.sin(angle)], axis=1).reshape(20, 128).astype(np.float32)
    return hi, lo, twiddle


def to_grid(dep_lat, received, order, index, mix, levs):
    hi, lo, twiddle = dft_tables()
    vmem = pl.BlockSpec(memory_space=pltpu.VMEM)
    outside = pl.BlockSpec(memory_space=pl.ANY)

    def kernel(*refs):
        grid_kernel(*refs, levs)

    return pl.pallas_call(
        kernel,
        out_shape=[jax.ShapeDtypeStruct((2, 4, 1280), f32)] * 2,
        in_specs=[outside] + [vmem] * 7,
        out_specs=[vmem, vmem],
        scratch_shapes=[
            pltpu.VMEM((2, 192, 512), bf16),
            pltpu.VMEM((10, 48, 128), f32),
            pltpu.VMEM((10, 48, 128), f32),
            pltpu.SMEM(dep_lat.shape, jnp.int32),
            pltpu.SemaphoreType.DMA,
        ],
        compiler_params=pltpu.CompilerParams(vmem_limit_bytes=LIMIT),
        name="grid",
    )(dep_lat, received, order, index, mix, jnp.asarray(hi), jnp.asarray(lo), jnp.asarray(twiddle))


def per_device(legendre, spectral, pair_low, dep_lat, dep_col, lon_steps, tilt_steps):
    waves, levs = lax.axis_size("wave"), lax.axis_size("lev")
    received, order, index, mix = exchange(
        pair_low, legendre, spectral, dep_col, lon_steps, tilt_steps, waves, levs
    )
    received = received.reshape(waves, 3, 8, 128)
    return tuple(to_grid(dep_lat, received, order, index, mix, levs))


def solution(mesh):
    return jax.shard_map(
        per_device,
        mesh=mesh,
        in_specs=(
            P("wave", None, None),
            P("wave", "lev", None, None),
            P(),
            P("wave"),
            P("wave"),
            P("wave", None),
            P("wave", None),
        ),
        out_specs=(P("lev", "wave", None), P("lev", "wave", None)),
        check_vma=False,
    )
```

```python
import functools
import math

import jax
import jax.numpy as jnp
import numpy as np
from jax import lax
from jax.experimental import pallas as pl
from jax.experimental.pallas import tpu as pltpu
from jax.sharding import PartitionSpec as P

MESH = pl.DeviceIdType.MESH
LIMIT = 16 * 1024 * 1024
ORDER = (28, 29, 4, 5, 12, 13, 20, 21, 2, 3, 30, 31, 10, 11, 14, 15, 6, 7, 26, 27, 24, 25, 8, 9, 22, 23, 18, 19, 1, 16, 17)
NT = (((1,), (1,)), ((), ()))
f32 = jnp.float32
bf16 = jnp.bfloat16


def split(x):
    hi = x.astype(bf16)
    lo = (x - hi.astype(f32)).astype(bf16)
    return hi, lo


def legendre_into(send_ref, low_of, leg_ref, spec_ref, wait_pair, y_ref, z_ref, turn):
    pairs, lats, slots = leg_ref.shape
    top = slots - 1
    k = lax.broadcasted_iota(jnp.int32, (8, slots), 1)
    row = lax.broadcasted_iota(jnp.int32, (8, slots), 0)
    southern, second, real = row >= 4, (row & 2) != 0, (row & 1) == 0
    signed_k = jnp.where(second, k, -k)

    def signs(parity):
        return jnp.where(jnp.logical_and(southern, parity != 0), -1.0, 1.0)

    sign_even = signs(k & 1)
    sign_odd = jnp.where(second, signs((k + 1) & 1), sign_even)
    y_ref[...] = jnp.zeros_like(y_ref)
    send_ref[0] = jnp.zeros(send_ref.shape[1:], f32)
    send_ref[lats // 2 + 1] = jnp.zeros(send_ref.shape[1:], f32)
    for s in range(pairs):
        wait_pair(s)
        first = top - low_of(s)
        keep = signed_k >= jnp.where(second, first, 1 - first)
        mask = jnp.where(keep, jnp.where((first & 1) == 0, sign_even, sign_odd), 0.0)
        both, small = None, None
        for a, b in ((0, 256), (256, 512), (512, slots)):
            rows = []
            for lev in range(2):
                re = jnp.broadcast_to(spec_ref[s, lev, 0:1, a:b], (8, b - a))
                im = jnp.broadcast_to(spec_ref[s, lev, 1:2, a:b], (8, b - a))
                rows.append(jnp.where(real[:, a:b], re, im) * mask[:, a:b])
            hi, lo = split(jnp.concatenate(rows, axis=0))
            leg_hi, leg_lo = split(leg_ref[s, :, a:b])
            d1 = lax.dot_general(jnp.concatenate([hi, lo], axis=0), leg_hi, NT, preferred_element_type=f32)
            d2 = lax.dot_general(hi, leg_lo, NT, preferred_element_type=f32)
            both = d1 if both is None else both + d1
            small = d2 if small is None else small + d2
        y_ref[pl.ds(s, 16, stride=16), :] = both[:16] + (both[16:] + small)
    lane = lax.broadcasted_iota(jnp.int32, (lats // 2, 128), 1)
    for lev in range(2):
        z_ref[...] = y_ref[pl.ds(128 * lev, 128), :].T
        even = z_ref[pl.ds(0, lats // 2, stride=2), :]
        odd = z_ref[pl.ds(1, lats // 2, stride=2), :]
        for h in range(2):
            if h == 0:
                val = jnp.where(lane < 64, even, pltpu.roll(odd, 64, 1))
            else:
                val = jnp.where(lane < 64, pltpu.roll(even, 64, 1), odd)
            val = pltpu.roll(val, 16 * turn, 1)
            for j in range(lats // 2):
                send_ref[1 + j, lev, h : h + 1, :] = val[j : j + 1, :]


def exchange_kernel(
    waves, levs, low_hbm, leg_hbm, spec_hbm, col_hbm, lon_hbm, tilt_hbm,
    recv_ref, order_ref, index_ref, mix_ref,
    low_smem, low_vmem, leg_ref, spec_ref, y_ref, z_ref, send_ref,
    low_sem, leg_sem, spec_sem, send_sem, recv_sem, down_send_sem, down_recv_sem,
    proxy_ref, proxy_sem, proxy_down_sem, relay_sem, relay_down_sem, ready,
    col_smem, lon_vmem, tilt_vmem, plan_sem,
):
    me = lax.axis_index("wave")
    lev = lax.axis_index("lev")
    pairs, _, slots = leg_ref.shape
    low_copy = pltpu.make_async_copy(low_hbm, low_smem, low_sem.at[0])
    low_copy.start()
    spec_copy = pltpu.make_async_copy(spec_hbm, spec_ref, spec_sem)
    spec_copy.start()
    for s in range(0, pairs, 2):
        pltpu.make_async_copy(leg_hbm.at[pl.ds(s, 2)], leg_ref.at[pl.ds(s, 2)], leg_sem).start()
    low_again = pltpu.make_async_copy(low_hbm, low_vmem, low_sem.at[1])
    low_again.start()
    plan_copies = [
        pltpu.make_async_copy(src, dst, plan_sem.at[i])
        for i, (src, dst) in enumerate([(col_hbm, col_smem), (lon_hbm, lon_vmem), (tilt_hbm, tilt_vmem)])
    ]
    for copy in plan_copies:
        copy.start()

    barrier = pltpu.get_barrier_semaphore()
    late = me == 0
    lower, upper = lev > 0, lev < levs - 1
    peers = waves - 1

    def signal(sem, to_lev, to_wave):
        pl.semaphore_signal(sem, inc=1, device_id={"lev": to_lev, "wave": to_wave}, device_id_type=MESH)

    def each(first, body):
        def step(d, _):
            body(d)
            return 0

        lax.fori_loop(first, waves, step, 0)

    @pl.when(jnp.logical_not(late))
    def _():
        each(1, lambda d: signal(barrier, lev, lax.rem(me + d, waves)))

        @pl.when(upper)
        def _():
            each(0, lambda w: signal(barrier, lev + 1, w))

    @pl.when(late)
    def _():
        pl.semaphore_wait(barrier, peers + jnp.where(lower, peers, 0))
        signal(ready, lev, 1)

    low_copy.wait()

    def wait_pair(s):
        if s == 0:
            spec_copy.wait()
            pltpu.make_async_copy(leg_hbm, leg_ref, leg_sem).wait()

    legendre_into(
        send_ref, lambda s: low_smem[me * pairs + s], leg_ref, spec_ref, wait_pair, y_ref, z_ref,
        lax.rem(me, 8),
    )

    @pl.when(jnp.logical_not(late))
    def _():
        pl.semaphore_wait(barrier, peers - 1 + jnp.where(lower, peers, 0))

    def across(peer, slots_of, to_wave, sem):
        pltpu.make_async_remote_copy(
            src_ref=send_ref.at[pl.ds(peer, 3)],
            dst_ref=slots_of.at[me, :, pl.ds(0, 2)],
            send_sem=send_sem,
            recv_sem=sem,
            device_id={"lev": lev, "wave": to_wave},
            device_id_type=MESH,
        ).start()

    def down(peer, slots_of, to_wave, sem):
        pltpu.make_async_remote_copy(
            src_ref=send_ref.at[pl.ds(peer, 3), 0],
            dst_ref=slots_of.at[me, :, 2],
            send_sem=down_send_sem,
            recv_sem=sem,
            device_id={"lev": lev - 1, "wave": to_wave},
            device_id_type=MESH,
        ).start()

    def turn(quarter):
        return jnp.where(quarter == 0, 0, jnp.where(quarter == 1, 3, quarter - 1))

    def spread(d):
        peer = lax.rem(me + 8 * turn(d // 8) + d % 8, waves)

        @pl.when(peer != 0)
        def _():
            across(peer, recv_ref, peer, recv_sem)

    @pl.when(late)
    def _():
        for peer in ORDER:
            across(peer, recv_ref, peer, recv_sem)

    @pl.when(jnp.logical_not(late))
    def _():
        each(1, spread)

    @pl.when(me > 1)
    def _():
        across(0, proxy_ref, 1, proxy_sem)

    @pl.when(lower)
    def _():
        each(1, lambda w: down(w, recv_ref, w, down_recv_sem))
        down(0, proxy_ref, 1, proxy_down_sem)

    pltpu.make_async_copy(send_ref.at[pl.ds(me, 3)], recv_ref.at[me, :, pl.ds(0, 2)], recv_sem).start()
    low_again.wait()
    order_into(order_ref, low_vmem, slots - 1)
    for copy in plan_copies:
        copy.wait()
    plan_into(index_ref, mix_ref, col_smem, lon_vmem, tilt_vmem)

    def wait_for(part, sem):
        pltpu.make_async_copy(part, part, sem).wait()

    def relay(part_of, sem, to_sem):
        return pltpu.make_async_remote_copy(
            src_ref=part_of(proxy_ref),
            dst_ref=part_of(recv_ref),
            send_sem=sem,
            recv_sem=to_sem,
            device_id={"lev": lev, "wave": 0},
            device_id_type=MESH,
        )

    def others(ref):
        return ref.at[pl.ds(1, waves - 1), :, pl.ds(0, 2)]

    def downs(ref):
        return ref.at[:, :, 2]

    @pl.when(me == 1)
    def _():
        pltpu.make_async_copy(send_ref.at[pl.ds(0, 3)], proxy_ref.at[me, :, pl.ds(0, 2)], proxy_sem).start()
        wait_for(others(proxy_ref), proxy_sem)

        @pl.when(upper)
        def _():
            wait_for(downs(proxy_ref), proxy_down_sem)

        pl.semaphore_wait(ready, 1)
        relay(others, relay_sem, recv_sem).start()

        @pl.when(upper)
        def _():
            relay(downs, relay_down_sem, down_recv_sem).start()

    @pl.when(me == 1)
    def _():
        wait_for(others(proxy_ref), relay_sem)
        wait_for(recv_ref.at[pl.ds(0, waves - 2), :, pl.ds(0, 2)], send_sem)

        @pl.when(upper)
        def _():
            wait_for(downs(proxy_ref), relay_down_sem)

    @pl.when(me != 1)
    def _():
        wait_for(others(recv_ref), send_sem)

    @pl.when(lower)
    def _():
        wait_for(downs(recv_ref), down_send_sem)

    @pl.when(upper)
    def _():
        wait_for(downs(recv_ref), down_recv_sem)

    wait_for(recv_ref.at[:, :, pl.ds(0, 2)], recv_sem)


def exchange(pair_low, legendre, spectral, dep_col, lon_steps, tilt_steps, waves, levs):
    pairs, lats, slots = legendre.shape
    any_space = pl.BlockSpec(memory_space=pltpu.HBM)
    operands = (pair_low, legendre, spectral, dep_col, lon_steps, tilt_steps)
    vmem = pl.BlockSpec(memory_space=pltpu.VMEM)
    return pl.pallas_call(
        functools.partial(exchange_kernel, waves, levs),
        out_shape=[
            jax.ShapeDtypeStruct((waves, 3, 4, 2, 128), f32),
            jax.ShapeDtypeStruct((2, 384, 512), bf16),
            jax.ShapeDtypeStruct((20, 8, 128), jnp.int32),
            jax.ShapeDtypeStruct((20, 5, 8, 128), f32),
        ],
        in_specs=[any_space] * 6,
        out_specs=[vmem] * 4,
        scratch_shapes=[
            pltpu.SMEM(pair_low.shape, jnp.int32),
            pltpu.VMEM(pair_low.shape, jnp.int32),
            pltpu.VMEM((pairs, lats, slots), f32),
            pltpu.VMEM(spectral.shape, f32),
            pltpu.VMEM((256, lats), f32),
            pltpu.VMEM((lats, 128), f32),
            pltpu.VMEM((lats // 2 + 2, 2, 2, 128), f32),
            pltpu.SemaphoreType.DMA((2,)),
            pltpu.SemaphoreType.DMA,
            pltpu.SemaphoreType.DMA,
            pltpu.SemaphoreType.DMA,
            pltpu.SemaphoreType.DMA,
            pltpu.SemaphoreType.DMA,
            pltpu.SemaphoreType.DMA,
            pltpu.VMEM((waves, 3, 4, 2, 128), f32),
            pltpu.SemaphoreType.DMA,
            pltpu.SemaphoreType.DMA,
            pltpu.SemaphoreType.DMA,
            pltpu.SemaphoreType.DMA,
            pltpu.SemaphoreType.REGULAR,
            pltpu.SMEM(dep_col.shape, jnp.int32),
            pltpu.VMEM(lon_steps.shape, jnp.int32),
            pltpu.VMEM(tilt_steps.shape, jnp.int32),
            pltpu.SemaphoreType.DMA((3,)),
        ],
        compiler_params=pltpu.CompilerParams(
            collective_id=0, has_side_effects=True, vmem_limit_bytes=LIMIT
        ),
    )(*[pltpu.with_memory_space_constraint(a, pltpu.HBM) for a in operands])


def spread_low(low_ref):
    lane = lax.broadcasted_iota(jnp.int32, (8, 128), 1)
    row = low_ref[...].reshape(1, low_ref.shape[0])
    ends = [(0, 128), (128, 256), (192, 320)]
    parts = [jnp.broadcast_to(row[:, a:b], (8, 128)) for a, b in ends]
    out = []
    for v in range(4):
        source = 80 * v + 10 * (lane // 16) + lane % 16
        first = 80 * v // 128
        last = (80 * v + 79) // 128
        shift = [0, 0, 64]
        got = jnp.take_along_axis(parts[first], (source + shift[first]) % 128, axis=1)
        if last != first:
            other = jnp.take_along_axis(parts[last], (source + shift[last]) % 128, axis=1)
            got = jnp.where(source // 128 == first, got, other)
        out.append(jnp.where(lane % 16 < 10, got, -1))
    return out


def order_into(order_ref, low_ref, top):
    low = spread_low(low_ref)
    columns = order_ref.shape[1]
    for e in range(2):
        for n0 in range(0, columns, 16):
            g, q, mu0 = n0 // 128, n0 % 128 // 32, n0 % 32
            p = 4 * g + q
            row = lax.broadcasted_iota(jnp.int32, (8, 128), 0)
            halves = []
            for half in range(2):
                m = p + 10 * (32 * e + mu0 + 8 * half + row)
                want = m if e == 0 else top - 1 - m
                weight = jnp.where(m == 0, 1.0, 2.0) if (e == 0 and p == 0) else jnp.full((8, 128), 2.0, f32)
                halves.append((want, weight))
            for v in range(4):
                if p >= 10:
                    block = jnp.zeros((16, 128), f32)
                else:
                    block = jnp.concatenate(
                        [jnp.where(low[v] == want, weight, 0.0) for want, weight in halves], axis=0
                    )
                order_ref[e, pl.ds(n0, 16), pl.ds(128 * v, 128)] = block.astype(bf16)


def plan_into(index_ref, mix_ref, col_ref, lon_ref, tilt_ref):
    lane = lax.broadcasted_iota(jnp.int32, (8, 128), 1)
    hemi = lax.broadcasted_iota(jnp.int32, (8, 128), 0) % 2 == 1
    for l in range(2):
        for x in range(10):
            north, south = 10 * l + x, 20 + 10 * l + x

            def pick(ref):
                return jnp.where(
                    hemi,
                    jnp.broadcast_to(ref[south : south + 1, :], (8, 128)),
                    jnp.broadcast_to(ref[north : north + 1, :], (8, 128)),
                )

            lon, tilt = pick(lon_ref), pick(tilt_ref)

            def shift_of(block):
                return lax.rem(col_ref[block] - 128 * x + 1280 + 640, 1280) - 643

            n = 10 * l + x
            index_ref[n] = lane + jnp.where(hemi, shift_of(south), shift_of(north)) + (lon >> 2)
            f = (lon & 3).astype(f32) * 0.25
            g = (tilt & 3).astype(f32) * 0.25
            mix_ref[n, 0] = (1.0 - g) * (1.0 - f)
            mix_ref[n, 1] = (1.0 - g) * f
            mix_ref[n, 2] = g * (1.0 - f)
            mix_ref[n, 3] = g * f
            mix_ref[n, 4] = (tilt >> 2).astype(f32) * 0.25


def grid_kernel(
    lat_ref, recv_ref, order_ref, index_ref, mix_ref, table_hi_ref, table_lo_ref, twiddle_ref,
    grid_ref, departed_ref, x_ref, field_ref, edge_ref, lat_smem, lat_sem, levs,
):
    lat_copy = pltpu.make_async_copy(lat_ref, lat_smem, lat_sem)
    lat_copy.start()
    wave = lax.axis_index("wave")
    last = lax.axis_index("lev") == levs - 1

    lane = lax.broadcasted_iota(jnp.int32, (8, 128), 1)
    slot = lane // 16
    for grp in range(4):
        for t in range(3):
            arr = [recv_ref[8 * grp + j, t] for j in range(8)]
            for bit in range(3):
                step = 1 << bit
                on = (slot & step) != 0
                arr = [jnp.where(on, arr[(j + step) % 8], arr[j]) for j in range(8)]
            for e in range(2):
                for r in range(2):
                    pieces = []
                    for l in range(2):
                        c = 4 * l + 2 * e + r
                        pieces.append(pltpu.roll(arr[-c % 8], (128 - 16 * c) % 128, 1))
                    hi, lo = split(jnp.concatenate(pieces, axis=0))
                    cols = pl.ds(128 * grp, 128)
                    x_ref[e, pl.ds(48 * r + 16 * t, 16), cols] = hi
                    x_ref[e, pl.ds(96 + 48 * r + 16 * t, 16), cols] = lo

    sums = []
    for e in range(2):
        both = lax.dot_general(x_ref[e], order_ref[e], NT, preferred_element_type=f32)
        sums.append(both[:96] + both[96:])

    slot48 = lax.broadcasted_iota(jnp.int32, (48, 128), 1) // 32
    by_q = [[] for _ in range(4)]
    for g in range(3):
        arr = []
        for i in range(4):
            block = sums[i // 2][48 * (i % 2) : 48 * (i % 2) + 48, 128 * g : 128 * g + 128]
            arr.append(pltpu.roll(block, 32 * i, 1) if i else block)
        for bit in range(2):
            step = 1 << bit
            on = (slot48 & step) != 0
            arr = [jnp.where(on, arr[(j + step) % 4], arr[j]) for j in range(4)]
        for q in range(4):
            if 4 * g + q < 10:
                by_q[q].append(arr[-q % 4])
    re, im = [None] * 10, [None] * 10
    for q in range(4):
        n = 48 * len(by_q[q])
        hi, lo = split(jnp.concatenate(by_q[q], axis=0))
        rows = pl.ds(32 * (-q % 4), 128)
        both = jnp.dot(jnp.concatenate([hi, lo], axis=0), table_hi_ref[rows, :], preferred_element_type=f32)
        small = jnp.dot(hi, table_lo_ref[rows, :], preferred_element_type=f32)
        total = both[:n] + (both[n:] + small)
        for g in range(len(by_q[q])):
            p = 4 * g + q
            a, b = total[48 * g : 48 * g + 48, :128], total[48 * g : 48 * g + 48, 128:]
            if p == 0:
                re[p], im[p] = a, b
            else:
                c = twiddle_ref[2 * p : 2 * p + 1, :]
                s = twiddle_ref[2 * p + 1 : 2 * p + 2, :]
                re[p] = a * c - b * s
                im[p] = a * s + b * c

    def put(x, value):
        field_ref[x] = value

    even = [re[p] + re[10 - p] for p in (1, 2, 3, 4)]
    diff = [im[p] - im[10 - p] for p in (1, 2, 3, 4)]
    for x in range(3):
        co = [math.cos(math.pi * p * x / 5) for p in (1, 2, 3, 4)]
        si = [math.sin(math.pi * p * x / 5) for p in (1, 2, 3, 4)]
        if x == 0:
            a_even = re[0] + (even[1] + even[3])
            a_odd = re[5] + (even[0] + even[2])
            put(0, a_even + a_odd)
            put(5, a_even - a_odd)
            continue
        a_even = re[0] + (co[1] * even[1] + co[3] * even[3])
        a_odd = (co[0] * even[0] + co[2] * even[2]) + (re[5] if x % 2 == 0 else -re[5])
        b_even = si[1] * diff[1] + si[3] * diff[3]
        b_odd = si[0] * diff[0] + si[2] * diff[2]
        a, b = a_even + a_odd, b_even + b_odd
        put(x, a - b)
        put(10 - x, a + b)
        a, b = a_even - a_odd, b_odd - b_even
        put(5 - x, a - b)
        put(5 + x, a + b)

    lane48 = lax.broadcasted_iota(jnp.int32, (48, 128), 1)
    for x in range(10):
        edge_ref[x] = jnp.where(lane48 < 64, field_ref[(x + 1) % 10], field_ref[(x + 9) % 10])
        for l in range(2):
            for row in range(4):
                lev, h = row // 2, row % 2
                grid_ref[lev, pl.ds(2 * h + l, 1), pl.ds(128 * x, 128)] = field_ref[x, pl.ds(8 * (2 + l) + row, 1), :]

    lat_copy.wait()
    hemi = lax.broadcasted_iota(jnp.int32, (8, 128), 0) % 2 == 1
    keep_own = jnp.logical_and(last, lax.broadcasted_iota(jnp.int32, (8, 128), 0) >= 2)
    for l in range(2):
        for x in range(10):
            north, south = 10 * l + x, 20 + 10 * l + x

            n = 10 * l + x
            index = index_ref[n]
            nxt = index + 1
            starts = [8 * (lat_smem[block] + (2 - 2 * wave)) for block in (north, south)]
            rows = []
            for off in range(2):
                at = [pl.multiple_of(start + 8 * off, 8) for start in starts]
                main = jnp.where(hemi, field_ref[x, pl.ds(at[1], 8), :], field_ref[x, pl.ds(at[0], 8), :])
                edge = jnp.where(hemi, edge_ref[x, pl.ds(at[1], 8), :], edge_ref[x, pl.ds(at[0], 8), :])

                def look(column):
                    wrapped = column & 127
                    return jnp.where(
                        wrapped == column,
                        jnp.take_along_axis(main, wrapped, axis=1),
                        jnp.take_along_axis(edge, wrapped, axis=1),
                    )

                rows.append(mix_ref[n, 2 * off] * look(index) + mix_ref[n, 2 * off + 1] * look(nxt))
            horizontal = rows[0] + rows[1]
            v = mix_ref[n, 4]
            upper = jnp.where(keep_own, horizontal, pltpu.roll(horizontal, 6, 0))
            departed = (1.0 - v) * horizontal + v * upper
            for row in range(4):
                lev, h = row // 2, row % 2
                departed_ref[lev, pl.ds(2 * h + l, 1), pl.ds(128 * x, 128)] = departed[row : row + 1, :]


def dft_tables():
    slot = np.arange(224) // 32 % 4
    member, part = slot // 2, slot % 2
    m2 = 32 * member + np.arange(224) % 32
    x = np.arange(128)
    theta = 2 * np.pi * ((m2[:, None] * x[None, :]) % 128) / 128
    c, s = np.cos(theta), np.sin(theta)
    part = part[:, None]
    table = np.concatenate([np.where(part == 0, c, -s), np.where(part == 0, s, c)], axis=1)
    hi = table.astype(jnp.bfloat16)
    lo = (table - hi.astype(np.float64)).astype(jnp.bfloat16)
    angle = 2 * np.pi * np.arange(10)[:, None] * x[None, :] / 1280
    twiddle = np.stack([np.cos(angle), np.sin(angle)], axis=1).reshape(20, 128).astype(np.float32)
    return hi, lo, twiddle


def to_grid(dep_lat, received, order, index, mix, levs):
    hi, lo, twiddle = dft_tables()
    vmem = pl.BlockSpec(memory_space=pltpu.VMEM)
    outside = pl.BlockSpec(memory_space=pl.ANY)

    def kernel(*refs):
        grid_kernel(*refs, levs)

    return pl.pallas_call(
        kernel,
        out_shape=[jax.ShapeDtypeStruct((2, 4, 1280), f32)] * 2,
        in_specs=[outside] + [vmem] * 7,
        out_specs=[vmem, vmem],
        scratch_shapes=[
            pltpu.VMEM((2, 192, 512), bf16),
            pltpu.VMEM((10, 48, 128), f32),
            pltpu.VMEM((10, 48, 128), f32),
            pltpu.SMEM(dep_lat.shape, jnp.int32),
            pltpu.SemaphoreType.DMA,
        ],
        compiler_params=pltpu.CompilerParams(vmem_limit_bytes=LIMIT),
        name="grid",
    )(dep_lat, received, order, index, mix, jnp.asarray(hi), jnp.asarray(lo), jnp.asarray(twiddle))


def per_device(legendre, spectral, pair_low, dep_lat, dep_col, lon_steps, tilt_steps):
    waves, levs = lax.axis_size("wave"), lax.axis_size("lev")
    received, order, index, mix = exchange(
        pair_low, legendre, spectral, dep_col, lon_steps, tilt_steps, waves, levs
    )
    received = received.reshape(waves, 3, 8, 128)
    return tuple(to_grid(dep_lat, received, order, index, mix, levs))


def solution(mesh):
    return jax.shard_map(
        per_device,
        mesh=mesh,
        in_specs=(
            P("wave", None, None),
            P("wave", "lev", None, None),
            P(),
            P("wave"),
            P("wave"),
            P("wave", None),
            P("wave", None),
        ),
        out_specs=(P("lev", "wave", None), P("lev", "wave", None)),
        check_vma=False,
    )
```
